32 devices in a mesh: dp: 8 (over z, x), tensor: 4 (over y, core).
Axes of the slice: x: 2, y: 2, z: 4, core: 2. Of those that a mesh axis runs over, the one named last changes fastest.
Arguments:
- hidden_in: bfloat16 [32768, 768], P(('dp', 'tensor')), may hold values from -6 to 6
- cotangent: bfloat16 [32768, 768], P(('dp', 'tensor')), may hold values from -6 to 6
- lengths: int32 [32], P('dp'), may hold values from 31 to 1024, as said below
- latent: int32 [32, 1024], P('dp'), may hold values from 0 to 1, as said below
- ln1_gain: float32 [768], replicated, may hold values from 0.5 to 1.5
- ln1_bias: float32 [768], replicated, may hold values from -1.75 to 1.75
- w_qkv: float32 [3, 768, 768], P(None, 'dp', 'tensor'), may hold values from -0.3125 to 0.3125
- b_qv: float32 [2, 768], replicated, may hold values from -1.75 to 1.75
- w_out: float32 [768, 768], P('tensor', 'dp'), may hold values from -1.25 to 1.25
- b_out: float32 [768], replicated, may hold values from -1.75 to 1.75
- ln2_gain: float32 [768], replicated, may hold values from 0.5 to 1.5
- ln2_bias: float32 [768], replicated, may hold values from -1.75 to 1.75
- w_up: float32 [768, 3072], P('dp', 'tensor'), may hold values from -0.21875 to 0.21875
- b_up: float32 [3072], replicated, may hold values from -1.75 to 1.75
- w_down: float32 [3072, 768], P('tensor', 'dp'), may hold values from -0.109375 to 0.109375
- b_down: float32 [768], replicated, may hold values from -1.75 to 1.75
Outputs:
- hidden_out: bfloat16 [32768, 768], P(('dp', 'tensor'))
- grad_in: float32 [32768, 768], P(('dp', 'tensor'))
- grad_ln1_gain: float32 [768], replicated
- grad_ln1_bias: float32 [768], replicated
- grad_w_qkv: float32 [3, 768, 768], P(None, 'dp', 'tensor')
- grad_b_qv: float32 [2, 768], replicated
- grad_w_out: float32 [768, 768], P('tensor', 'dp')
- grad_b_out: float32 [768], replicated
- grad_ln2_gain: float32 [768], replicated
- grad_ln2_bias: float32 [768], replicated
- grad_w_up: float32 [768, 3072], P('dp', 'tensor')
- grad_b_up: float32 [3072], replicated
- grad_w_down: float32 [3072, 768], P('tensor', 'dp')
- grad_b_down: float32 [768], replicated
The draws below stay inside these ranges and needn't reach their ends.
Inputs may be any that keep to these rules, and one draw needn't show every extreme that they name: `lengths`: A sequence's true length: a question of about 1024*30/1024 to 1024*400/1024 tokens, 0 to 6 latent thoughts and an answer, at most 1024; some sequence has exactly 1024, and some sequence has the shortest length, a shortest question and a one-token answer. `latent`: latent thoughts directly follow a sequence's question and lie within its true length.
All inputs are finite; a program needn't handle non-finite values.
Results may differ from the reference program's by a relative error of at most 0.015.
The reference program's roundings to bfloat16 on the way count: a program that leaves them out, or rounds other values in their place, can miss the bound.
Values may be sent and summed in bfloat16 or wider, within the bound.
No kernel may reach another device: no remote copies, remote signals or barrier semaphores. Data moves between devices by JAX's collectives and lax.ppermute only.
A program may use at most 320 MiB of HBM per device.

```python
import jax
import jax.numpy as jnp
from jax import lax

D = 768
HEADS = 12
HEAD_DIM = 64
FF = 3072
LEN = 1024
SEQ_DEV = 4
SEQS = 32
TOKENS = 32768
N_DP = 8


def thought_plan(key):
    plan_key = jax.random.fold_in(key, 11)
    key_question, key_thought, key_answer = jax.random.split(plan_key, 3)
    shortest = max(LEN * 30 // 1024, 1)
    question = jax.random.randint(key_question, (SEQS,), shortest, LEN * 400 // 1024 + 1)
    thoughts = 2 * jax.random.randint(key_thought, (SEQS,), 0, 4)
    answer = jax.random.randint(key_answer, (SEQS,), 1, LEN // 2 + 1)
    question = question.at[1].set(shortest)
    thoughts = thoughts.at[1].set(0)
    answer = answer.at[1].set(1)
    seq_length = jnp.minimum(question + thoughts + answer, LEN)
    seq_length = seq_length.at[0].set(LEN)
    return (question, thoughts, seq_length)


def draw_lengths(key, part):
    return thought_plan(key)[2].astype(jnp.int32)


def draw_latent(key, part):
    question, thoughts, seq_length = thought_plan(key)
    positions = jnp.arange(LEN, dtype=jnp.int32)[None, :]
    marked = (positions >= question[:, None]) & (positions < (question + thoughts)[:, None]) & (positions < seq_length[:, None])
    return marked.astype(jnp.int32)


def level_of(own_key, shape, cuts, least, top_value):
    def one(dim, shards_of):
        steps = jax.random.uniform(jax.random.fold_in(jax.random.fold_in(own_key, 6), dim), (shards_of,), jnp.float32, least / len(cuts), top_value / len(cuts))
        return jnp.repeat(jnp.exp(steps), shape[dim] // shards_of).reshape((-1,) + (1,) * (len(shape) - dim - 1))

    level = one(*cuts[0])
    for cut in cuts[1:]:
        level = level * one(*cut)
    return level


def scatter_about(stream_key, shape, scale, most, cuts=(), kind=jnp.bfloat16):
    array = scale * jax.random.normal(stream_key, shape, jnp.float32)
    if cuts:
        array = array * level_of(stream_key, shape, cuts, -0.22, 0.18)
    return jnp.clip(array, -most, most).astype(kind)


def setup_inputs(seed: int = 0) -> dict:
    splits = jax.random.split(jax.random.key(seed), 17)
    hidden_in = scatter_about(splits[0], (TOKENS, D), 1.0, 6.0, ((0, 32),))
    cotangent = scatter_about(splits[1], (TOKENS, D), 1.0, 6.0, ((0, 32),))
    lengths = draw_lengths(jax.random.fold_in(splits[16], 71), 0)
    latent = draw_latent(jax.random.fold_in(splits[16], 71), 0)
    ln1_gain = jnp.clip(1.0 + 0.1 * jax.random.normal(splits[4], (D,), jnp.float32), 0.5, 1.5)
    ln1_bias = scatter_about(splits[5], (D,), 0.3, 1.75, (), jnp.float32)
    w_qkv = scatter_about(splits[6], (3, D, D), (D // 2) ** -0.5, 0.3125, ((1, 8), (2, 4)), jnp.float32)
    b_qv = scatter_about(splits[7], (2, D), 0.3, 1.75, (), jnp.float32)
    w_out = scatter_about(splits[8], (D, D), (D // 32) ** -0.5, 1.25, ((0, 4), (1, 8)), jnp.float32)
    b_out = scatter_about(splits[9], (D,), 0.3, 1.75, (), jnp.float32)
    ln2_gain = jnp.clip(1.0 + 0.1 * jax.random.normal(splits[10], (D,), jnp.float32), 0.5, 1.5)
    ln2_bias = scatter_about(splits[11], (D,), 0.3, 1.75, (), jnp.float32)
    w_up = scatter_about(splits[12], (D, FF), D ** -0.5, 0.21875, ((0, 8), (1, 4)), jnp.float32)
    b_up = scatter_about(splits[13], (FF,), 0.3, 1.75, (), jnp.float32)
    w_down = scatter_about(splits[14], (FF, D), FF ** -0.5, 0.109375, ((0, 4), (1, 8)), jnp.float32)
    b_down = scatter_about(splits[15], (D,), 0.3, 1.75, (), jnp.float32)
    return {"hidden_in": hidden_in, "cotangent": cotangent, "lengths": lengths, "latent": latent, "ln1_gain": ln1_gain, "ln1_bias": ln1_bias, "w_qkv": w_qkv, "b_qv": b_qv, "w_out": w_out, "b_out": b_out, "ln2_gain": ln2_gain, "ln2_bias": ln2_bias, "w_up": w_up, "b_up": b_up, "w_down": w_down, "b_down": b_down}


@jax.custom_vjp
def low(v):
    return lax.optimization_barrier(v.astype(jnp.bfloat16)).astype(jnp.float32)

@jax.custom_vjp
def low_back(v):
    return v

def low_keep(v):
    return (low(v), None)

def low_pass(kept, grad):
    return (grad,)

def back_keep(v):
    return (v, None)

def back_low(kept, grad):
    return (low(grad),)
low.defvjp(low_keep, low_pass)
low_back.defvjp(back_keep, back_low)
NEG_BIG = -1e+30
EPSILON = 1e-05
HIGH = lax.Precision.HIGHEST

def round_both(values):
    return low(low_back(values))

def layer_norm(rows_in, gain, bias):
    center = rows_in - lax.optimization_barrier(jnp.mean(rows_in, axis=-1, keepdims=True))
    spread = lax.optimization_barrier(jnp.mean(center * center, axis=-1, keepdims=True))
    return center * lax.rsqrt(spread + EPSILON) * gain + bias

def score_block(q_block, offset, k_all, v_all, length):
    score_scale = HEAD_DIM ** (-0.5)
    scores = jnp.einsum('qhd,khd->hqk', q_block, k_all, precision=HIGH) * score_scale
    grid_shape = (q_block.shape[0], k_all.shape[0])
    q_pos = offset + lax.broadcasted_iota(jnp.int32, grid_shape, 0)
    k_pos = lax.broadcasted_iota(jnp.int32, grid_shape, 1)
    allowed = (k_pos <= q_pos) & (k_pos < length)
    scores = low_back(jnp.where(allowed[None], scores, NEG_BIG))
    row_peak = lax.optimization_barrier(jnp.max(scores, axis=-1, keepdims=True))
    shifted = jnp.exp(scores - row_peak)
    probs = low(shifted / lax.optimization_barrier(jnp.sum(shifted, axis=-1, keepdims=True)))
    return jnp.einsum('hqk,khd->qhd', probs, v_all, precision=HIGH)

def attend_sequence(packed):
    q_seq, k_seq, v_seq, length = packed
    block_rows = min(512, LEN)
    block_count = LEN // block_rows
    q_blocks = q_seq.reshape(block_count, block_rows, HEADS, HEAD_DIM)
    offsets = jnp.arange(block_count, dtype=jnp.int32) * block_rows
    checked = jax.checkpoint(score_block)
    pieces = lax.map(lambda packet: checked(packet[0], packet[1], k_seq, v_seq, length), (q_blocks, offsets))
    return pieces.reshape(LEN, HEADS * HEAD_DIM)

def block_forward(x_rows, seq_lengths, weights):
    ln1_gain, ln1_bias, w_qkv, b_qv, w_out, b_out, ln2_gain, ln2_bias, w_up, b_up, w_down, b_down = weights
    row_count = x_rows.shape[0]
    seq_count = row_count // LEN
    normed = low(layer_norm(x_rows, ln1_gain, ln1_bias))
    qkv_low = low(w_qkv)
    q_all = round_both(jnp.dot(normed, qkv_low[0], precision=HIGH, preferred_element_type=jnp.float32) + b_qv[0])
    k_all = round_both(jnp.dot(normed, qkv_low[1], precision=HIGH, preferred_element_type=jnp.float32))
    v_all = round_both(jnp.dot(normed, qkv_low[2], precision=HIGH, preferred_element_type=jnp.float32) + b_qv[1])

    def heads_of(values):
        return values.reshape(seq_count, LEN, HEADS, HEAD_DIM)
    attended = lax.map(attend_sequence, (heads_of(q_all), heads_of(k_all), heads_of(v_all), seq_lengths))
    attended = round_both(attended.reshape(row_count, D))
    attn_branch = low_back(jnp.dot(attended, low(w_out), precision=HIGH, preferred_element_type=jnp.float32))
    resid_one = x_rows + attn_branch + b_out
    normed_two = low(layer_norm(resid_one, ln2_gain, ln2_bias))
    pre_act = low_back(jnp.dot(normed_two, low(w_up), precision=HIGH, preferred_element_type=jnp.float32) + b_up)
    act_low = low(jax.nn.gelu(pre_act, approximate=True))
    mlp_branch = low_back(jnp.dot(act_low, low(w_down), precision=HIGH, preferred_element_type=jnp.float32))
    return resid_one + mlp_branch + b_down

def reference(hidden_in, cotangent, lengths, latent, ln1_gain, ln1_bias, w_qkv, b_qv, w_out, b_out, ln2_gain, ln2_bias, w_up, b_up, w_down, b_down):
    params = (ln1_gain, ln1_bias, w_qkv, b_qv, w_out, b_out, ln2_gain, ln2_bias, w_up, b_up, w_down, b_down)
    group_rows = SEQ_DEV * LEN
    x_groups = hidden_in.astype(jnp.float32).reshape(N_DP, group_rows, D)
    cot_groups = cotangent.astype(jnp.float32).reshape(N_DP, group_rows, D)
    len_groups = lengths.reshape(N_DP, SEQ_DEV)
    latent_groups = latent.reshape(N_DP, SEQ_DEV, LEN)

    def one_group(totals, packet):
        x_rows, cot_rows, seq_lengths, latent_rows = packet
        positions = lax.broadcasted_iota(jnp.int32, (SEQ_DEV, LEN), 1)
        keep_mask = ((positions < seq_lengths[:, None]) & (latent_rows == 0)).astype(jnp.float32).reshape(group_rows, 1)

        def forward(x_in, *weights):
            return block_forward(x_in, seq_lengths, weights)
        output, pullback = jax.vjp(forward, x_rows, *params)
        grads = pullback(cot_rows * keep_mask)
        totals = tuple((acc_sum + new_grad for acc_sum, new_grad in zip(totals, grads[1:])))
        return (totals, (output.astype(jnp.bfloat16), grads[0]))
    zero_grads = tuple((jnp.zeros_like(master) for master in params))
    totals, (out_rows, grad_rows) = lax.scan(one_group, zero_grads, (x_groups, cot_groups, len_groups, latent_groups))
    return (out_rows.reshape(TOKENS, D), grad_rows.reshape(TOKENS, D), totals[0], totals[1], totals[2], totals[3], totals[4], totals[5], totals[6], totals[7], totals[8], totals[9], totals[10], totals[11])
```

```python
import functools

import jax
import jax.numpy as jnp
from jax import lax
from jax.experimental import pallas as pl
from jax.experimental.pallas import tpu as pltpu
from jax.sharding import PartitionSpec as P

HEAD_DIM = 64
LEN = 1024
PAIR = 2 * HEAD_DIM
TILE = 256
NEG_BIG = -1e30
EPSILON = 1e-05
VMEM_BYTES = 66_900_000
BF = jnp.bfloat16
F32 = jnp.float32
BOTH = ("dp", "tensor")


def dot_nn(a, b):
    return lax.dot_general(a, b, (((1,), (0,)), ((), ())), preferred_element_type=F32)


def dot_nt(a, b):
    return lax.dot_general(a, b, (((1,), (1,)), ((), ())), preferred_element_type=F32)


def dot_tn(a, b):
    return lax.dot_general(a, b, (((0,), (0,)), ((), ())), preferred_element_type=F32)


def norm_parts(rows_in):
    center = rows_in - jnp.mean(rows_in, axis=-1, keepdims=True)
    spread = jnp.mean(center * center, axis=-1, keepdims=True)
    scale = lax.rsqrt(spread + EPSILON)
    return center * scale, scale


def norm_back(gy, normed, scale):
    mean_gy = jnp.mean(gy, axis=-1, keepdims=True)
    mean_gyn = jnp.mean(gy * normed, axis=-1, keepdims=True)
    return (gy - mean_gy - normed * mean_gyn) * scale


def col_sum(values):
    return jnp.sum(values, axis=0, keepdims=True)


def once(shape, index):
    return pl.BlockSpec(shape, index, pipeline_mode=pl.Buffered(1))


def params():
    return pltpu.CompilerParams(
        dimension_semantics=("arbitrary",), vmem_limit_bytes=VMEM_BYTES
    )


def qkv_kernel(blocks, x_ref, gain_ref, bias_ref, bqv_ref, raw_ref, q_ref, k_ref, v_ref, n_ref, w_ref):
    width = x_ref.shape[1]

    @pl.when(pl.program_id(0) == 0)
    def _():
        def piece(t, c):
            return raw_ref[:, t, :, c * PAIR : (c + 1) * PAIR].reshape(width, PAIR)

        for t in range(blocks):
            for c in range(4):
                w_ref[c, :, t * PAIR : (t + 1) * PAIR] = piece(t, c)
        for u in range(blocks // 2):
            col = (blocks + u) * PAIR
            for half in range(2):
                left = piece(2 * u, 4 + half)
                right = piece(2 * u + 1, 4 + half)
                w_ref[2 * half, :, col : col + PAIR] = jnp.concatenate(
                    [left[:, :HEAD_DIM], right[:, :HEAD_DIM]], axis=1
                )
                w_ref[2 * half + 1, :, col : col + PAIR] = jnp.concatenate(
                    [left[:, HEAD_DIM:], right[:, HEAD_DIM:]], axis=1
                )

    normed, _ = norm_parts(x_ref[...].astype(F32))
    low = (normed * gain_ref[...] + bias_ref[...]).astype(BF)
    n_ref[...] = low
    q_low = (dot_nn(low, w_ref[0]) + bqv_ref[0:1, :]).astype(BF)
    q_ref[...] = q_low * BF(HEAD_DIM ** (-0.5))
    k_ref[...] = dot_nn(low, w_ref[1]).astype(BF)
    v_ref[...] = (dot_nn(low, w_ref[2]) + bqv_ref[1:2, :]).astype(BF)


def project(x, gain, bias, bqv, raw):
    rows, width = x.shape
    blocks = raw.shape[1]
    row_spec = pl.BlockSpec((TILE, width), lambda i: (i, 0))
    return pl.pallas_call(
        functools.partial(qkv_kernel, blocks),
        grid=(rows // TILE,),
        in_specs=[
            row_spec,
            once((1, width), lambda i: (0, 0)),
            once((1, width), lambda i: (0, 0)),
            once((2, width), lambda i: (0, 0)),
            once(raw.shape, lambda i: (0, 0, 0, 0)),
        ],
        out_specs=[row_spec] * 4 + [once((4, width, width), lambda i: (0, 0, 0))],
        out_shape=[jax.ShapeDtypeStruct((rows, width), BF)] * 4
        + [jax.ShapeDtypeStruct((4, width, width), BF)],
        compiler_params=params(),
        name="project",
    )(x, gain, bias, bqv, raw)


def half_masks():
    lane = lax.broadcasted_iota(jnp.int32, (1, PAIR), 1)
    first = (lane < HEAD_DIM).astype(F32)
    return first.astype(BF), (1.0 - first).astype(BF)


def attend_kernel(len_ref, q_ref, k_ref, v_ref, o_ref, lse_ref):
    rows = q_ref.shape[0]
    length = len_ref[0]
    masks = half_masks()
    lane = lax.broadcasted_iota(jnp.int32, (TILE, PAIR), 1)
    k_pos = lax.broadcasted_iota(jnp.int32, (1, rows), 1)
    bias = jnp.where(k_pos < length, 0.0, NEG_BIG)
    tri = lax.broadcasted_iota(jnp.int32, (TILE, TILE), 0) >= lax.broadcasted_iota(
        jnp.int32, (TILE, TILE), 1
    )
    for n in range(0, rows, TILE):
        q_block = q_ref[n : n + TILE, :]
        outs = []
        lses = []
        for mask in masks:
            q_one = q_block * mask
            s_diag = dot_nt(q_one, k_ref[n : n + TILE, :]) + bias[:, n : n + TILE]
            s_diag = jnp.where(tri, s_diag, NEG_BIG)
            peak = jnp.max(s_diag, axis=1, keepdims=True)
            if n:
                s_rest = dot_nt(q_one, k_ref[:n, :]) + bias[:, :n]
                peak = jnp.maximum(peak, jnp.max(s_rest, axis=1, keepdims=True))
            e_diag = jnp.exp(s_diag - peak)
            total = jnp.sum(e_diag, axis=1, keepdims=True)
            acc = dot_nn(e_diag.astype(BF), v_ref[n : n + TILE, :])
            if n:
                e_rest = jnp.exp(s_rest - peak)
                total = total + jnp.sum(e_rest, axis=1, keepdims=True)
                acc = acc + dot_nn(e_rest.astype(BF), v_ref[:n, :])
            outs.append(acc / total)
            lses.append(peak + jnp.log(total))
        o_ref[n : n + TILE, :] = jnp.where(lane < HEAD_DIM, outs[0], outs[1]).astype(BF)
        both = jnp.where(lane == 0, lses[0], jnp.where(lane == 1, lses[1], 0.0))
        lse_ref[0, :, n : n + TILE] = jnp.transpose(both)[:8, :]


def attend(lengths, q, k, v):
    rows, width = q.shape
    pairs = width // PAIR
    pair_spec = pl.BlockSpec((rows, PAIR), lambda i, *_: (0, i))
    return pl.pallas_call(
        attend_kernel,
        grid_spec=pltpu.PrefetchScalarGridSpec(
            num_scalar_prefetch=1,
            grid=(pairs,),
            in_specs=[pair_spec] * 3,
            out_specs=[pair_spec, pl.BlockSpec((1, 8, rows), lambda i, *_: (i, 0, 0))],
        ),
        out_shape=[
            jax.ShapeDtypeStruct((rows, width), BF),
            jax.ShapeDtypeStruct((pairs, 8, rows), F32),
        ],
        compiler_params=params(),
        name="attend",
    )(lengths, q, k, v)


def attend_back_kernel(
    len_ref, q_ref, k_ref, v_ref, o_ref, do_ref, lse_ref, dq_ref, dk_ref, dv_ref, dq_acc
):
    rows = q_ref.shape[0]
    length = len_ref[0]
    masks = half_masks()
    prod = jnp.transpose(do_ref[...].astype(F32) * o_ref[...].astype(F32))
    tri = lax.broadcasted_iota(jnp.int32, (TILE, TILE), 0) <= lax.broadcasted_iota(
        jnp.int32, (TILE, TILE), 1
    )
    k_pos = lax.broadcasted_iota(jnp.int32, (TILE, 1), 0)
    dq_acc[...] = jnp.zeros_like(dq_acc)
    heads = []
    for h, mask in enumerate(masks):
        heads.append(
            (
                mask,
                q_ref[...] * mask,
                do_ref[...] * mask,
                lse_ref[0, h : h + 1, :],
                jnp.sum(prod[h * HEAD_DIM : (h + 1) * HEAD_DIM, :], axis=0, keepdims=True),
            )
        )
    for n in range(0, rows, TILE):
        k_block = k_ref[n : n + TILE, :]
        v_block = v_ref[n : n + TILE, :]
        bias = jnp.where(k_pos + n < length, 0.0, NEG_BIG)
        dk = jnp.zeros((TILE, PAIR), F32)
        dv = jnp.zeros((TILE, PAIR), F32)
        for mask, q_one, do_one, lse, delta in heads:
            k_one = k_block * mask
            for low, high in ((n, n + TILE), (n + TILE, rows)):
                if low == high:
                    continue
                s = dot_nt(k_block, q_one[low:high]) + bias
                if low == n:
                    s = jnp.where(tri, s, NEG_BIG)
                p = jnp.exp(s - lse[:, low:high])
                dp = dot_nt(v_block, do_one[low:high])
                ds = (p * (dp - delta[:, low:high])).astype(BF)
                dv = dv + dot_nn(p.astype(BF), do_one[low:high])
                dk = dk + dot_nn(ds, q_one[low:high])
                dq_acc[low:high, :] += dot_tn(ds, k_one)
        dk_ref[n : n + TILE, :] = dk.astype(BF)
        dv_ref[n : n + TILE, :] = dv.astype(BF)
    dq_ref[...] = (dq_acc[...] * (HEAD_DIM ** (-0.5))).astype(BF)


def attend_back(lengths, q, k, v, out, d_out, lse):
    rows, width = q.shape
    pairs = width // PAIR
    pair_spec = pl.BlockSpec((rows, PAIR), lambda i, *_: (0, i))
    return pl.pallas_call(
        attend_back_kernel,
        grid_spec=pltpu.PrefetchScalarGridSpec(
            num_scalar_prefetch=1,
            grid=(pairs,),
            in_specs=[pair_spec] * 5 + [pl.BlockSpec((1, 8, rows), lambda i, *_: (i, 0, 0))],
            out_specs=[pair_spec] * 3,
            scratch_shapes=[pltpu.VMEM((rows, PAIR), F32)],
        ),
        out_shape=[jax.ShapeDtypeStruct((rows, width), BF)] * 3,
        compiler_params=params(),
        name="attend_back",
    )(lengths, q, k, v, out, d_out, lse)


def mlp_kernel(
    att_ref, x_ref, cot_ref, wo_ref, vec_ref, bup_ref, wm_ref,
    hid_ref, dres_ref, datt_ref, go_ref, gm_ref, sums_ref, gbup_ref,
    resid, n_two, mlp, d_norm, act_s, dpre_s,
):
    rows, width = x_ref.shape
    step = pl.program_id(0)
    last = pl.num_programs(0) - 1
    tiles = rows // TILE
    nd, _, block, _ = wm_ref.shape

    def tile(i):
        return pl.ds(pl.multiple_of(i * TILE, TILE), TILE)

    def vec(i):
        return vec_ref[i : i + 1, :]

    @pl.when(step == 0)
    def _():
        def body(i, _):
            r = tile(i)
            res = x_ref[r, :].astype(F32) + dot_nt(att_ref[r, :], wo_ref[0]) + vec(0)
            resid[r, :] = res
            normed, _ = norm_parts(res)
            n_two[r, :] = (normed * vec(1) + vec(2)).astype(BF)
            mlp[r, :] = jnp.zeros((TILE, width), F32)
            d_norm[r, :] = jnp.zeros((TILE, width), F32)
            return 0

        lax.fori_loop(0, tiles, body, 0)

    w_up = wm_ref[:, 0, :, :width].reshape(width, width)
    w_down = wm_ref[:, 0, :, width:].reshape(width, width)
    c_one = 0.7978845608028654
    c_two = 0.044715

    def body(i, total):
        r = tile(i)
        u = dot_nn(n_two[r, :], w_up) + bup_ref[0]
        d_act = dot_nn(cot_ref[r, :], w_down)
        square = u * u
        t = jnp.tanh(c_one * u * (1.0 + c_two * square))
        half = 0.5 * (1.0 + t)
        act = (u * half).astype(BF)
        slope = half + 0.5 * u * (1.0 - t * t) * (c_one * (1.0 + 3.0 * c_two * square))
        d_pre = (d_act * slope).astype(BF)
        act_s[r, :] = act
        dpre_s[r, :] = d_pre
        mlp[r, :] += dot_nt(act, w_down)
        d_norm[r, :] += dot_nt(d_pre, w_up)
        return total + col_sum(d_pre.astype(F32))

    gbup_ref[0] = lax.fori_loop(0, tiles, body, jnp.zeros((1, width), F32))
    per = max(nd // 2, 1)
    for d in range(0, nd, per):
        cols = slice(d * block, (d + per) * block)
        gm_ref[d : d + per, 0, :, :width] = (
            dot_tn(n_two[:, cols], dpre_s[...]).astype(BF).reshape(per, block, width)
        )
        gm_ref[d : d + per, 0, :, width:] = (
            dot_tn(cot_ref[:, cols], act_s[...]).astype(BF).reshape(per, block, width)
        )

    @pl.when(step == last)
    def _():
        def body(i, sums):
            r = tile(i)
            res = resid[r, :]
            hid_ref[r, :] = (res + mlp[r, :] + vec(3)).astype(BF)
            normed, scale = norm_parts(res)
            d_n = d_norm[r, :]
            d_out = cot_ref[r, :].astype(F32)
            d_res = d_out + norm_back(d_n * vec(1), normed, scale)
            dres_ref[r, :] = d_res
            low = d_res.astype(BF)
            act_s[r, :] = low
            datt_ref[r, :] = dot_nn(low, wo_ref[0]).astype(BF)
            more = (col_sum(d_n * normed), col_sum(d_n), col_sum(d_res), col_sum(d_out))
            return tuple(a + b for a, b in zip(sums, more, strict=True))

        sums = lax.fori_loop(0, tiles, body, (jnp.zeros((1, width), F32),) * 4)
        for i in range(4):
            sums_ref[i : i + 1, :] = sums[i]
        half = width // 2
        for c in range(0, width, half):
            go_ref[c : c + half, :] = dot_tn(act_s[:, c : c + half], att_ref[...]).astype(BF)


def feed_forward(att, x, cot, w_all, vecs, b_up, w_mlp):
    rows, width = x.shape
    nd, blocks, block, wide = w_mlp.shape
    whole = once((rows, width), lambda t: (0, 0))
    chunk = pl.BlockSpec((nd, 1, block, wide), lambda t: (0, t, 0, 0))
    up_vec = pl.BlockSpec((1, 1, width), lambda t: (t, 0, 0))
    return pl.pallas_call(
        mlp_kernel,
        grid=(blocks,),
        in_specs=[
            whole,
            whole,
            whole,
            once((1, width, width), lambda t: (3, 0, 0)),
            once((8, width), lambda t: (0, 0)),
            up_vec,
            chunk,
        ],
        out_specs=[
            whole,
            whole,
            whole,
            once((width, width), lambda t: (0, 0)),
            chunk,
            once((8, width), lambda t: (0, 0)),
            up_vec,
        ],
        out_shape=[
            jax.ShapeDtypeStruct((rows, width), BF),
            jax.ShapeDtypeStruct((rows, width), F32),
            jax.ShapeDtypeStruct((rows, width), BF),
            jax.ShapeDtypeStruct((width, width), BF),
            jax.ShapeDtypeStruct(w_mlp.shape, BF),
            jax.ShapeDtypeStruct((8, width), F32),
            jax.ShapeDtypeStruct((blocks, 1, width), F32),
        ],
        scratch_shapes=[
            pltpu.VMEM((rows, width), F32),
            pltpu.VMEM((rows, width), BF),
            pltpu.VMEM((rows, width), F32),
            pltpu.VMEM((rows, width), F32),
            pltpu.VMEM((rows, width), BF),
            pltpu.VMEM((rows, width), BF),
        ],
        compiler_params=params(),
        name="feed_forward",
    )(att, x, cot, w_all, vecs, b_up, w_mlp)


def grad_kernel(blocks, n_ref, dq_ref, dk_ref, dv_ref, go_ref, g_ref):
    per, _, block, _ = g_ref.shape
    rows = per * block
    n_part = n_ref[...]
    full = [dot_tn(n_part, d[...]).astype(BF) for d in (dq_ref, dk_ref, dv_ref)]
    full.append(go_ref[...])

    def put(t, c, value):
        g_ref[:, t, :, c * PAIR : (c + 1) * PAIR] = value.reshape(per, block, PAIR)

    for t in range(blocks):
        for c in range(4):
            put(t, c, full[c][:, t * PAIR : (t + 1) * PAIR])
    for u in range(blocks // 2):
        col = (blocks + u) * PAIR
        for half in range(2):
            left = full[2 * half][:, col : col + PAIR]
            right = full[2 * half + 1][:, col : col + PAIR]
            put(
                2 * u,
                4 + half,
                jnp.concatenate([left[:, :HEAD_DIM], right[:, :HEAD_DIM]], axis=1),
            )
            put(
                2 * u + 1,
                4 + half,
                jnp.concatenate([left[:, HEAD_DIM:], right[:, HEAD_DIM:]], axis=1),
            )


def project_grads(normed, dq, dk, dv, go, shape):
    rows, width = normed.shape
    nd, blocks, block, wide = shape
    parts = 2 if nd > 1 else 1
    part = width // parts
    whole = once((rows, width), lambda i: (0, 0))
    return pl.pallas_call(
        functools.partial(grad_kernel, blocks),
        grid=(parts,),
        in_specs=[
            pl.BlockSpec((rows, part), lambda i: (0, i)),
            whole,
            whole,
            whole,
            pl.BlockSpec((part, width), lambda i: (i, 0)),
        ],
        out_specs=pl.BlockSpec((nd // parts, blocks, block, wide), lambda i: (i, 0, 0, 0)),
        out_shape=jax.ShapeDtypeStruct(shape, BF),
        compiler_params=params(),
        name="project_grads",
    )(normed, dq, dk, dv, go)


def input_kernel(dq_ref, dk_ref, dv_ref, w_ref, x_ref, dres_ref, gain_ref, gin_ref, sums_ref):
    @pl.when(pl.program_id(0) == 0)
    def _():
        sums_ref[...] = jnp.zeros_like(sums_ref)

    d_norm = dot_nt(dq_ref[...], w_ref[0])
    d_norm = d_norm + dot_nt(dk_ref[...], w_ref[1])
    d_norm = d_norm + dot_nt(dv_ref[...], w_ref[2])
    normed, scale = norm_parts(x_ref[...].astype(F32))
    gin_ref[...] = dres_ref[...] + norm_back(d_norm * gain_ref[...], normed, scale)
    more = (
        col_sum(d_norm * normed),
        col_sum(d_norm),
        col_sum(dq_ref[...].astype(F32)),
        col_sum(dv_ref[...].astype(F32)),
    )
    for i, value in enumerate(more):
        sums_ref[i : i + 1, :] += value


def input_grad(dq, dk, dv, w_all, x, d_resid, gain):
    rows, width = x.shape
    row_spec = pl.BlockSpec((TILE, width), lambda i: (i, 0))
    return pl.pallas_call(
        input_kernel,
        grid=(rows // TILE,),
        in_specs=[
            row_spec,
            row_spec,
            row_spec,
            once((3, width, width), lambda i: (0, 0, 0)),
            row_spec,
            row_spec,
            once((1, width), lambda i: (0, 0)),
        ],
        out_specs=[row_spec, pl.BlockSpec((8, width), lambda i: (0, 0))],
        out_shape=[
            jax.ShapeDtypeStruct((rows, width), F32),
            jax.ShapeDtypeStruct((8, width), F32),
        ],
        compiler_params=params(),
        name="input_grad",
    )(dq, dk, dv, w_all, x, d_resid, gain)


def body(
    n_dp,
    n_tensor,
    hidden_in,
    cotangent,
    lengths,
    latent,
    ln1_gain,
    ln1_bias,
    w_qkv,
    b_qv,
    w_out,
    b_out,
    ln2_gain,
    ln2_bias,
    w_up,
    b_up,
    w_down,
    b_down,
):
    rows, width = hidden_in.shape
    t_index = lax.axis_index("tensor")
    block = w_up.shape[0]
    aligned = block % 16 == 0
    heads = w_qkv.shape[2] // HEAD_DIM

    out_t = w_out.T
    packed = jnp.concatenate(
        [w_qkv[0, :, :PAIR], w_qkv[1, :, :PAIR], w_qkv[2, :, :PAIR], out_t[:, :PAIR]]
        + [w_qkv[0, :, PAIR:], w_qkv[1, :, PAIR:], w_qkv[2, :, PAIR:], out_t[:, PAIR:]],
        axis=1,
    ).astype(BF)
    packed_mlp = jnp.concatenate([w_up, w_down.T], axis=1).astype(BF)

    def gather(piece):
        wide = piece.shape[1]
        full = lax.all_gather(piece, BOTH, axis=0, tiled=False)
        full = full.reshape(n_dp, n_tensor, block, wide)
        if aligned:
            return full
        return full.transpose(1, 0, 2, 3).reshape(1, n_tensor, width, wide)

    raw = gather(packed)
    w_mlp = gather(packed_mlp)

    own_length = lax.dynamic_slice_in_dim(lengths, t_index, 1, 0)
    own_latent = lax.dynamic_slice_in_dim(latent, t_index, 1, 0)
    positions = lax.broadcasted_iota(jnp.int32, (1, rows), 1)
    keep = ((positions < own_length) & (own_latent == 0)).astype(BF).reshape(rows, 1)
    cot = cotangent * keep

    def to_inner(b):
        split = b.reshape(b.shape[0], n_tensor, heads, HEAD_DIM)
        return jnp.concatenate(
            [split[:, :, :2].reshape(b.shape[0], -1), split[:, :, 2:].reshape(b.shape[0], -1)],
            axis=1,
        )

    def from_inner(b):
        cut = n_tensor * PAIR
        first = b[:, :cut].reshape(b.shape[0], n_tensor, 2, HEAD_DIM)
        rest = b[:, cut:].reshape(b.shape[0], n_tensor, heads - 2, HEAD_DIM)
        return jnp.concatenate([first, rest], axis=2).reshape(b.shape[0], width)

    q, k, v, normed_one, w_all = project(
        hidden_in, ln1_gain[None], ln1_bias[None], to_inner(b_qv), raw
    )
    attended, lse = attend(own_length, q, k, v)
    zero = jnp.zeros_like(b_out)
    vecs = jnp.stack([b_out, ln2_gain, ln2_bias, b_down, zero, zero, zero, zero])
    hidden_out, d_resid, d_attended, go, gm, sums_two, g_b_up = feed_forward(
        attended, hidden_in, cot, w_all, vecs, b_up.reshape(n_tensor, 1, width), w_mlp
    )
    dq, dk, dv = attend_back(own_length, q, k, v, attended, d_attended, lse)
    ga = project_grads(normed_one, dq, dk, dv, go, raw.shape)
    grad_in, sums_one = input_grad(dq, dk, dv, w_all, hidden_in, d_resid, ln1_gain[None])

    def scatter(grads):
        wide = grads.shape[3]
        if not aligned:
            grads = grads.reshape(n_tensor, n_dp, block, wide).transpose(1, 0, 2, 3)
        flat = grads.reshape(n_dp * n_tensor * block, wide)
        return lax.psum_scatter(flat, BOTH, scatter_dimension=0, tiled=True).astype(F32)

    gm = scatter(gm)
    ga = scatter(ga)
    small = lax.psum(
        jnp.concatenate([sums_one[:4], sums_two[:4], g_b_up.reshape(n_tensor, width)]), BOTH
    )
    g_bqv = from_inner(small[2:4])

    def both_parts(i):
        side = 4 * PAIR + i * HEAD_DIM
        return jnp.concatenate(
            [ga[:, i * PAIR : (i + 1) * PAIR], ga[:, side : side + HEAD_DIM]], axis=1
        )

    return (
        hidden_out,
        grad_in,
        small[0],
        small[1],
        jnp.stack([both_parts(0), both_parts(1), both_parts(2)]),
        g_bqv,
        both_parts(3).T,
        small[6],
        small[4],
        small[5],
        gm[:, :width],
        small[8:].reshape(-1),
        gm[:, width:].T,
        small[7],
    )


def solution(mesh):
    placed = (
        P(BOTH, None),
        P(BOTH, None),
        P("dp"),
        P("dp", None),
        P(),
        P(),
        P(None, "dp", "tensor"),
        P(),
        P("tensor", "dp"),
        P(),
        P(),
        P(),
        P("dp", "tensor"),
        P(),
        P("tensor", "dp"),
        P(),
    )
    return jax.shard_map(
        functools.partial(body, mesh.shape["dp"], mesh.shape["tensor"]),
        mesh=mesh,
        in_specs=placed,
        out_specs=(
            P(BOTH, None),
            P(BOTH, None),
            P(),
            P(),
            P(None, "dp", "tensor"),
            P(),
            P("tensor", "dp"),
            P(),
            P(),
            P(),
            P("dp", "tensor"),
            P(),
            P("tensor", "dp"),
            P(),
        ),
        check_vma=False,
    )
```

```python
import functools

import jax
import jax.numpy as jnp
from jax import lax
from jax.experimental import pallas as pl
from jax.experimental.pallas import tpu as pltpu
from jax.sharding import PartitionSpec as P

HEAD_DIM = 64
LEN = 1024
PAIR = 2 * HEAD_DIM
TILE = 256
NEG_BIG = -1e30
EPSILON = 1e-05
VMEM_BYTES = 66_900_000
BF = jnp.bfloat16
F32 = jnp.float32
BOTH = ("dp", "tensor")


def dot_nn(a, b):
    return lax.dot_general(a, b, (((1,), (0,)), ((), ())), preferred_element_type=F32)


def dot_nt(a, b):
    return lax.dot_general(a, b, (((1,), (1,)), ((), ())), preferred_element_type=F32)


def dot_tn(a, b):
    return lax.dot_general(a, b, (((0,), (0,)), ((), ())), preferred_element_type=F32)


def norm_parts(rows_in):
    center = rows_in - jnp.mean(rows_in, axis=-1, keepdims=True)
    spread = jnp.mean(center * center, axis=-1, keepdims=True)
    scale = lax.rsqrt(spread + EPSILON)
    return center * scale, scale


def norm_back(gy, normed, scale):
    mean_gy = jnp.mean(gy, axis=-1, keepdims=True)
    mean_gyn = jnp.mean(gy * normed, axis=-1, keepdims=True)
    return (gy - mean_gy - normed * mean_gyn) * scale


def col_sum(values):
    return jnp.sum(values, axis=0, keepdims=True)


def once(shape, index):
    return pl.BlockSpec(shape, index, pipeline_mode=pl.Buffered(1))


def params(side_effects=False):
    return pltpu.CompilerParams(
        dimension_semantics=("arbitrary",),
        vmem_limit_bytes=VMEM_BYTES,
        has_side_effects=side_effects,
    )


def cost(flops, moved, exps=0):
    return pl.CostEstimate(flops=int(flops), bytes_accessed=int(moved), transcendentals=int(exps))


def place_of(index):
    return (index >> 3) & 3, (index >> 2) & 1, (index >> 1) & 1, index & 1


def index_of(z, x, y, core):
    return (z << 3) | (x << 2) | (y << 1) | core


def exchange(array, flip):
    pairs = [(i, index_of(*flip(*place_of(i)))) for i in range(32)]
    return lax.ppermute(array, BOTH, pairs)


def flip_first(z, x, y, core):
    return (z, x, y ^ 1, core) if core else (z, x ^ 1, y, core)


def flip_second(z, x, y, core):
    return (z, x ^ 1, y, core) if core else (z, x, y ^ 1, core)


def flip_core(z, x, y, core):
    return z, x, y, core ^ 1


def flip_near(z, x, y, core):
    return z ^ 1, x, y, core


def flip_far(z, x, y, core):
    return z ^ 2, x, y, core


class Scatter:
    def __init__(self, kept, sent):
        self.terms, self.sent = [kept], sent
        self.flips = [flip_core, flip_second, flip_first, flip_far, flip_near]

    def step(self):
        return exchange(self.sent, self.flips.pop(0))

    def add(self, came):
        self.terms.append(came)
        count = came.shape[0] // 2
        total = self.terms[0][count : 2 * count].astype(F32)
        for term in self.terms[1:]:
            total = total + term[count : 2 * count].astype(F32)
        self.sent = total.astype(BF)

    def last(self, came):
        total = came[0].astype(F32)
        for term in self.terms:
            total = total + term[0].astype(F32)
        return total


def after(value, *others):
    return lax.optimization_barrier((value, *others))


def start_blocks(place_ref, sources, cols, raw, to, sems):
    if len(sources) == 1:
        nd, blocks, block, _ = sources[0].shape
        for d in range(nd):
            for t in range(blocks):
                pltpu.make_async_copy(
                    sources[0].at[d, t, :, cols],
                    raw.at[t, d * block : (d + 1) * block, to],
                    sems.at[t],
                ).start()
        return
    z, x, y, core = (place_ref[i] for i in range(4))
    block = sources[0].shape[1]
    for i, source in enumerate(sources):
        for slot in range(8):
            to_core = core ^ (i >> 1)
            second, first = i & 1, slot >> 2
            to_x = x ^ (first + to_core * (second - first))
            to_y = y ^ (second + to_core * (first - second))
            to_z = z ^ (slot & 3)
            to_t = to_y * 2 + to_core
            low = pl.multiple_of((to_z * 2 + to_x) * block, block)
            pltpu.make_async_copy(
                source.at[slot, :, cols], raw.at[to_t, pl.ds(low, block), to], sems.at[to_t]
            ).start()


def wait_all(ref, sem):
    pltpu.make_async_copy(ref, ref, sem).wait()


def send_block(place_ref, staged, outs, sem, d, t):
    z, x, y, core = (place_ref[i] for i in range(4))
    far, near_core = d >> 1, t & 1
    x_off, y_off = x ^ (d & 1), y ^ (t >> 1)
    first, second = (y_off, x_off) if near_core else (x_off, y_off)
    slot = second * 8 + first * 4 + (z ^ far)
    for side in range(2):

        @pl.when((core ^ near_core) == side)
        def _(side=side):
            pltpu.make_async_copy(staged, outs[side].at[slot], sem).start()


def send_rows(place_ref, stage, outs, sem, t, cols):
    if len(outs) == 1:
        pltpu.make_async_copy(stage, outs[0].at[t, :, cols], sem).start()
        return
    block = outs[0].shape[1]
    for d in range(8):
        staged = stage.at[d * block : (d + 1) * block, :]
        send_block(place_ref, staged, [out.at[:, :, cols] for out in outs], sem, d, t)


ANY_SPEC = pl.BlockSpec(memory_space=pl.ANY)


def qkv_kernel(count, place_ref, x_ref, gain_ref, bias_ref, bqv_ref, *refs):
    sources = refs[:count]
    q_ref, k_ref, v_ref, n_ref, w_ref, raw, sems = refs[count:]
    blocks = raw.shape[0]
    normed, _ = norm_parts(x_ref[...].astype(F32))
    low = (normed * gain_ref[...] + bias_ref[...]).astype(BF)
    n_ref[...] = low

    @pl.when(pl.program_id(0) == 0)
    def _():
        cols = slice(0, raw.shape[2])
        start_blocks(place_ref, sources, cols, raw, cols, sems)
        for t in range(blocks):
            wait_all(raw.at[t], sems.at[t])

        def piece(t, c):
            return raw[t, :, c * PAIR : (c + 1) * PAIR]

        for t in range(blocks):
            for c in range(4):
                w_ref[c, :, t * PAIR : (t + 1) * PAIR] = piece(t, c)
        for u in range(blocks // 2):
            col = (blocks + u) * PAIR
            for half in range(2):
                left = piece(2 * u, 4 + half)
                right = piece(2 * u + 1, 4 + half)
                w_ref[2 * half, :, col : col + PAIR] = jnp.concatenate(
                    [left[:, :HEAD_DIM], right[:, :HEAD_DIM]], axis=1
                )
                w_ref[2 * half + 1, :, col : col + PAIR] = jnp.concatenate(
                    [left[:, HEAD_DIM:], right[:, HEAD_DIM:]], axis=1
                )

    q_low = (dot_nn(low, w_ref[0]) + bqv_ref[0:1, :]).astype(BF)
    q_ref[...] = q_low * BF(HEAD_DIM ** (-0.5))
    k_ref[...] = dot_nn(low, w_ref[1]).astype(BF)
    v_ref[...] = (dot_nn(low, w_ref[2]) + bqv_ref[1:2, :]).astype(BF)


def project(place, x, gain, bias, bqv, sources, blocks):
    rows, width = x.shape
    row_spec = pl.BlockSpec((TILE, width), lambda i, *_: (i, 0))
    return pl.pallas_call(
        functools.partial(qkv_kernel, len(sources)),
        grid_spec=pltpu.PrefetchScalarGridSpec(
            num_scalar_prefetch=1,
            grid=(rows // TILE,),
            in_specs=[
                row_spec,
                once((1, width), lambda i, *_: (0, 0)),
                once((1, width), lambda i, *_: (0, 0)),
                once((2, width), lambda i, *_: (0, 0)),
            ]
            + [ANY_SPEC] * len(sources),
            out_specs=[row_spec] * 4 + [once((4, width, width), lambda i, *_: (0, 0, 0))],
            scratch_shapes=[
                pltpu.VMEM((blocks, width, sources[0].shape[-1]), BF),
                pltpu.SemaphoreType.DMA((blocks,)),
            ],
        ),
        out_shape=[jax.ShapeDtypeStruct((rows, width), BF)] * 4
        + [jax.ShapeDtypeStruct((4, width, width), BF)],
        compiler_params=params(),
        cost_estimate=cost(6 * rows * width * width, 16 * rows * width),
        name="project",
    )(place, x, gain, bias, bqv, *sources)


def half_masks():
    lane = lax.broadcasted_iota(jnp.int32, (1, PAIR), 1)
    first = (lane < HEAD_DIM).astype(F32)
    return first.astype(BF), (1.0 - first).astype(BF)


def attend_kernel(len_ref, q_ref, k_ref, v_ref, o_ref, lse_ref):
    rows = q_ref.shape[0]
    length = len_ref[0]
    masks = half_masks()
    lane = lax.broadcasted_iota(jnp.int32, (TILE, PAIR), 1)
    k_pos = lax.broadcasted_iota(jnp.int32, (1, rows), 1)
    bias = jnp.where(k_pos < length, 0.0, NEG_BIG)
    tri = lax.broadcasted_iota(jnp.int32, (TILE, TILE), 0) >= lax.broadcasted_iota(
        jnp.int32, (TILE, TILE), 1
    )
    for n in range(0, rows, TILE):
        q_block = q_ref[n : n + TILE, :]
        outs = []
        lses = []
        for mask in masks:
            q_one = q_block * mask
            s_diag = dot_nt(q_one, k_ref[n : n + TILE, :]) + bias[:, n : n + TILE]
            s_diag = jnp.where(tri, s_diag, NEG_BIG)
            peak = jnp.max(s_diag, axis=1, keepdims=True)
            if n:
                s_rest = dot_nt(q_one, k_ref[:n, :]) + bias[:, :n]
                peak = jnp.maximum(peak, jnp.max(s_rest, axis=1, keepdims=True))
            e_diag = jnp.exp(s_diag - peak)
            total = jnp.sum(e_diag, axis=1, keepdims=True)
            acc = dot_nn(e_diag.astype(BF), v_ref[n : n + TILE, :])
            if n:
                e_rest = jnp.exp(s_rest - peak)
                total = total + jnp.sum(e_rest, axis=1, keepdims=True)
                acc = acc + dot_nn(e_rest.astype(BF), v_ref[:n, :])
            outs.append(acc / total)
            lses.append(peak + jnp.log(total))
        o_ref[n : n + TILE, :] = jnp.where(lane < HEAD_DIM, outs[0], outs[1]).astype(BF)
        both = jnp.where(lane == 0, lses[0], jnp.where(lane == 1, lses[1], 0.0))
        lse_ref[0, :, n : n + TILE] = jnp.transpose(both)[:8, :]


def attend(lengths, q, k, v):
    rows, width = q.shape
    pairs = width // PAIR
    pair_spec = pl.BlockSpec((rows, PAIR), lambda i, *_: (0, i))
    return pl.pallas_call(
        attend_kernel,
        grid_spec=pltpu.PrefetchScalarGridSpec(
            num_scalar_prefetch=1,
            grid=(pairs,),
            in_specs=[pair_spec] * 3,
            out_specs=[pair_spec, pl.BlockSpec((1, 8, rows), lambda i, *_: (i, 0, 0))],
        ),
        out_shape=[
            jax.ShapeDtypeStruct((rows, width), BF),
            jax.ShapeDtypeStruct((pairs, 8, rows), F32),
        ],
        compiler_params=params(),
        cost_estimate=cost(16e9 * width / 768, 8 * rows * width),
        name="attend",
    )(lengths, q, k, v)


def attend_back_kernel(
    first, n_out, more, len_ref, place_ref, q_ref, k_ref, v_ref, o_ref, do_ref, lse_ref, n_ref, *refs
):
    refs = refs[n_out:] if more else refs
    dq_ref, dk_ref, dv_ref = refs[:3]
    outs = refs[3 : 3 + n_out]
    dq_acc, side_s, stage, sem = refs[3 + n_out :]
    rows = q_ref.shape[0]
    width = n_ref.shape[1]
    step = pl.program_id(0)
    length = len_ref[0]
    masks = half_masks()
    wide = stage.shape[2]
    narrow = wide != 3 * PAIR

    prod = jnp.transpose(do_ref[...].astype(F32) * o_ref[...].astype(F32))
    tri = lax.broadcasted_iota(jnp.int32, (TILE, TILE), 0) <= lax.broadcasted_iota(
        jnp.int32, (TILE, TILE), 1
    )
    k_pos = lax.broadcasted_iota(jnp.int32, (TILE, 1), 0)
    dq_acc[...] = jnp.zeros_like(dq_acc)
    heads = []
    for h, mask in enumerate(masks):
        heads.append(
            (
                mask,
                q_ref[...] * mask,
                do_ref[...] * mask,
                lse_ref[0, h : h + 1, :],
                jnp.sum(prod[h * HEAD_DIM : (h + 1) * HEAD_DIM, :], axis=0, keepdims=True),
            )
        )
    for n in range(0, rows, TILE):
        k_block = k_ref[n : n + TILE, :]
        v_block = v_ref[n : n + TILE, :]
        bias = jnp.where(k_pos + n < length, 0.0, NEG_BIG)
        dk = jnp.zeros((TILE, PAIR), F32)
        dv = jnp.zeros((TILE, PAIR), F32)
        for mask, q_one, do_one, lse, delta in heads:
            k_one = k_block * mask
            for low, high in ((n, n + TILE), (n + TILE, rows)):
                if low == high:
                    continue
                s = dot_nt(k_block, q_one[low:high]) + bias
                if low == n:
                    s = jnp.where(tri, s, NEG_BIG)
                p = jnp.exp(s - lse[:, low:high])
                dp = dot_nt(v_block, do_one[low:high])
                ds = (p * (dp - delta[:, low:high])).astype(BF)
                dv = dv + dot_nn(p.astype(BF), do_one[low:high])
                dk = dk + dot_nn(ds, q_one[low:high])
                dq_acc[low:high, :] += dot_tn(ds, k_one)
        dk_ref[n : n + TILE, :] = dk.astype(BF)
        dv_ref[n : n + TILE, :] = dv.astype(BF)
    dq_ref[...] = (dq_acc[...] * (HEAD_DIM ** (-0.5))).astype(BF)

    grads = [dq_ref[...], dk_ref[...], dv_ref[...]]
    if narrow:
        blank = jnp.zeros((rows, HEAD_DIM), BF)
        sides = [
            jnp.concatenate([g[:, c : c + HEAD_DIM] for g in grads] + [blank], axis=1)
            for c in (0, HEAD_DIM)
        ]
    else:
        sides = [jnp.concatenate(grads, axis=1)]
    for at in range(2):

        @pl.when(step == at)
        def _(at=at):
            for i, side in enumerate(sides):
                spot = at * len(sides) + i
                side_s[:, spot * wide : (spot + 1) * wide] = side

    @pl.when(step == 1)
    def _():
        low_col = 3 * PAIR if narrow else 0
        for low in range(0, width, TILE):
            cols = slice(low, low + TILE)
            grad = dot_tn(n_ref[:, cols], side_s[...]).astype(BF)
            for spot in range(stage.shape[0]):
                stage[spot, cols, :] = grad[:, spot * wide : (spot + 1) * wide]
        for spot in range(stage.shape[0]):
            t = spot if narrow else first + spot
            send_rows(place_ref, stage.at[spot], outs, sem, t, slice(low_col, low_col + wide))
        wait_all(stage, sem)


def attend_back(place, lengths, first, wide, q, k, v, out, d_out, lse, normed, blocks, so_far, fast):
    rows, width = q.shape
    at_pair = pl.BlockSpec((rows, PAIR), lambda i, *_: (0, first + i))
    own_pair = pl.BlockSpec((rows, PAIR), lambda i, *_: (0, i))
    grads = grad_shapes(fast, blocks, width, 5 * PAIR)
    so_far = so_far or []
    sides = 1 if wide == 3 * PAIR else 2
    return pl.pallas_call(
        functools.partial(attend_back_kernel, first, len(grads), bool(so_far)),
        grid_spec=pltpu.PrefetchScalarGridSpec(
            num_scalar_prefetch=2,
            grid=(2,),
            in_specs=[at_pair] * 5
            + [
                pl.BlockSpec((1, 8, rows), lambda i, *_: (first + i, 0, 0)),
                once((rows, width), lambda i, *_: (0, 0)),
            ]
            + [ANY_SPEC] * len(so_far),
            out_specs=[own_pair] * 3 + [ANY_SPEC] * len(grads),
            scratch_shapes=[
                pltpu.VMEM((rows, PAIR), F32),
                pltpu.VMEM((rows, 2 * sides * wide), BF),
                pltpu.VMEM((2 * sides, width, wide), BF),
                pltpu.SemaphoreType.DMA(()),
            ],
        ),
        out_shape=[jax.ShapeDtypeStruct((rows, 2 * PAIR), BF)] * 3 + grads,
        input_output_aliases={9 + i: 3 + i for i in range(len(so_far))},
        compiler_params=params(),
        cost_estimate=cost(11e9, 10e6),
        name="attend_back",
    )(lengths, place, q, k, v, out, d_out, lse, normed, *so_far)


def vec_rows(vec_ref):
    return lambda i: vec_ref[i : i + 1, :]


def tile_rows(i):
    return pl.ds(pl.multiple_of(i * TILE, TILE), TILE)


def grad_shapes(fast, blocks, width, wide):
    if fast:
        return [jax.ShapeDtypeStruct((16, width // 8, wide), BF)] * 2
    return [jax.ShapeDtypeStruct((blocks, width, wide), BF)]


def feed_kernel(
    counts, place_ref, att_ref, x_ref, cot_ref, wo_ref, vec_ref, bup_ref, *refs
):
    one, two = counts
    refs, sources = refs[one + two :], (refs[:one], refs[one : one + two])
    resid_ref, act_ref, g_ref, gbup_ref, dres_ref, datt_ref, sums_ref = refs[:7]
    outs = refs[7:-8]
    raw, sems, n_two, d_pre_s, d_norm, low, stage, sem = refs[-8:]
    rows, width = x_ref.shape
    step = pl.program_id(0)
    tiles = rows // TILE
    blocks = stage.shape[0]
    vec = vec_rows(vec_ref)
    half_width = width // 2
    nd, _, block, wide = g_ref.shape
    cut = wide // 2
    left = width - cut

    @pl.when(step == 0)
    def _():
        begin = 0
        for source, size in zip(sources, (cut, left), strict=True):
            for to in (begin, width + begin):
                start_blocks(
                    place_ref,
                    source,
                    slice(0 if to < width else size, size if to < width else 2 * size),
                    raw,
                    slice(to, to + size),
                    sems,
                )
            begin += size

        def body(i, _):
            r = tile_rows(i)
            res = x_ref[r, :].astype(F32) + dot_nt(att_ref[r, :], wo_ref[0]) + vec(0)
            resid_ref[r, :] = res
            normed, _ = norm_parts(res)
            n_two[r, :] = (normed * vec(1) + vec(2)).astype(BF)
            d_norm[r, :] = jnp.zeros((TILE, width), F32)
            return 0

        lax.fori_loop(0, tiles, body, 0, unroll=True)

    wait_all(raw.at[step], sems.at[step])
    w_up = raw[step, :, :width]
    w_down = raw[step, :, width:]
    c_one = 0.7978845608028654
    c_two = 0.044715

    def body(i, total):
        r = tile_rows(i)
        u = dot_nn(n_two[r, :], w_up) + bup_ref[0]
        d_act = dot_nn(cot_ref[r, :], w_down)
        square = u * u
        t = jnp.tanh(c_one * u * (1.0 + c_two * square))
        half = 0.5 * (1.0 + t)
        act_ref[r, :] = (u * half).astype(BF)
        slope = half + 0.5 * u * (1.0 - t * t) * (c_one * (1.0 + 3.0 * c_two * square))
        d_pre = (d_act * slope).astype(BF)
        d_pre_s[r, :] = d_pre
        d_norm[r, :] += dot_nt(d_pre, w_up)
        return total + col_sum(d_pre.astype(F32))

    gbup_ref[0] = lax.fori_loop(0, tiles, body, jnp.zeros((1, width), F32), unroll=True)
    per = max(nd // 2, 1)
    for d in range(0, nd, per):
        cols = slice(d * block, (d + per) * block)
        for side, source, grad in ((0, n_two, d_pre_s), (1, cot_ref, act_ref)):
            full = dot_tn(source[:, cols], grad[...]).astype(BF)
            g_ref[d : d + per, 0, :, side * cut : (side + 1) * cut] = full[:, :cut].reshape(
                per, block, cut
            )
            stage[step, cols, side * left : (side + 1) * left] = full[:, cut:]
    first_cols = slice(0, 2 * left)
    for t in range(blocks):

        @pl.when(step == t)
        def _(t=t):
            send_rows(place_ref, stage.at[t, :, first_cols], outs, sem, t, first_cols)

    @pl.when(step == pl.num_programs(0) - 1)
    def _():
        def body(i, sums):
            r = tile_rows(i)
            normed, scale = norm_parts(resid_ref[r, :])
            d_n = d_norm[r, :]
            d_out = cot_ref[r, :].astype(F32)
            d_res = d_out + norm_back(d_n * vec(1), normed, scale)
            dres_ref[r, :] = d_res
            d_low = d_res.astype(BF)
            low[r, :] = d_low
            datt_ref[r, :] = dot_nn(d_low, wo_ref[0]).astype(BF)
            more = (col_sum(d_n * normed), col_sum(d_n), col_sum(d_res), col_sum(d_out))
            return tuple(a + b for a, b in zip(sums, more, strict=True))

        sums = lax.fori_loop(0, tiles, body, (jnp.zeros((1, width), F32),) * 4, unroll=True)
        sums_ref[...] = jnp.zeros_like(sums_ref)
        for i in range(4):
            sums_ref[i : i + 1, :] = sums[i]
        side = 2 * left
        for c in range(0, width, half_width):
            rows_c = slice(c, c + half_width)
            go = dot_tn(low[:, rows_c], att_ref[...]).astype(BF)
            blank = jnp.zeros((half_width, HEAD_DIM), BF)
            for t in range(blocks):
                stage[t, rows_c, side : side + PAIR] = go[:, t * PAIR : (t + 1) * PAIR]
                col = blocks * PAIR + t * HEAD_DIM
                stage[t, rows_c, side + PAIR :] = jnp.concatenate(
                    [go[:, col : col + HEAD_DIM], blank], axis=1
                )
        cols = slice(side, side + 2 * PAIR)
        for t in range(blocks):
            send_rows(place_ref, stage.at[t, :, cols], outs, sem, t, cols)
        wait_all(stage, sem)


def feed_forward(place, att, x, cot, w_all, vecs, b_up, sources_one, sources_two, cut, fast):
    rows, width = x.shape
    blocks = b_up.shape[0]
    nd = 8 if fast else 1
    left = width - cut
    whole = once((rows, width), lambda t, *_: (0, 0))
    up_vec = pl.BlockSpec((1, 1, width), lambda t, *_: (t, 0, 0))
    grads = grad_shapes(fast, blocks, width, 2 * left + 2 * PAIR)
    counts = (len(sources_one), len(sources_two))
    return pl.pallas_call(
        functools.partial(feed_kernel, counts),
        grid_spec=pltpu.PrefetchScalarGridSpec(
            num_scalar_prefetch=1,
            grid=(blocks,),
            in_specs=[
                whole,
                whole,
                whole,
                once((1, width, width), lambda t, *_: (3, 0, 0)),
                once((8, width), lambda t, *_: (0, 0)),
                up_vec,
            ]
            + [ANY_SPEC] * sum(counts),
            out_specs=[
                whole,
                pl.BlockSpec((rows, width), lambda t, *_: (0, t)),
                pl.BlockSpec((nd, 1, width // nd, 2 * cut), lambda t, *_: (0, t, 0, 0)),
                up_vec,
                whole,
                whole,
                once((8, width), lambda t, *_: (0, 0)),
            ]
            + [ANY_SPEC] * len(grads),
            scratch_shapes=[
                pltpu.VMEM((blocks, width, 2 * width), BF),
                pltpu.SemaphoreType.DMA((blocks,)),
                pltpu.VMEM((rows, width), BF),
                pltpu.VMEM((rows, width), BF),
                pltpu.VMEM((rows, width), F32),
                pltpu.VMEM((rows, width), BF),
                pltpu.VMEM((blocks, width, 2 * left + 2 * PAIR), BF),
                pltpu.SemaphoreType.DMA(()),
            ],
        ),
        out_shape=[
            jax.ShapeDtypeStruct((rows, width), F32),
            jax.ShapeDtypeStruct((rows, blocks * width), BF),
            jax.ShapeDtypeStruct((nd, blocks, width // nd, 2 * cut), BF),
            jax.ShapeDtypeStruct((blocks, 1, width), F32),
            jax.ShapeDtypeStruct((rows, width), F32),
            jax.ShapeDtypeStruct((rows, width), BF),
            jax.ShapeDtypeStruct((8, width), F32),
        ]
        + grads,
        compiler_params=params(),
        cost_estimate=cost(40e9, 40e6),
        name="feed_forward",
    )(place, att, x, cot, w_all, vecs, b_up, *sources_one, *sources_two)


def hidden_kernel(counts, place_ref, act_ref, resid_ref, vec_ref, *refs):
    one, two = counts
    refs, sources = refs[one + two :], (refs[:one], refs[one : one + two])
    out_ref, raw, sems = refs
    blocks, _, width = raw.shape
    cut = sources[0][0].shape[-1] // 2

    @pl.when(pl.program_id(0) == 0)
    def _():
        begin = 0
        for source, size in zip(sources, (cut, width - cut), strict=True):
            to = slice(begin, begin + size)
            start_blocks(place_ref, source, slice(size, 2 * size), raw, to, sems)
            begin += size
        for t in range(blocks):
            wait_all(raw.at[t], sems.at[t])

    acc = resid_ref[...] + vec_ref[3:4, :]
    for t in range(blocks):
        acc = acc + dot_nt(act_ref[:, t * width : (t + 1) * width], raw[t])
    out_ref[...] = acc.astype(BF)


def hidden_rows(place, act, resid, vecs, sources_one, sources_two):
    rows, width = resid.shape
    blocks = act.shape[1] // width
    row_spec = pl.BlockSpec((TILE, width), lambda i, *_: (i, 0))
    counts = (len(sources_one), len(sources_two))
    return pl.pallas_call(
        functools.partial(hidden_kernel, counts),
        grid_spec=pltpu.PrefetchScalarGridSpec(
            num_scalar_prefetch=1,
            grid=(rows // TILE,),
            in_specs=[
                pl.BlockSpec((TILE, blocks * width), lambda i, *_: (i, 0)),
                row_spec,
                once((8, width), lambda i, *_: (0, 0)),
            ]
            + [ANY_SPEC] * sum(counts),
            out_specs=row_spec,
            scratch_shapes=[
                pltpu.VMEM((blocks, width, width), BF),
                pltpu.SemaphoreType.DMA((blocks,)),
            ],
        ),
        out_shape=jax.ShapeDtypeStruct((rows, width), BF),
        compiler_params=params(),
        cost_estimate=cost(5e9, 12e6),
        name="hidden_rows",
    )(place, act, resid, vecs, *sources_one, *sources_two)


def input_kernel(*refs):
    parts = refs[:9]
    w_ref, x_ref, dres_ref, gain_ref, gin_ref, sums_ref = refs[9:]

    @pl.when(pl.program_id(0) == 0)
    def _():
        sums_ref[...] = jnp.zeros_like(sums_ref)

    dq, dk, dv = (jnp.concatenate([part[...] for part in parts[i::3]], axis=1) for i in range(3))
    d_norm = dot_nt(dq, w_ref[0]) + dot_nt(dk, w_ref[1]) + dot_nt(dv, w_ref[2])
    normed, scale = norm_parts(x_ref[...].astype(F32))
    gin_ref[...] = dres_ref[...] + norm_back(d_norm * gain_ref[...], normed, scale)
    more = (
        col_sum(d_norm * normed),
        col_sum(d_norm),
        col_sum(dq.astype(F32)),
        col_sum(dv.astype(F32)),
    )
    for i, value in enumerate(more):
        sums_ref[i : i + 1, :] += value


def input_grad(parts, w_all, x, d_resid, gain):
    rows, width = x.shape
    row_spec = pl.BlockSpec((TILE, width), lambda i: (i, 0))
    return pl.pallas_call(
        input_kernel,
        grid=(rows // TILE,),
        in_specs=[pl.BlockSpec((TILE, 2 * PAIR), lambda i: (i, 0))] * 9
        + [
            once((3, width, width), lambda i: (0, 0, 0)),
            row_spec,
            row_spec,
            once((1, width), lambda i: (0, 0)),
        ],
        out_specs=[row_spec, pl.BlockSpec((8, width), lambda i: (0, 0))],
        out_shape=[
            jax.ShapeDtypeStruct((rows, width), F32),
            jax.ShapeDtypeStruct((8, width), F32),
        ],
        compiler_params=params(),
        cost_estimate=cost(6 * rows * width * width, 16 * rows * width),
        name="input_grad",
    )(*parts, w_all, x, d_resid, gain)


def body(
    n_dp,
    n_tensor,
    hidden_in,
    cotangent,
    lengths,
    latent,
    ln1_gain,
    ln1_bias,
    w_qkv,
    b_qv,
    w_out,
    b_out,
    ln2_gain,
    ln2_bias,
    w_up,
    b_up,
    w_down,
    b_down,
):
    rows, width = hidden_in.shape
    t_index = lax.axis_index("tensor")
    block = w_up.shape[0]
    heads = w_qkv.shape[2] // HEAD_DIM

    out_t = w_out.T
    packed = jnp.concatenate(
        [w_qkv[0, :, :PAIR], w_qkv[1, :, :PAIR], w_qkv[2, :, :PAIR], out_t[:, :PAIR]]
        + [w_qkv[0, :, PAIR:], w_qkv[1, :, PAIR:], w_qkv[2, :, PAIR:], out_t[:, PAIR:]],
        axis=1,
    ).astype(BF)
    down_t = w_down.T
    cut = w_up.shape[1] * 2 // 3
    packed_one = jnp.concatenate([w_up[:, :cut], down_t[:, :cut]], axis=1).astype(BF)
    packed_two = jnp.concatenate([w_up[:, cut:], down_t[:, cut:]], axis=1).astype(BF)
    own_length = lax.dynamic_slice_in_dim(lengths, t_index, 1, 0)
    own_latent = lax.dynamic_slice_in_dim(latent, t_index, 1, 0)
    positions = lax.broadcasted_iota(jnp.int32, (1, rows), 1)
    keep = ((positions < own_length) & (own_latent == 0)).astype(BF).reshape(rows, 1)
    cot = cotangent * keep

    fast = n_dp == 8 and n_tensor == 4
    d_index = lax.axis_index("dp")
    place = jnp.stack([d_index >> 1, d_index & 1, t_index >> 1, t_index & 1]).astype(jnp.int32)

    def gather(piece):
        wide = piece.shape[1]
        full = lax.all_gather(piece, BOTH, axis=0, tiled=False)
        full = full.reshape(n_dp, n_tensor, block, wide)
        if fast:
            return full
        return full.transpose(1, 0, 2, 3).reshape(1, n_tensor, width, wide)

    project_place = place
    if fast:
        def grow(array, came):
            return jnp.concatenate([array, came])

        att, one = packed[None], packed_one[None]
        sources_two = [gather(packed_two)]
        att_came, one_came, cot = after(exchange(att, flip_near), exchange(one, flip_near), cot)
        att, one = grow(att, att_came), grow(one, one_came)
        att_came, one = after(exchange(att, flip_far), one)
        att = grow(att, att_came)
        att_came, att = after(exchange(att, flip_first), att)
        att, one_came = grow(att, att_came), exchange(one, flip_far)
        att_other, att_core, one_came = after(
            exchange(att, flip_second), exchange(att, flip_core), one_came
        )
        one = grow(one, one_came)
        sources = [att, att_other, att_core, exchange(att_other, flip_core)]
        one_came = exchange(one, flip_first)
    else:
        sources = [gather(packed)]
        sources_one, sources_two = [gather(packed_one)], [gather(packed_two)]

    def to_inner(b):
        split = b.reshape(b.shape[0], n_tensor, heads, HEAD_DIM)
        return jnp.concatenate(
            [split[:, :, :2].reshape(b.shape[0], -1), split[:, :, 2:].reshape(b.shape[0], -1)],
            axis=1,
        )

    def from_inner(b):
        cut = n_tensor * PAIR
        first = b[:, :cut].reshape(b.shape[0], n_tensor, 2, HEAD_DIM)
        rest = b[:, cut:].reshape(b.shape[0], n_tensor, heads - 2, HEAD_DIM)
        return jnp.concatenate([first, rest], axis=2).reshape(b.shape[0], width)

    q, k, v, normed_one, w_all = project(
        place, hidden_in, ln1_gain[None], ln1_bias[None], to_inner(b_qv), sources, n_tensor
    )
    if fast:
        one_came, q = after(one_came, q)
        one, q = after(grow(one, one_came), q)
        one_other, one_core = exchange(one, flip_second), exchange(one, flip_core)
    attended, lse = attend(own_length, q, k, v)
    if fast:
        one_other, one_core, attended = after(one_other, one_core, attended)
        sources_one = [one, one_other, one_core, exchange(one_other, flip_core)]
    zero = jnp.zeros_like(b_out)
    vecs = jnp.stack([b_out, ln2_gain, ln2_bias, b_down, zero, zero, zero, zero])
    up_bias = b_up.reshape(n_tensor, 1, width)
    resid, act, g_one, g_b_up, d_resid, d_attended, sums_two, *g_two = feed_forward(
        place, attended, hidden_in, cot, w_all, vecs, up_bias, sources_one, sources_two, cut, fast
    )

    def scatter_all(grads):
        wide = grads.shape[-1]
        if not fast:
            grads = grads.reshape(n_tensor, n_dp, block, wide).transpose(1, 0, 2, 3)
        flat = grads.reshape(n_dp * n_tensor * block, wide)
        return lax.psum_scatter(flat, BOTH, scatter_dimension=0, tiled=True)

    g_one = scatter_all(g_one)
    def back(length, first, wide, so_far):
        return list(
            attend_back(
                place, length, first, wide, q, k, v, attended, d_attended, lse, normed_one,
                n_tensor, so_far, fast,
            )
        )

    def vectors(sums_one):
        return jnp.concatenate([sums_one[:4], sums_two[:4], g_b_up.reshape(n_tensor, width)])

    gain = ln1_gain[None]
    if fast:
        up = Scatter(*g_two)
        came = up.step()
        back_one = back(own_length, 0, 3 * PAIR, None)
        came, length, *back_one = after(came, own_length, *back_one)
        up.add(came)
        came = up.step()
        back_two = back(length, 2, 3 * PAIR, back_one[3:])
        came, length, *back_two = after(came, own_length, *back_two)
        up.add(came)
        came = up.step()
        back_three = back(length, 4, 2 * PAIR, back_two[3:])
        came, gain, *back_three = after(came, gain, *back_three)
        up.add(came)
        rest = Scatter(*back_three[3:])
        rest.add(rest.step())
        came, came_rest = up.step(), rest.step()
        parts = [*back_one[:3], *back_two[:3], *back_three[:3]]
        grad_in, sums_one = input_grad(parts, w_all, hidden_in, d_resid, gain)
        came_rest, sums_one, last_place = after(came_rest, sums_one, place)
        small = vectors(sums_one)
        small = small + exchange(small, flip_core)
        rest.add(came_rest)
        came_rest, came_small = rest.step(), exchange(small, flip_second)
        hidden_out = hidden_rows(last_place, act, resid, vecs, sources_one, sources_two)
        came, came_rest, came_small, hidden_out = after(came, came_rest, came_small, hidden_out)
        up.add(came)
        rest.add(came_rest)
        small = small + came_small
        came, came_rest, came_small = after(up.step(), rest.step(), exchange(small, flip_first))
        g_two = up.last(came)
        rest.add(came_rest)
        small = small + came_small
        came_rest, came_small = after(rest.step(), exchange(small, flip_far))
        came_rest, g_one = after(came_rest, g_one)
        g_rest = rest.last(came_rest)
        small = small + came_small
        small = small + exchange(small, flip_near)
    else:
        back_one = back(own_length, 0, 3 * PAIR, None)
        back_two = back(own_length, 2, 3 * PAIR, back_one[3:])
        back_three = back(own_length, 4, 2 * PAIR, back_two[3:])
        parts = [*back_one[:3], *back_two[:3], *back_three[:3]]
        grad_in, sums_one = input_grad(parts, w_all, hidden_in, d_resid, gain)
        hidden_out = hidden_rows(place, act, resid, vecs, sources_one, sources_two)
        small = lax.psum(vectors(sums_one), BOTH)
        g_two, g_rest = (scatter_all(g).astype(F32) for g in (g_two[0], back_three[3]))
    g_one = g_one.astype(F32)
    rest_cut = width - cut
    g_out = g_two[:, 2 * rest_cut : 2 * rest_cut + PAIR + HEAD_DIM]
    g_bqv = from_inner(small[2:4])

    def both_parts(i):
        side = 3 * PAIR + i * HEAD_DIM
        return jnp.concatenate(
            [g_rest[:, i * PAIR : (i + 1) * PAIR], g_rest[:, side : side + HEAD_DIM]], axis=1
        )

    return (
        hidden_out,
        grad_in,
        small[0],
        small[1],
        jnp.stack([both_parts(0), both_parts(1), both_parts(2)]),
        g_bqv,
        g_out.T,
        small[6],
        small[4],
        small[5],
        jnp.concatenate([g_one[:, :cut], g_two[:, :rest_cut]], axis=1),
        small[8:].reshape(-1),
        jnp.concatenate([g_one[:, cut:], g_two[:, rest_cut : 2 * rest_cut]], axis=1).T,
        small[7],
    )


def solution(mesh):
    placed = (
        P(BOTH, None),
        P(BOTH, None),
        P("dp"),
        P("dp", None),
        P(),
        P(),
        P(None, "dp", "tensor"),
        P(),
        P("tensor", "dp"),
        P(),
        P(),
        P(),
        P("dp", "tensor"),
        P(),
        P("tensor", "dp"),
        P(),
    )
    return jax.shard_map(
        functools.partial(body, mesh.shape["dp"], mesh.shape["tensor"]),
        mesh=mesh,
        in_specs=placed,
        out_specs=(
            P(BOTH, None),
            P(BOTH, None),
            P(),
            P(),
            P(None, "dp", "tensor"),
            P(),
            P("tensor", "dp"),
            P(),
            P(),
            P(),
            P("dp", "tensor"),
            P(),
            P("tensor", "dp"),
            P(),
        ),
        check_vma=False,
    )
```

```python
import functools

import jax
import jax.numpy as jnp
from jax import lax
from jax.experimental import pallas as pl
from jax.experimental.pallas import tpu as pltpu
from jax.sharding import PartitionSpec as P

HEAD_DIM = 64
LEN = 1024
PAIR = 2 * HEAD_DIM
TILE = 256
NEG_BIG = -1e30
EPSILON = 1e-05
VMEM_BYTES = 66_900_000
BF = jnp.bfloat16
F32 = jnp.float32
BOTH = ("dp", "tensor")
ANY_SPEC = pl.BlockSpec(memory_space=pl.ANY)


def dot_nn(a, b):
    return lax.dot_general(a, b, (((1,), (0,)), ((), ())), preferred_element_type=F32)


def dot_nt(a, b):
    return lax.dot_general(a, b, (((1,), (1,)), ((), ())), preferred_element_type=F32)


def dot_tn(a, b):
    return lax.dot_general(a, b, (((0,), (0,)), ((), ())), preferred_element_type=F32)


def norm_parts(rows_in):
    center = rows_in - jnp.mean(rows_in, axis=-1, keepdims=True)
    spread = jnp.mean(center * center, axis=-1, keepdims=True)
    scale = lax.rsqrt(spread + EPSILON)
    return center * scale, scale


def norm_back(gy, normed, scale):
    mean_gy = jnp.mean(gy, axis=-1, keepdims=True)
    mean_gyn = jnp.mean(gy * normed, axis=-1, keepdims=True)
    return (gy - mean_gy - normed * mean_gyn) * scale


def col_sum(values):
    return jnp.sum(values, axis=0, keepdims=True)


def once(shape, index):
    return pl.BlockSpec(shape, index, pipeline_mode=pl.Buffered(1))


def params(side_effects=False):
    return pltpu.CompilerParams(
        dimension_semantics=("arbitrary",),
        vmem_limit_bytes=VMEM_BYTES,
        has_side_effects=side_effects,
    )


def cost(flops, moved, exps=0):
    return pl.CostEstimate(flops=int(flops), bytes_accessed=int(moved), transcendentals=int(exps))


def place_of(index):
    return (index >> 3) & 3, (index >> 2) & 1, (index >> 1) & 1, index & 1


def index_of(z, x, y, core):
    return (z << 3) | (x << 2) | (y << 1) | core


def exchange(array, flip):
    pairs = [(i, index_of(*flip(*place_of(i)))) for i in range(32)]
    return lax.ppermute(array, BOTH, pairs)


def flip_first(z, x, y, core):
    return (z, x, y ^ 1, core) if core else (z, x ^ 1, y, core)


def flip_second(z, x, y, core):
    return (z, x ^ 1, y, core) if core else (z, x, y ^ 1, core)


def flip_core(z, x, y, core):
    return z, x, y, core ^ 1


def flip_near(z, x, y, core):
    return z ^ 1, x, y, core


def flip_far(z, x, y, core):
    return z ^ 2, x, y, core


def sums_kernel(plan, *refs):
    count_in = sum(len(offsets) for offsets, _ in plan)
    outs = refs[count_in : count_in + len(plan)]
    scratch = refs[count_in + len(plan) :]
    position = 0
    for i, (offsets, count) in enumerate(plan):
        terms, _, sems, _ = scratch[4 * i : 4 * i + 4]
        for slot in range(count):
            for k, offset in enumerate(offsets):
                pltpu.make_async_copy(
                    refs[position + k].at[offset + slot], terms.at[slot, k], sems.at[slot]
                ).start()
        position += len(offsets)
    for i, (offsets, count) in enumerate(plan):
        terms, result, sems, out_sem = scratch[4 * i : 4 * i + 4]

        def body(slot, _, i=i, size=len(offsets)):
            terms, result, sems, out_sem = scratch[4 * i : 4 * i + 4]
            wait_all(terms.at[slot], sems.at[slot])
            total = terms[slot, 0].astype(F32)
            for k in range(1, size):
                total = total + terms[slot, k].astype(F32)
            result[slot] = total.astype(BF)
            pltpu.make_async_copy(result.at[slot], outs[i].at[slot], out_sem).start()
            return 0

        lax.fori_loop(0, count, body, 0)
    for i in range(len(plan)):
        wait_all(scratch[4 * i + 1], scratch[4 * i + 3])


def sums(*requests):
    plan, arrays, shapes, scratch = [], [], [], []
    for terms, count in requests:
        block = terms[0][0].shape[1:]
        plan.append((tuple(offset for _, offset in terms), count))
        arrays += [array for array, _ in terms]
        shapes.append(jax.ShapeDtypeStruct((count, *block), BF))
        scratch += [
            pltpu.VMEM((count, len(terms), *block), BF),
            pltpu.VMEM((count, *block), BF),
            pltpu.SemaphoreType.DMA((count,)),
            pltpu.SemaphoreType.DMA(()),
        ]
    return pl.pallas_call(
        functools.partial(sums_kernel, plan),
        in_specs=[ANY_SPEC] * len(arrays),
        out_specs=[ANY_SPEC] * len(shapes),
        out_shape=shapes,
        scratch_shapes=scratch,
        compiler_params=pltpu.CompilerParams(vmem_limit_bytes=VMEM_BYTES),
        cost_estimate=cost(1e6, 8e6),
        name="sums",
    )(*arrays)


def plain_sums(*requests):
    results = []
    for terms, count in requests:
        total = None
        for array, offset in terms:
            part = array[offset : offset + count].astype(F32)
            total = part if total is None else total + part
        results.append(total.astype(BF))
    return results


class Scatter:
    def __init__(self, kept, sent):
        self.terms, self.sent = [kept], sent
        self.flips = [flip_core, flip_second, flip_first, flip_far, flip_near]

    def step(self):
        return exchange(self.sent, self.flips.pop(0))

    def want(self, came):
        self.terms = [*self.terms, came]
        count = came.shape[0] // 2
        return [(array, count) for array in self.terms], count

    def last(self, came):
        total = came[0].astype(F32)
        for array in self.terms:
            total = total + array[0].astype(F32)
        return total


def after(value, *others):
    return lax.optimization_barrier((value, *others))


def ring_place(z):
    z = z & 3
    return z ^ (z >> 1)


def flip_ring(z, x, y, core):
    return ring_place(ring_place(z) + 1), x, y, core


def start_blocks(place_ref, sources, cols, raw, to, sems, order="xor"):
    if len(sources) == 1:
        nd, blocks, block, _ = sources[0].shape
        for d in range(nd):
            for t in range(blocks):
                pltpu.make_async_copy(
                    sources[0].at[d, t, :, cols],
                    raw.at[t, d * block : (d + 1) * block, to],
                    sems.at[t],
                ).start()
        return
    z, x, y, core = (place_ref[i] for i in range(4))
    block = sources[0].shape[1]
    for i, source in enumerate(sources):
        for slot in range(4):
            to_core = core ^ (i >> 2)
            pair, step = (slot, i & 3) if order == "last" else (i & 3, slot)
            second, first = pair >> 1, pair & 1
            to_x = x ^ (first + to_core * (second - first))
            to_y = y ^ (second + to_core * (first - second))
            to_z = z ^ step if order == "xor" else ring_place(ring_place(z) - step)
            to_t = to_y * 2 + to_core
            low = pl.multiple_of((to_z * 2 + to_x) * block, block)
            pltpu.make_async_copy(
                source.at[slot, :, cols], raw.at[to_t, pl.ds(low, block), to], sems.at[to_t]
            ).start()


def wait_all(ref, sem):
    pltpu.make_async_copy(ref, ref, sem).wait()


def send_block(place_ref, staged, outs, sem, d, t, ring):
    z, x, y, core = (place_ref[i] for i in range(4))
    far, near_core = d >> 1, t & 1
    x_off, y_off = x ^ (d & 1), y ^ (t >> 1)
    first, second = (y_off, x_off) if near_core else (x_off, y_off)
    along = (ring_place(far) - ring_place(z)) & 3 if ring else z ^ far
    slot = second * 8 + first * 4 + along
    for side in range(2):

        @pl.when((core ^ near_core) == side)
        def _(side=side):
            pltpu.make_async_copy(staged, outs[side].at[slot], sem).start()


def send_rows(place_ref, stage, outs, sem, t, cols, part=None, ring=False):
    if len(outs) == 1:
        half = stage.shape[0] // 2
        rows = slice(None) if part is None else slice(part * half, (part + 1) * half)
        pltpu.make_async_copy(stage.at[rows, :], outs[0].at[t, rows, cols], sem).start()
        return
    block = outs[0].shape[1]
    for d in range(8) if part is None else range(4 * part, 4 * part + 4):
        staged = stage.at[d * block : (d + 1) * block, :]
        send_block(place_ref, staged, [out.at[:, :, cols] for out in outs], sem, d, t, ring)


def qkv_kernel(count, place_ref, x_ref, gain_ref, bias_ref, bqv_ref, *refs):
    sources = refs[:count]
    q_ref, k_ref, v_ref, n_ref, w_out, raw, sems, w_ref, w_sem = refs[count:]
    blocks = raw.shape[0]
    normed, _ = norm_parts(x_ref[...].astype(F32))
    low = (normed * gain_ref[...] + bias_ref[...]).astype(BF)
    n_ref[...] = low

    @pl.when(pl.program_id(0) == 0)
    def _():
        cols = slice(0, raw.shape[2])
        start_blocks(place_ref, sources, cols, raw, cols, sems)
        for t in range(blocks):
            wait_all(raw.at[t], sems.at[t])

        def piece(t, c):
            return raw[t, :, c * PAIR : (c + 1) * PAIR]

        for t in range(blocks):
            for c in range(4):
                w_ref[c, :, t * PAIR : (t + 1) * PAIR] = piece(t, c)
        for u in range(blocks // 2):
            col = (blocks + u) * PAIR
            for half in range(2):
                left = piece(2 * u, 4 + half)
                right = piece(2 * u + 1, 4 + half)
                w_ref[2 * half, :, col : col + PAIR] = jnp.concatenate(
                    [left[:, :HEAD_DIM], right[:, :HEAD_DIM]], axis=1
                )
                w_ref[2 * half + 1, :, col : col + PAIR] = jnp.concatenate(
                    [left[:, HEAD_DIM:], right[:, HEAD_DIM:]], axis=1
                )
        pltpu.make_async_copy(w_ref, w_out, w_sem).start()

    q_low = (dot_nn(low, w_ref[0]) + bqv_ref[0:1, :]).astype(BF)
    q_ref[...] = q_low * BF(HEAD_DIM ** (-0.5))
    k_ref[...] = dot_nn(low, w_ref[1]).astype(BF)
    v_ref[...] = (dot_nn(low, w_ref[2]) + bqv_ref[1:2, :]).astype(BF)

    @pl.when(pl.program_id(0) == pl.num_programs(0) - 1)
    def _():
        wait_all(w_ref, w_sem)


def project(place, x, gain, bias, bqv, sources, blocks):
    rows, width = x.shape
    row_spec = pl.BlockSpec((TILE, width), lambda i, *_: (i, 0))
    return pl.pallas_call(
        functools.partial(qkv_kernel, len(sources)),
        grid_spec=pltpu.PrefetchScalarGridSpec(
            num_scalar_prefetch=1,
            grid=(rows // TILE,),
            in_specs=[
                row_spec,
                once((1, width), lambda i, *_: (0, 0)),
                once((1, width), lambda i, *_: (0, 0)),
                once((2, width), lambda i, *_: (0, 0)),
            ]
            + [ANY_SPEC] * len(sources),
            out_specs=[row_spec] * 4 + [ANY_SPEC],
            scratch_shapes=[
                pltpu.VMEM((blocks, width, sources[0].shape[-1]), BF),
                pltpu.SemaphoreType.DMA((blocks,)),
                pltpu.VMEM((4, width, width), BF),
                pltpu.SemaphoreType.DMA(()),
            ],
        ),
        out_shape=[jax.ShapeDtypeStruct((rows, width), BF)] * 4
        + [jax.ShapeDtypeStruct((4, width, width), BF)],
        compiler_params=params(),
        cost_estimate=cost(6 * rows * width * width, 16 * rows * width),
        name="project",
    )(place, x, gain, bias, bqv, *sources)


def half_masks():
    lane = lax.broadcasted_iota(jnp.int32, (1, PAIR), 1)
    first = (lane < HEAD_DIM).astype(F32)
    return first.astype(BF), (1.0 - first).astype(BF)


def attend_kernel(len_ref, q_ref, k_ref, v_ref, o_ref, lse_ref):
    rows = q_ref.shape[0]
    length = len_ref[0]
    masks = half_masks()
    lane = lax.broadcasted_iota(jnp.int32, (TILE, PAIR), 1)
    k_pos = lax.broadcasted_iota(jnp.int32, (1, rows), 1)
    bias = jnp.where(k_pos < length, 0.0, NEG_BIG)
    tri = lax.broadcasted_iota(jnp.int32, (TILE, TILE), 0) >= lax.broadcasted_iota(
        jnp.int32, (TILE, TILE), 1
    )
    for n in range(0, rows, TILE):
        q_block = q_ref[n : n + TILE, :]
        scores = []
        for mask in masks:
            q_one = q_block * mask
            s_diag = dot_nt(q_one, k_ref[n : n + TILE, :]) + bias[:, n : n + TILE]
            s_diag = jnp.where(tri, s_diag, NEG_BIG)
            s_rest = dot_nt(q_one, k_ref[:n, :]) + bias[:, :n] if n else None
            scores.append((s_diag, s_rest))
        outs = []
        peaks = []
        totals = []
        for s_diag, s_rest in scores:
            peak = jnp.max(s_diag, axis=1, keepdims=True)
            if n:
                peak = jnp.maximum(peak, jnp.max(s_rest, axis=1, keepdims=True))
            e_diag = jnp.exp(s_diag - peak)
            total = jnp.sum(e_diag, axis=1, keepdims=True)
            acc = dot_nn(e_diag.astype(BF), v_ref[n : n + TILE, :])
            if n:
                e_rest = jnp.exp(s_rest - peak)
                total = total + jnp.sum(e_rest, axis=1, keepdims=True)
                acc = acc + dot_nn(e_rest.astype(BF), v_ref[:n, :])
            outs.append(acc)
            peaks.append(peak)
            totals.append(total)
        first = lane < HEAD_DIM
        both = jnp.where(first, outs[0], outs[1])
        o_ref[n : n + TILE, :] = (both / jnp.where(first, totals[0], totals[1])).astype(BF)
        packed = jnp.where(lane < 8, peaks[0], totals[0])
        packed = jnp.where(lane % 8 == 1, jnp.where(lane < 8, peaks[1], totals[1]), packed)
        flipped = jnp.transpose(packed)
        lse_ref[0, :, n : n + TILE] = flipped[:8, :] + jnp.log(flipped[8:16, :])


def attend(lengths, q, k, v):
    rows, width = q.shape
    pairs = width // PAIR
    pair_spec = pl.BlockSpec((rows, PAIR), lambda i, *_: (0, i))
    return pl.pallas_call(
        attend_kernel,
        grid_spec=pltpu.PrefetchScalarGridSpec(
            num_scalar_prefetch=1,
            grid=(pairs,),
            in_specs=[pair_spec] * 3,
            out_specs=[pair_spec, pl.BlockSpec((1, 8, rows), lambda i, *_: (i, 0, 0))],
        ),
        out_shape=[
            jax.ShapeDtypeStruct((rows, width), BF),
            jax.ShapeDtypeStruct((pairs, 8, rows), F32),
        ],
        compiler_params=params(),
        cost_estimate=cost(16e9 * width / 768, 8 * rows * width),
        name="attend",
    )(lengths, q, k, v)


def attend_back_kernel(
    first, n_out, more, len_ref, place_ref, q_ref, k_ref, v_ref, o_ref, do_ref, lse_ref, n_ref,
    out_ref, *refs
):
    refs = refs[n_out:] if more else refs
    dq_ref, dk_ref, dv_ref = refs[:3]
    outs = refs[3 : 3 + n_out]
    dq_acc, side_s, n_s, stage, n_sem, sem = refs[3 + n_out :]
    rows = q_ref.shape[0]
    width = n_ref.shape[1]
    step = pl.program_id(0)
    length = len_ref[0]
    masks = half_masks()
    wide = stage.shape[2]
    narrow = wide != 3 * PAIR

    @pl.when(step == 0)
    def _():
        pltpu.make_async_copy(n_ref, n_s, n_sem).start()

    prod = jnp.transpose(do_ref[...].astype(F32) * o_ref[...].astype(F32))
    tri = lax.broadcasted_iota(jnp.int32, (TILE, TILE), 0) <= lax.broadcasted_iota(
        jnp.int32, (TILE, TILE), 1
    )
    k_pos = lax.broadcasted_iota(jnp.int32, (TILE, 1), 0)
    dq_acc[...] = jnp.zeros_like(dq_acc)
    heads = []
    for h, mask in enumerate(masks):
        heads.append(
            (
                mask,
                q_ref[...] * mask,
                do_ref[...] * mask,
                lse_ref[0, h : h + 1, :],
                jnp.sum(prod[h * HEAD_DIM : (h + 1) * HEAD_DIM, :], axis=0, keepdims=True),
            )
        )
    for n in range(0, rows, TILE):
        k_block = k_ref[n : n + TILE, :]
        v_block = v_ref[n : n + TILE, :]
        bias = jnp.where(k_pos + n < length, 0.0, NEG_BIG)
        dk = jnp.zeros((TILE, PAIR), F32)
        dv = jnp.zeros((TILE, PAIR), F32)
        work = []
        for mask, q_one, do_one, lse, delta in heads:
            for low, high in ((n, n + TILE), (n + TILE, rows)):
                if low == high:
                    continue
                s = dot_nt(k_block, q_one[low:high]) + bias
                dp = dot_nt(v_block, do_one[low:high])
                work.append((mask, q_one, do_one, lse, delta, low, high, s, dp))
        for mask, q_one, do_one, lse, delta, low, high, s, dp in work:
            if low == n:
                s = jnp.where(tri, s, NEG_BIG)
            p = jnp.exp(s - lse[:, low:high])
            ds = (p * (dp - delta[:, low:high])).astype(BF)
            dv = dv + dot_nn(p.astype(BF), do_one[low:high])
            dk = dk + dot_nn(ds, q_one[low:high])
            dq_acc[low:high, :] += dot_tn(ds, k_block * mask)
        dk_ref[n : n + TILE, :] = dk.astype(BF)
        dv_ref[n : n + TILE, :] = dv.astype(BF)
    dq_ref[...] = (dq_acc[...] * (HEAD_DIM ** (-0.5))).astype(BF)

    grads = [dq_ref[...], dk_ref[...], dv_ref[...]]
    if narrow:
        blank = jnp.zeros((rows, HEAD_DIM), BF)
        sides = [
            jnp.concatenate([g[:, c : c + HEAD_DIM] for g in grads] + [blank], axis=1)
            for c in (0, HEAD_DIM)
        ]
    else:
        sides = [jnp.concatenate(grads, axis=1)]
    pairs = side_s.shape[1] // (wide * len(sides))
    for at in range(pairs):

        @pl.when(step == at)
        def _(at=at):
            for i, side in enumerate(sides):
                spot = at * len(sides) + i
                side_s[:, spot * wide : (spot + 1) * wide] = side

    @pl.when(step == pairs - 1)
    def _():
        pltpu.make_async_copy(n_ref, n_s, n_sem).wait()
        low_col = 3 * PAIR if narrow else 0
        columns = slice(low_col, low_col + wide)
        for part in range(2):
            cols = slice(part * width // 2, (part + 1) * width // 2)
            grad = dot_tn(n_s[:, cols], side_s[...]).astype(BF)
            for spot in range(stage.shape[0]):
                t = spot if narrow else first + spot
                begin = spot * wide
                if narrow:
                    stage[spot, cols, :PAIR] = grad[:, begin : begin + PAIR]
                    extra = out_ref[cols, spot * HEAD_DIM : (spot + 1) * HEAD_DIM]
                    stage[spot, cols, PAIR:] = jnp.concatenate(
                        [grad[:, begin + PAIR : begin + PAIR + HEAD_DIM], extra], axis=1
                    )
                else:
                    stage[spot, cols, :] = grad[:, begin : begin + wide]
                send_rows(place_ref, stage.at[spot], outs, sem, t, columns, part)
        wait_all(stage, sem)


def attend_back(
    place, lengths, first, pairs, wide, q, k, v, out, d_out, lse, normed, last_out, blocks,
    so_far, fast,
):
    rows, width = q.shape
    at_pair = pl.BlockSpec((rows, PAIR), lambda i, *_: (0, first + i))
    own_pair = pl.BlockSpec((rows, PAIR), lambda i, *_: (0, i))
    grads = grad_shapes(fast, blocks, width, 5 * PAIR)
    so_far = so_far or []
    sides = 1 if wide == 3 * PAIR else 2
    return pl.pallas_call(
        functools.partial(attend_back_kernel, first, len(grads), bool(so_far)),
        grid_spec=pltpu.PrefetchScalarGridSpec(
            num_scalar_prefetch=2,
            grid=(pairs,),
            in_specs=[at_pair] * 5
            + [
                pl.BlockSpec((1, 8, rows), lambda i, *_: (first + i, 0, 0)),
                ANY_SPEC,
                once(last_out.shape, lambda i, *_: (0, 0)),
            ]
            + [ANY_SPEC] * len(so_far),
            out_specs=[own_pair] * 3 + [ANY_SPEC] * len(grads),
            scratch_shapes=[
                pltpu.VMEM((rows, PAIR), F32),
                pltpu.VMEM((rows, pairs * sides * wide), BF),
                pltpu.VMEM((rows, width), BF),
                pltpu.VMEM((pairs * sides, width, wide), BF),
                pltpu.SemaphoreType.DMA(()),
                pltpu.SemaphoreType.DMA(()),
            ],
        ),
        out_shape=[jax.ShapeDtypeStruct((rows, pairs * PAIR), BF)] * 3 + grads,
        input_output_aliases={10 + i: 3 + i for i in range(len(so_far))},
        compiler_params=params(),
        cost_estimate=cost(5.5e9 * pairs, 5e6 * pairs),
        name="attend_back",
    )(lengths, place, q, k, v, out, d_out, lse, normed, last_out, *so_far)


def vec_rows(vec_ref):
    return lambda i: vec_ref[i : i + 1, :]


def tile_rows(i):
    return pl.ds(pl.multiple_of(i * TILE, TILE), TILE)


def grad_shapes(fast, blocks, width, wide):
    if fast:
        return [jax.ShapeDtypeStruct((16, width // 8, wide), BF)] * 2
    return [jax.ShapeDtypeStruct((blocks, width, wide), BF)]


def feed_kernel(
    counts, place_ref, att_ref, x_ref, cot_ref, wo_ref, vec_ref, bup_ref, *refs
):
    one, two = counts
    refs, sources = refs[one + two :], (refs[:one], refs[one : one + two])
    resid_out, act_ref, gbup_ref, dres_out, datt_out, sums_ref, last_out_ref = refs[:7]
    refs = refs[7:]
    n_out = (len(refs) - 13) // 2
    up_outs, down_outs = refs[:n_out], refs[n_out : 2 * n_out]
    raw, sems, n_two, d_pre_s, d_norm, low, stage, stage_down, sem = refs[2 * n_out : -4]
    resid_ref, dres_ref, datt_ref, out_sems = refs[-4:]
    rows, width = x_ref.shape
    step = pl.program_id(0)
    tiles = rows // TILE
    blocks = stage.shape[0]
    vec = vec_rows(vec_ref)
    half_width = width // 2
    cut = sources[0][0].shape[-1] // 2

    @pl.when(step == 0)
    def _():
        begin = 0
        sizes, orders = (cut, width - cut), ("ring", "last")
        for source, size, order in zip(sources, sizes, orders, strict=True):
            for to in (begin, width + begin):
                start_blocks(
                    place_ref,
                    source,
                    slice(0 if to < width else size, size if to < width else 2 * size),
                    raw,
                    slice(to, to + size),
                    sems,
                    order,
                )
            begin += size

        def body(i, _):
            r = tile_rows(i)
            res = x_ref[r, :].astype(F32) + dot_nt(att_ref[r, :], wo_ref[0]) + vec(0)
            resid_ref[r, :] = res
            normed, _ = norm_parts(res)
            n_two[r, :] = (normed * vec(1) + vec(2)).astype(BF)
            d_norm[r, :] = jnp.zeros((TILE, width), F32)
            return 0

        lax.fori_loop(0, tiles, body, 0, unroll=True)
        pltpu.make_async_copy(resid_ref, resid_out, out_sems.at[0]).start()

    wait_all(raw.at[step], sems.at[step])
    w_up = raw[step, :, :width]
    w_down = raw[step, :, width:]
    c_one = 0.7978845608028654
    c_two = 0.044715

    def body(i, total):
        r = tile_rows(i)
        u = dot_nn(n_two[r, :], w_up) + bup_ref[0]
        d_act = dot_nn(cot_ref[r, :], w_down)
        square = u * u
        t = jnp.tanh(c_one * u * (1.0 + c_two * square))
        half = 0.5 * (1.0 + t)
        act_ref[r, :] = (u * half).astype(BF)
        slope = half + 0.5 * u * (1.0 - t * t) * (c_one * (1.0 + 3.0 * c_two * square))
        d_pre = (d_act * slope).astype(BF)
        d_pre_s[r, :] = d_pre
        d_norm[r, :] += dot_nt(d_pre, w_up)
        return total + col_sum(d_pre.astype(F32))

    gbup_ref[0] = lax.fori_loop(0, tiles, body, jnp.zeros((1, width), F32), unroll=True)
    for c in (0, half_width):
        cols = slice(c, c + half_width)
        stage[step, cols, :width] = dot_tn(n_two[:, cols], d_pre_s[...]).astype(BF)
        stage_down[step, cols, :] = dot_tn(cot_ref[:, cols], act_ref[...]).astype(BF)
    first_cols = slice(0, width)
    for t in range(blocks):

        @pl.when(step == t)
        def _(t=t):
            send_rows(place_ref, stage.at[t, :, first_cols], up_outs, sem, t, first_cols)
            send_rows(place_ref, stage_down.at[t], down_outs, sem, t, first_cols)

    @pl.when(step == pl.num_programs(0) - 1)
    def _():
        def body(i, sums):
            r = tile_rows(i)
            normed, scale = norm_parts(resid_ref[r, :])
            d_n = d_norm[r, :]
            d_out = cot_ref[r, :].astype(F32)
            d_res = d_out + norm_back(d_n * vec(1), normed, scale)
            dres_ref[r, :] = d_res
            d_low = d_res.astype(BF)
            low[r, :] = d_low
            datt_ref[r, :] = dot_nn(d_low, wo_ref[0]).astype(BF)
            pltpu.make_async_copy(dres_ref.at[r, :], dres_out.at[r, :], out_sems.at[1]).start()
            pltpu.make_async_copy(datt_ref.at[r, :], datt_out.at[r, :], out_sems.at[2]).start()
            more = (col_sum(d_n * normed), col_sum(d_n), col_sum(d_res), col_sum(d_out))
            return tuple(a + b for a, b in zip(sums, more, strict=True))

        sums = lax.fori_loop(0, tiles, body, (jnp.zeros((1, width), F32),) * 4, unroll=True)
        sums_ref[...] = jnp.zeros_like(sums_ref)
        for i in range(4):
            sums_ref[i : i + 1, :] = sums[i]
        side = width
        for c in range(0, width, half_width):
            rows_c = slice(c, c + half_width)
            go = dot_tn(low[:, rows_c], att_ref[...]).astype(BF)
            last_out_ref[rows_c, :] = go[:, blocks * PAIR :]
            for t in range(blocks):
                stage[t, rows_c, side:] = go[:, t * PAIR : (t + 1) * PAIR]
        cols = slice(side, side + PAIR)
        for t in range(blocks):
            send_rows(place_ref, stage.at[t, :, cols], up_outs, sem, t, cols)
        wait_all(stage, sem)
        wait_all(stage_down, sem)
        for i, ref in enumerate((resid_ref, dres_ref, datt_ref)):
            wait_all(ref, out_sems.at[i])


def feed_forward(place, att, x, cot, w_all, vecs, b_up, sources_one, sources_two, fast):
    rows, width = x.shape
    blocks = b_up.shape[0]
    whole = once((rows, width), lambda t, *_: (0, 0))
    up_vec = pl.BlockSpec((1, 1, width), lambda t, *_: (t, 0, 0))
    grads = grad_shapes(fast, blocks, width, width + PAIR)
    grads += grad_shapes(fast, blocks, width, width)
    counts = (len(sources_one), len(sources_two))
    return pl.pallas_call(
        functools.partial(feed_kernel, counts),
        grid_spec=pltpu.PrefetchScalarGridSpec(
            num_scalar_prefetch=1,
            grid=(blocks,),
            in_specs=[
                whole,
                whole,
                whole,
                once((1, width, width), lambda t, *_: (3, 0, 0)),
                once((8, width), lambda t, *_: (0, 0)),
                up_vec,
            ]
            + [ANY_SPEC] * sum(counts),
            out_specs=[
                ANY_SPEC,
                pl.BlockSpec((rows, width), lambda t, *_: (0, t)),
                up_vec,
                ANY_SPEC,
                ANY_SPEC,
                once((8, width), lambda t, *_: (0, 0)),
                once((width, width - blocks * PAIR), lambda t, *_: (0, 0)),
            ]
            + [ANY_SPEC] * len(grads),
            scratch_shapes=[
                pltpu.VMEM((blocks, width, 2 * width), BF),
                pltpu.SemaphoreType.DMA((blocks,)),
                pltpu.VMEM((rows, width), BF),
                pltpu.VMEM((rows, width), BF),
                pltpu.VMEM((rows, width), F32),
                pltpu.VMEM((rows, width), BF),
                pltpu.VMEM((blocks, width, width + PAIR), BF),
                pltpu.VMEM((blocks, width, width), BF),
                pltpu.SemaphoreType.DMA(()),
                pltpu.VMEM((rows, width), F32),
                pltpu.VMEM((rows, width), F32),
                pltpu.VMEM((rows, width), BF),
                pltpu.SemaphoreType.DMA((3,)),
            ],
        ),
        out_shape=[
            jax.ShapeDtypeStruct((rows, width), F32),
            jax.ShapeDtypeStruct((rows, blocks * width), BF),
            jax.ShapeDtypeStruct((blocks, 1, width), F32),
            jax.ShapeDtypeStruct((rows, width), F32),
            jax.ShapeDtypeStruct((rows, width), BF),
            jax.ShapeDtypeStruct((8, width), F32),
            jax.ShapeDtypeStruct((width, width - blocks * PAIR), BF),
        ]
        + grads,
        compiler_params=params(),
        cost_estimate=cost(40e9, 40e6),
        name="feed_forward",
    )(place, att, x, cot, w_all, vecs, b_up, *sources_one, *sources_two)


def hidden_kernel(counts, place_ref, act_ref, resid_ref, vec_ref, *refs):
    one, two = counts
    refs, sources = refs[one + two :], (refs[:one], refs[one : one + two])
    out_ref, raw, sems = refs
    blocks, _, width = raw.shape
    cut = sources[0][0].shape[-1] // 2

    @pl.when(pl.program_id(0) == 0)
    def _():
        begin = 0
        sizes, orders = (cut, width - cut), ("ring", "last")
        for source, size, order in zip(sources, sizes, orders, strict=True):
            to = slice(begin, begin + size)
            start_blocks(place_ref, source, slice(size, 2 * size), raw, to, sems, order)
            begin += size
        for t in range(blocks):
            wait_all(raw.at[t], sems.at[t])

    acc = resid_ref[...] + vec_ref[3:4, :]
    for t in range(blocks):
        acc = acc + dot_nt(act_ref[:, t * width : (t + 1) * width], raw[t])
    out_ref[...] = acc.astype(BF)


def hidden_rows(place, act, resid, vecs, sources_one, sources_two):
    rows, width = resid.shape
    blocks = act.shape[1] // width
    row_spec = pl.BlockSpec((TILE, width), lambda i, *_: (i, 0))
    counts = (len(sources_one), len(sources_two))
    return pl.pallas_call(
        functools.partial(hidden_kernel, counts),
        grid_spec=pltpu.PrefetchScalarGridSpec(
            num_scalar_prefetch=1,
            grid=(rows // TILE,),
            in_specs=[
                pl.BlockSpec((TILE, blocks * width), lambda i, *_: (i, 0)),
                row_spec,
                once((8, width), lambda i, *_: (0, 0)),
            ]
            + [ANY_SPEC] * sum(counts),
            out_specs=row_spec,
            scratch_shapes=[
                pltpu.VMEM((blocks, width, width), BF),
                pltpu.SemaphoreType.DMA((blocks,)),
            ],
        ),
        out_shape=jax.ShapeDtypeStruct((rows, width), BF),
        compiler_params=params(),
        cost_estimate=cost(5e9, 12e6),
        name="hidden_rows",
    )(place, act, resid, vecs, *sources_one, *sources_two)


def input_kernel(*refs):
    parts = refs[:9]
    w_ref, x_ref, dres_ref, gain_ref, gin_ref, sums_ref = refs[9:]

    @pl.when(pl.program_id(0) == 0)
    def _():
        sums_ref[...] = jnp.zeros_like(sums_ref)

    dq, dk, dv = (jnp.concatenate([part[...] for part in parts[i::3]], axis=1) for i in range(3))
    d_norm = dot_nt(dq, w_ref[0]) + dot_nt(dk, w_ref[1]) + dot_nt(dv, w_ref[2])
    normed, scale = norm_parts(x_ref[...].astype(F32))
    gin_ref[...] = dres_ref[...] + norm_back(d_norm * gain_ref[...], normed, scale)
    more = (
        col_sum(d_norm * normed),
        col_sum(d_norm),
        col_sum(dq.astype(F32)),
        col_sum(dv.astype(F32)),
    )
    for i, value in enumerate(more):
        sums_ref[i : i + 1, :] += value


def input_grad(parts, w_all, x, d_resid, gain):
    rows, width = x.shape
    row_spec = pl.BlockSpec((TILE, width), lambda i: (i, 0))
    return pl.pallas_call(
        input_kernel,
        grid=(rows // TILE,),
        in_specs=[pl.BlockSpec((TILE, part.shape[1]), lambda i: (i, 0)) for part in parts]
        + [
            once((3, width, width), lambda i: (0, 0, 0)),
            row_spec,
            row_spec,
            once((1, width), lambda i: (0, 0)),
        ],
        out_specs=[row_spec, pl.BlockSpec((8, width), lambda i: (0, 0))],
        out_shape=[
            jax.ShapeDtypeStruct((rows, width), F32),
            jax.ShapeDtypeStruct((8, width), F32),
        ],
        compiler_params=params(),
        cost_estimate=cost(6 * rows * width * width, 16 * rows * width),
        name="input_grad",
    )(*parts, w_all, x, d_resid, gain)


def body(
    n_dp,
    n_tensor,
    hidden_in,
    cotangent,
    lengths,
    latent,
    ln1_gain,
    ln1_bias,
    w_qkv,
    b_qv,
    w_out,
    b_out,
    ln2_gain,
    ln2_bias,
    w_up,
    b_up,
    w_down,
    b_down,
):
    rows, width = hidden_in.shape
    t_index = lax.axis_index("tensor")
    block = w_up.shape[0]
    heads = w_qkv.shape[2] // HEAD_DIM

    out_t = w_out.T
    packed = jnp.concatenate(
        [w_qkv[0, :, :PAIR], w_qkv[1, :, :PAIR], w_qkv[2, :, :PAIR], out_t[:, :PAIR]]
        + [w_qkv[0, :, PAIR:], w_qkv[1, :, PAIR:], w_qkv[2, :, PAIR:], out_t[:, PAIR:]],
        axis=1,
    ).astype(BF)
    packed, up_part, down_part = after(packed, w_up, w_down)
    down_t = down_part.T
    cut = w_up.shape[1] * 2 // 3
    packed_one = jnp.concatenate([up_part[:, :cut], down_t[:, :cut]], axis=1).astype(BF)
    packed_two = jnp.concatenate([up_part[:, cut:], down_t[:, cut:]], axis=1).astype(BF)
    own_length = lax.dynamic_slice_in_dim(lengths, t_index, 1, 0)
    own_latent = lax.dynamic_slice_in_dim(latent, t_index, 1, 0)
    positions = lax.broadcasted_iota(jnp.int32, (1, rows), 1)
    keep = ((positions < own_length) & (own_latent == 0)).astype(BF).reshape(rows, 1)
    cot = cotangent * keep

    fast = n_dp == 8 and n_tensor == 4
    d_index = lax.axis_index("dp")
    place = jnp.stack([d_index >> 1, d_index & 1, t_index >> 1, t_index & 1]).astype(jnp.int32)

    def gather(piece):
        wide = piece.shape[1]
        full = lax.all_gather(piece, BOTH, axis=0, tiled=False)
        full = full.reshape(n_dp, n_tensor, block, wide)
        if fast:
            return full
        return full.transpose(1, 0, 2, 3).reshape(1, n_tensor, width, wide)

    project_place = place
    def to_inner(b):
        split = b.reshape(b.shape[0], n_tensor, heads, HEAD_DIM)
        return jnp.concatenate(
            [split[:, :, :2].reshape(b.shape[0], -1), split[:, :, 2:].reshape(b.shape[0], -1)],
            axis=1,
        )

    zero = jnp.zeros_like(b_out)
    early = [
        cot,
        place,
        own_length,
        to_inner(b_qv),
        ln1_gain[None],
        ln1_bias[None],
        jnp.stack([b_out, ln2_gain, ln2_bias, b_down, zero, zero, zero, zero]),
        b_up.reshape(n_tensor, 1, width),
    ]
    if fast:
        def grow(array, came):
            return jnp.concatenate([array, came])

        att, one, two = packed[None], packed_one[None], packed_two[None]
        att_came, two_came, one, *early = after(
            exchange(att, flip_near), exchange(two, flip_first), one, *early
        )
        att, two = grow(att, att_came), grow(two, two_came)
        att_came, two_came, one_one = after(
            exchange(att, flip_far), exchange(two, flip_second), exchange(one, flip_ring)
        )
        att, two = grow(att, att_came), grow(two, two_came)
        att_first, att_second, one_two, two_one = after(
            exchange(att, flip_first),
            exchange(att, flip_second),
            exchange(one_one, flip_ring),
            exchange(two, flip_ring),
        )
        halves = [att, att_first, att_second]
        att_both, one_last, *cores = after(
            exchange(att_first, flip_second),
            exchange(one_two, flip_ring),
            *(exchange(half, flip_core) for half in halves),
        )
        sources = [*halves, att_both, *cores, exchange(att_both, flip_core)]
        one = jnp.concatenate([one, one_one, one_two, one_last])
        one_first, two_two = exchange(one, flip_first), exchange(two_one, flip_ring)
    else:
        sources = [gather(packed)]
        sources_one, sources_two = [gather(packed_one)], [gather(packed_two)]

    def from_inner(b):
        cut = n_tensor * PAIR
        first = b[:, :cut].reshape(b.shape[0], n_tensor, 2, HEAD_DIM)
        rest = b[:, cut:].reshape(b.shape[0], n_tensor, heads - 2, HEAD_DIM)
        return jnp.concatenate([first, rest], axis=2).reshape(b.shape[0], width)

    cot, place, own_length, inner_bqv, gain, bias, vecs, up_bias = early
    q, k, v, normed_one, w_all = project(
        place, hidden_in, gain, bias, inner_bqv, sources, n_tensor
    )
    if fast:
        one_first, two_two, q = after(one_first, two_two, q)
        halves = [one, one_first, two, two_one, two_two]
        cores = [exchange(half, flip_core) for half in halves]
        came = [exchange(half, flip_second) for half in halves[:2]]
        came.append(exchange(two_two, flip_ring))
    attended, lse = attend(own_length, q, k, v)
    if fast:
        attended, *moved = after(attended, *came, *cores)
        came, cores = moved[:3], moved[3:]
        cores += [exchange(half, flip_core) for half in came]
        sources_one = [*halves[:2], *came[:2], *cores[:2], *cores[5:7]]
        sources_two = [*halves[2:], came[2], *cores[2:5], cores[7]]
    resid, act, g_b_up, d_resid, d_attended, sums_two, last_out, *g_mlp = feed_forward(
        place, attended, hidden_in, cot, w_all, vecs, up_bias, sources_one, sources_two, fast
    )

    half = len(g_mlp) // 2

    def back(length, first, pairs, wide, so_far):
        return list(
            attend_back(
                place, length, first, pairs, wide, q, k, v, attended, d_attended, lse,
                normed_one, last_out, n_tensor, so_far, fast,
            )
        )

    def vectors(sums_one):
        return jnp.concatenate([sums_one[:4], sums_two[:4], g_b_up.reshape(n_tensor, width)])

    if fast:
        up, down = Scatter(*g_mlp[:half]), Scatter(*g_mlp[half:])
        came_up, came_down = up.step(), down.step()
        back_one = back(own_length, 0, 1, 3 * PAIR, None)
        came_up, came_down, length, *back_one = after(came_up, came_down, own_length, *back_one)
        (up.sent,) = sums(up.want(came_up))
        up.sent, came_down = after(up.sent, came_down)
        came_up = up.step()
        (down.sent,) = sums(down.want(came_down))
        came_down = down.step()
        back_two = back(length, 1, 3, 3 * PAIR, back_one[3:])
        came_up, length, *back_two = after(came_up, own_length, *back_two)
        (up.sent,) = sums(up.want(came_up))
        came_up = up.step()
        back_three = back(length, 4, 2, 2 * PAIR, back_two[3:])
        came_up, came_down, gain, *back_three = after(came_up, came_down, gain, *back_three)
        rest = Scatter(*back_three[3:])
        came_rest = rest.step()
        up.sent, down.sent = sums(up.want(came_up), down.want(came_down))
        came_rest, up.sent, down.sent = after(came_rest, up.sent, down.sent)
        came_up, came_down = up.step(), down.step()
        (rest.sent,) = sums(rest.want(came_rest))
        came_rest = rest.step()
        parts = [*back_one[:3], *back_two[:3], *back_three[:3]]
        grad_in, sums_one = input_grad(parts, w_all, hidden_in, d_resid, gain)
        came_rest, came_up, came_down, sums_one, grad_in = after(
            came_rest, came_up, came_down, sums_one, grad_in
        )
        rest.sent, up.sent, down.sent = sums(
            rest.want(came_rest), up.want(came_up), down.want(came_down)
        )
        came_rest, came_up, came_down = rest.step(), up.step(), down.step()
        small = vectors(sums_one)
        small = small + exchange(small, flip_core)
        came_small = exchange(small, flip_second)
        small = small + came_small
        came_small = exchange(small, flip_first)
        came_rest, came_small, last_place = after(came_rest, came_small, place)
        (rest.sent,) = plain_sums(rest.want(came_rest))
        small = small + came_small
        came_rest, came_small = rest.step(), exchange(small, flip_far)
        hidden_out = hidden_rows(last_place, act, resid, vecs, sources_one, sources_two)
        came_rest, came_small, came_up, came_down, hidden_out = after(
            came_rest, came_small, came_up, came_down, hidden_out
        )
        rest.sent, down.sent = plain_sums(rest.want(came_rest), down.want(came_down))
        small = small + came_small
        rest.sent, down.sent, came_up, small = after(rest.sent, down.sent, came_up, small)
        came_rest, came_down, came_small = rest.step(), down.step(), exchange(small, flip_near)
        g_up = up.last(came_up)
        small = small + came_small
        g_rest, g_down = rest.last(came_rest), down.last(came_down)
    else:
        back_one = back(own_length, 0, 1, 3 * PAIR, None)
        back_two = back(own_length, 1, 3, 3 * PAIR, back_one[3:])
        back_three = back(own_length, 4, 2, 2 * PAIR, back_two[3:])
        parts = [*back_one[:3], *back_two[:3], *back_three[:3]]
        grad_in, sums_one = input_grad(parts, w_all, hidden_in, d_resid, gain)
        hidden_out = hidden_rows(place, act, resid, vecs, sources_one, sources_two)
        small = lax.psum(vectors(sums_one), BOTH)

        def scatter_all(grads):
            wide = grads.shape[-1]
            grads = grads.reshape(n_tensor, n_dp, block, wide).transpose(1, 0, 2, 3)
            flat = grads.reshape(n_dp * n_tensor * block, wide)
            total = lax.psum_scatter(flat, BOTH, scatter_dimension=0, tiled=True)
            return total.astype(F32)

        g_up, g_down, g_rest = (scatter_all(g) for g in (*g_mlp, back_three[3]))
    out_col = 3 * PAIR + 3 * HEAD_DIM
    g_out = jnp.concatenate(
        [g_up[:, width:], g_rest[:, out_col : out_col + HEAD_DIM]], axis=1
    ).T
    g_bqv = from_inner(small[2:4])

    def both_parts(i):
        side = 3 * PAIR + i * HEAD_DIM
        return jnp.concatenate(
            [g_rest[:, i * PAIR : (i + 1) * PAIR], g_rest[:, side : side + HEAD_DIM]], axis=1
        )

    return (
        hidden_out,
        grad_in,
        small[0],
        small[1],
        jnp.stack([both_parts(0), both_parts(1), both_parts(2)]),
        g_bqv,
        g_out,
        small[6],
        small[4],
        small[5],
        g_up[:, :width],
        small[8:].reshape(-1),
        g_down.T,
        small[7],
    )


def solution(mesh):
    placed = (
        P(BOTH, None),
        P(BOTH, None),
        P("dp"),
        P("dp", None),
        P(),
        P(),
        P(None, "dp", "tensor"),
        P(),
        P("tensor", "dp"),
        P(),
        P(),
        P(),
        P("dp", "tensor"),
        P(),
        P("tensor", "dp"),
        P(),
    )
    return jax.shard_map(
        functools.partial(body, mesh.shape["dp"], mesh.shape["tensor"]),
        mesh=mesh,
        in_specs=placed,
        out_specs=(
            P(BOTH, None),
            P(BOTH, None),
            P(),
            P(),
            P(None, "dp", "tensor"),
            P(),
            P("tensor", "dp"),
            P(),
            P(),
            P(),
            P("dp", "tensor"),
            P(),
            P("tensor", "dp"),
            P(),
        ),
        check_vma=False,
    )
```

```python
import functools

import jax
import jax.numpy as jnp
from jax import lax
from jax.experimental import pallas as pl
from jax.experimental.pallas import tpu as pltpu
from jax.sharding import PartitionSpec as P

HEAD_DIM = 64
LEN = 1024
PAIR = 2 * HEAD_DIM
TILE = 256
NEG_BIG = -1e30
EPSILON = 1e-05
VMEM_BYTES = 66_900_000
BF = jnp.bfloat16
F32 = jnp.float32
BOTH = ("dp", "tensor")
ANY_SPEC = pl.BlockSpec(memory_space=pl.ANY)


def dot_nn(a, b):
    return lax.dot_general(a, b, (((1,), (0,)), ((), ())), preferred_element_type=F32)


def dot_nt(a, b):
    return lax.dot_general(a, b, (((1,), (1,)), ((), ())), preferred_element_type=F32)


def dot_tn(a, b):
    return lax.dot_general(a, b, (((0,), (0,)), ((), ())), preferred_element_type=F32)


def norm_parts(rows_in):
    center = rows_in - jnp.mean(rows_in, axis=-1, keepdims=True)
    spread = jnp.mean(center * center, axis=-1, keepdims=True)
    scale = lax.rsqrt(spread + EPSILON)
    return center * scale, scale


def norm_back(gy, normed, scale):
    mean_gy = jnp.mean(gy, axis=-1, keepdims=True)
    mean_gyn = jnp.mean(gy * normed, axis=-1, keepdims=True)
    return (gy - mean_gy - normed * mean_gyn) * scale


def col_sum(values):
    return jnp.sum(values, axis=0, keepdims=True)


def once(shape, index):
    return pl.BlockSpec(shape, index, pipeline_mode=pl.Buffered(1))


def params(side_effects=False):
    return pltpu.CompilerParams(
        dimension_semantics=("arbitrary",),
        vmem_limit_bytes=VMEM_BYTES,
        has_side_effects=side_effects,
    )


def cost(flops, moved, exps=0):
    return pl.CostEstimate(flops=int(flops), bytes_accessed=int(moved), transcendentals=int(exps))


def place_of(index):
    return (index >> 3) & 3, (index >> 2) & 1, (index >> 1) & 1, index & 1


def index_of(z, x, y, core):
    return (z << 3) | (x << 2) | (y << 1) | core


def exchange(array, flip):
    pairs = [(i, index_of(*flip(*place_of(i)))) for i in range(32)]
    return lax.ppermute(array, BOTH, pairs)


def flip_first(z, x, y, core):
    return (z, x, y ^ 1, core) if core else (z, x ^ 1, y, core)


def flip_second(z, x, y, core):
    return (z, x ^ 1, y, core) if core else (z, x, y ^ 1, core)


def flip_core(z, x, y, core):
    return z, x, y, core ^ 1


def flip_near(z, x, y, core):
    return z ^ 1, x, y, core


def flip_far(z, x, y, core):
    return z ^ 2, x, y, core


def sums_kernel(plan, *refs):
    count_in = sum(len(offsets) for offsets, _ in plan)
    outs = refs[count_in : count_in + len(plan)]
    scratch = refs[count_in + len(plan) :]
    position = 0
    for i, (offsets, count) in enumerate(plan):
        terms, _, sems, _ = scratch[4 * i : 4 * i + 4]
        for slot in range(count):
            for k, offset in enumerate(offsets):
                pltpu.make_async_copy(
                    refs[position + k].at[offset + slot], terms.at[slot, k], sems.at[slot]
                ).start()
        position += len(offsets)
    for i, (offsets, count) in enumerate(plan):
        terms, result, sems, out_sem = scratch[4 * i : 4 * i + 4]

        def body(slot, _, i=i, size=len(offsets)):
            terms, result, sems, out_sem = scratch[4 * i : 4 * i + 4]
            wait_all(terms.at[slot], sems.at[slot])
            total = terms[slot, 0].astype(F32)
            for k in range(1, size):
                total = total + terms[slot, k].astype(F32)
            result[slot] = total.astype(BF)
            pltpu.make_async_copy(result.at[slot], outs[i].at[slot], out_sem).start()
            return 0

        lax.fori_loop(0, count, body, 0)
    for i in range(len(plan)):
        wait_all(scratch[4 * i + 1], scratch[4 * i + 3])


def sums(*requests):
    plan, arrays, shapes, scratch = [], [], [], []
    for terms, count in requests:
        block = terms[0][0].shape[1:]
        plan.append((tuple(offset for _, offset in terms), count))
        arrays += [array for array, _ in terms]
        shapes.append(jax.ShapeDtypeStruct((count, *block), BF))
        scratch += [
            pltpu.VMEM((count, len(terms), *block), BF),
            pltpu.VMEM((count, *block), BF),
            pltpu.SemaphoreType.DMA((count,)),
            pltpu.SemaphoreType.DMA(()),
        ]
    return pl.pallas_call(
        functools.partial(sums_kernel, plan),
        in_specs=[ANY_SPEC] * len(arrays),
        out_specs=[ANY_SPEC] * len(shapes),
        out_shape=shapes,
        scratch_shapes=scratch,
        compiler_params=pltpu.CompilerParams(vmem_limit_bytes=VMEM_BYTES),
        cost_estimate=cost(1e6, 8e6),
        name="sums",
    )(*arrays)


def plain_sums(*requests):
    results = []
    for terms, count in requests:
        total = None
        for array, offset in terms:
            part = array[offset : offset + count].astype(F32)
            total = part if total is None else total + part
        results.append(total.astype(BF))
    return results


def split_columns(up, rest):
    width = up.shape[1] - PAIR
    side = 3 * PAIR
    out = jnp.concatenate([up[:, width:], rest[:, side + 3 * HEAD_DIM :]], axis=1)
    three = []
    for i in range(3):
        begin = side + i * HEAD_DIM
        parts = [rest[:, i * PAIR : (i + 1) * PAIR], rest[:, begin : begin + HEAD_DIM]]
        three.append(jnp.concatenate(parts, axis=1))
    return out, jnp.stack(three)


def last_kernel(counts, *refs):
    sources, rest_of = refs[: sum(counts)], refs[sum(counts) :]
    up_ref, out_ref, down_ref, qkv_ref = rest_of[:4]
    scratch, sems = rest_of[4:7], rest_of[7]
    position = 0
    for i, count in enumerate(counts):
        for k in range(count):
            pltpu.make_async_copy(
                sources[position + k].at[0], scratch[i].at[k], sems.at[i]
            ).start()
        position += count
    totals = []
    for i, count in enumerate(counts):
        wait_all(scratch[i], sems.at[i])
        total = scratch[i][0].astype(F32)
        for k in range(1, count):
            total = total + scratch[i][k].astype(F32)
        totals.append(total)
    up, down, rest = totals
    up_ref[...] = up[:, : up_ref.shape[1]]
    down_ref[...] = down
    out, qkv_ref[...] = split_columns(up, rest)
    out_ref[...] = jnp.transpose(out)


def last_sums(*chains):
    counts = [len(terms) for terms in chains]
    block = chains[0][0].shape[1]
    width, third = chains[1][0].shape[2], 3 * HEAD_DIM
    whole = pl.BlockSpec(memory_space=pltpu.VMEM)
    return pl.pallas_call(
        functools.partial(last_kernel, counts),
        in_specs=[ANY_SPEC] * sum(counts),
        out_specs=[whole] * 4,
        out_shape=[
            jax.ShapeDtypeStruct((block, width), F32),
            jax.ShapeDtypeStruct((third, block), F32),
            jax.ShapeDtypeStruct((block, width), F32),
            jax.ShapeDtypeStruct((3, block, third), F32),
        ],
        scratch_shapes=[
            pltpu.VMEM((len(terms), block, terms[0].shape[2]), BF) for terms in chains
        ]
        + [pltpu.SemaphoreType.DMA((3,))],
        compiler_params=pltpu.CompilerParams(vmem_limit_bytes=VMEM_BYTES),
        cost_estimate=cost(1e6, 4e6),
        name="last_sums",
    )(*(term for terms in chains for term in terms))


class Scatter:
    def __init__(self, kept, sent):
        self.terms, self.sent = [kept], sent
        self.flips = [flip_core, flip_second, flip_first, flip_far, flip_near]

    def step(self):
        return exchange(self.sent, self.flips.pop(0))

    def want(self, came):
        self.terms = [*self.terms, came]
        count = came.shape[0] // 2
        return [(array, count) for array in self.terms], count


def after(value, *others):
    return lax.optimization_barrier((value, *others))


def ring_place(z):
    z = z & 3
    return z ^ (z >> 1)


def flip_ring(z, x, y, core):
    return ring_place(ring_place(z) + 1), x, y, core


def start_blocks(place_ref, sources, cols, raw, to, sems, order="xor"):
    if len(sources) == 1:
        nd, blocks, block, _ = sources[0].shape
        for d in range(nd):
            for t in range(blocks):
                pltpu.make_async_copy(
                    sources[0].at[d, t, :, cols],
                    raw.at[t, d * block : (d + 1) * block, to],
                    sems.at[t],
                ).start()
        return
    z, x, y, core = (place_ref[i] for i in range(4))
    block = sources[0].shape[1]
    for i, source in enumerate(sources):
        for slot in range(4):
            to_core = core ^ (i >> 2)
            pair, step = (slot, i & 3) if order == "last" else (i & 3, slot)
            second, first = pair >> 1, pair & 1
            to_x = x ^ (first + to_core * (second - first))
            to_y = y ^ (second + to_core * (first - second))
            to_z = z ^ step if order == "xor" else ring_place(ring_place(z) - step)
            to_t = to_y * 2 + to_core
            low = pl.multiple_of((to_z * 2 + to_x) * block, block)
            pltpu.make_async_copy(
                source.at[slot, :, cols], raw.at[to_t, pl.ds(low, block), to], sems.at[to_t]
            ).start()


def wait_all(ref, sem):
    pltpu.make_async_copy(ref, ref, sem).wait()


def send_block(place_ref, staged, outs, sem, d, t, ring):
    z, x, y, core = (place_ref[i] for i in range(4))
    far, near_core = d >> 1, t & 1
    x_off, y_off = x ^ (d & 1), y ^ (t >> 1)
    first, second = (y_off, x_off) if near_core else (x_off, y_off)
    along = (ring_place(far) - ring_place(z)) & 3 if ring else z ^ far
    slot = second * 8 + first * 4 + along
    for side in range(2):

        @pl.when((core ^ near_core) == side)
        def _(side=side):
            pltpu.make_async_copy(staged, outs[side].at[slot], sem).start()


def send_rows(place_ref, stage, outs, sem, t, cols, part=None, ring=False):
    if len(outs) == 1:
        half = stage.shape[0] // 2
        rows = slice(None) if part is None else slice(part * half, (part + 1) * half)
        pltpu.make_async_copy(stage.at[rows, :], outs[0].at[t, rows, cols], sem).start()
        return
    block = outs[0].shape[1]
    for d in range(8) if part is None else range(4 * part, 4 * part + 4):
        staged = stage.at[d * block : (d + 1) * block, :]
        send_block(place_ref, staged, [out.at[:, :, cols] for out in outs], sem, d, t, ring)


def qkv_kernel(count, place_ref, x_ref, gain_ref, bias_ref, bqv_ref, *refs):
    sources = refs[:count]
    q_ref, k_ref, v_ref, n_ref, w_out, raw, sems, w_ref, w_sem = refs[count:]
    blocks = raw.shape[0]
    normed, _ = norm_parts(x_ref[...].astype(F32))
    low = (normed * gain_ref[...] + bias_ref[...]).astype(BF)
    n_ref[...] = low

    @pl.when(pl.program_id(0) == 0)
    def _():
        cols = slice(0, raw.shape[2])
        start_blocks(place_ref, sources, cols, raw, cols, sems)
        for t in range(blocks):
            wait_all(raw.at[t], sems.at[t])

        def piece(t, c):
            return raw[t, :, c * PAIR : (c + 1) * PAIR]

        for t in range(blocks):
            for c in range(4):
                w_ref[c, :, t * PAIR : (t + 1) * PAIR] = piece(t, c)
        for u in range(blocks // 2):
            col = (blocks + u) * PAIR
            for half in range(2):
                left = piece(2 * u, 4 + half)
                right = piece(2 * u + 1, 4 + half)
                w_ref[2 * half, :, col : col + PAIR] = jnp.concatenate(
                    [left[:, :HEAD_DIM], right[:, :HEAD_DIM]], axis=1
                )
                w_ref[2 * half + 1, :, col : col + PAIR] = jnp.concatenate(
                    [left[:, HEAD_DIM:], right[:, HEAD_DIM:]], axis=1
                )
        pltpu.make_async_copy(w_ref, w_out, w_sem).start()

    q_low = (dot_nn(low, w_ref[0]) + bqv_ref[0:1, :]).astype(BF)
    q_ref[...] = q_low * BF(HEAD_DIM ** (-0.5))
    k_ref[...] = dot_nn(low, w_ref[1]).astype(BF)
    v_ref[...] = (dot_nn(low, w_ref[2]) + bqv_ref[1:2, :]).astype(BF)

    @pl.when(pl.program_id(0) == pl.num_programs(0) - 1)
    def _():
        wait_all(w_ref, w_sem)


def project(place, x, gain, bias, bqv, sources, blocks):
    rows, width = x.shape
    row_spec = pl.BlockSpec((TILE, width), lambda i, *_: (i, 0))
    return pl.pallas_call(
        functools.partial(qkv_kernel, len(sources)),
        grid_spec=pltpu.PrefetchScalarGridSpec(
            num_scalar_prefetch=1,
            grid=(rows // TILE,),
            in_specs=[
                row_spec,
                once((1, width), lambda i, *_: (0, 0)),
                once((1, width), lambda i, *_: (0, 0)),
                once((2, width), lambda i, *_: (0, 0)),
            ]
            + [ANY_SPEC] * len(sources),
            out_specs=[row_spec] * 4 + [ANY_SPEC],
            scratch_shapes=[
                pltpu.VMEM((blocks, width, sources[0].shape[-1]), BF),
                pltpu.SemaphoreType.DMA((blocks,)),
                pltpu.VMEM((4, width, width), BF),
                pltpu.SemaphoreType.DMA(()),
            ],
        ),
        out_shape=[jax.ShapeDtypeStruct((rows, width), BF)] * 4
        + [jax.ShapeDtypeStruct((4, width, width), BF)],
        compiler_params=params(),
        cost_estimate=cost(6 * rows * width * width, 16 * rows * width),
        name="project",
    )(place, x, gain, bias, bqv, *sources)


def half_masks():
    lane = lax.broadcasted_iota(jnp.int32, (1, PAIR), 1)
    first = (lane < HEAD_DIM).astype(F32)
    return first.astype(BF), (1.0 - first).astype(BF)


def attend_kernel(len_ref, q_ref, k_ref, v_ref, o_ref, lse_ref):
    rows = q_ref.shape[0]
    length = len_ref[0]
    masks = half_masks()
    lane = lax.broadcasted_iota(jnp.int32, (TILE, PAIR), 1)
    k_pos = lax.broadcasted_iota(jnp.int32, (1, rows), 1)
    bias = jnp.where(k_pos < length, 0.0, NEG_BIG)
    tri = lax.broadcasted_iota(jnp.int32, (TILE, TILE), 0) >= lax.broadcasted_iota(
        jnp.int32, (TILE, TILE), 1
    )
    for n in range(0, rows, TILE):
        q_block = q_ref[n : n + TILE, :]
        scores = []
        for mask in masks:
            q_one = q_block * mask
            s_diag = dot_nt(q_one, k_ref[n : n + TILE, :]) + bias[:, n : n + TILE]
            s_diag = jnp.where(tri, s_diag, NEG_BIG)
            s_rest = dot_nt(q_one, k_ref[:n, :]) + bias[:, :n] if n else None
            scores.append((s_diag, s_rest))
        outs = []
        peaks = []
        totals = []
        for s_diag, s_rest in scores:
            peak = jnp.max(s_diag, axis=1, keepdims=True)
            if n:
                peak = jnp.maximum(peak, jnp.max(s_rest, axis=1, keepdims=True))
            e_diag = jnp.exp(s_diag - peak)
            total = jnp.sum(e_diag, axis=1, keepdims=True)
            acc = dot_nn(e_diag.astype(BF), v_ref[n : n + TILE, :])
            if n:
                e_rest = jnp.exp(s_rest - peak)
                total = total + jnp.sum(e_rest, axis=1, keepdims=True)
                acc = acc + dot_nn(e_rest.astype(BF), v_ref[:n, :])
            outs.append(acc)
            peaks.append(peak)
            totals.append(total)
        first = lane < HEAD_DIM
        both = jnp.where(first, outs[0], outs[1])
        o_ref[n : n + TILE, :] = (both / jnp.where(first, totals[0], totals[1])).astype(BF)
        packed = jnp.where(lane < 8, peaks[0], totals[0])
        packed = jnp.where(lane % 8 == 1, jnp.where(lane < 8, peaks[1], totals[1]), packed)
        flipped = jnp.transpose(packed)
        lse_ref[0, :, n : n + TILE] = flipped[:8, :] + jnp.log(flipped[8:16, :])


def attend(lengths, q, k, v):
    rows, width = q.shape
    pairs = width // PAIR
    pair_spec = pl.BlockSpec((rows, PAIR), lambda i, *_: (0, i))
    return pl.pallas_call(
        attend_kernel,
        grid_spec=pltpu.PrefetchScalarGridSpec(
            num_scalar_prefetch=1,
            grid=(pairs,),
            in_specs=[pair_spec] * 3,
            out_specs=[pair_spec, pl.BlockSpec((1, 8, rows), lambda i, *_: (i, 0, 0))],
        ),
        out_shape=[
            jax.ShapeDtypeStruct((rows, width), BF),
            jax.ShapeDtypeStruct((pairs, 8, rows), F32),
        ],
        compiler_params=params(),
        cost_estimate=cost(16e9 * width / 768, 8 * rows * width),
        name="attend",
    )(lengths, q, k, v)


def attend_back_kernel(
    first, n_out, more, len_ref, place_ref, q_ref, k_ref, v_ref, o_ref, do_ref, lse_ref, n_ref,
    out_ref, *refs
):
    refs = refs[n_out:] if more else refs
    dq_ref, dk_ref, dv_ref = refs[:3]
    outs = refs[3 : 3 + n_out]
    dq_acc, side_s, n_s, stage, n_sem, sem = refs[3 + n_out :]
    rows = q_ref.shape[0]
    width = n_ref.shape[1]
    step = pl.program_id(0)
    length = len_ref[0]
    masks = half_masks()
    wide = stage.shape[2]
    narrow = wide != 3 * PAIR

    @pl.when(step == 0)
    def _():
        pltpu.make_async_copy(n_ref, n_s, n_sem).start()

    prod = jnp.transpose(do_ref[...].astype(F32) * o_ref[...].astype(F32))
    tri = lax.broadcasted_iota(jnp.int32, (TILE, TILE), 0) <= lax.broadcasted_iota(
        jnp.int32, (TILE, TILE), 1
    )
    k_pos = lax.broadcasted_iota(jnp.int32, (TILE, 1), 0)
    dq_acc[...] = jnp.zeros_like(dq_acc)
    heads = []
    for h, mask in enumerate(masks):
        heads.append(
            (
                mask,
                q_ref[...] * mask,
                do_ref[...] * mask,
                lse_ref[0, h : h + 1, :],
                jnp.sum(prod[h * HEAD_DIM : (h + 1) * HEAD_DIM, :], axis=0, keepdims=True),
            )
        )
    for n in range(0, rows, TILE):
        k_block = k_ref[n : n + TILE, :]
        v_block = v_ref[n : n + TILE, :]
        bias = jnp.where(k_pos + n < length, 0.0, NEG_BIG)
        dk = jnp.zeros((TILE, PAIR), F32)
        dv = jnp.zeros((TILE, PAIR), F32)
        work = []
        for mask, q_one, do_one, lse, delta in heads:
            for low, high in ((n, n + TILE), (n + TILE, rows)):
                if low == high:
                    continue
                s = dot_nt(k_block, q_one[low:high]) + bias
                dp = dot_nt(v_block, do_one[low:high])
                work.append((mask, q_one, do_one, lse, delta, low, high, s, dp))
        for mask, q_one, do_one, lse, delta, low, high, s, dp in work:
            if low == n:
                s = jnp.where(tri, s, NEG_BIG)
            p = jnp.exp(s - lse[:, low:high])
            ds = (p * (dp - delta[:, low:high])).astype(BF)
            dv = dv + dot_nn(p.astype(BF), do_one[low:high])
            dk = dk + dot_nn(ds, q_one[low:high])
            dq_acc[low:high, :] += dot_tn(ds, k_block * mask)
        dk_ref[n : n + TILE, :] = dk.astype(BF)
        dv_ref[n : n + TILE, :] = dv.astype(BF)
    dq_ref[...] = (dq_acc[...] * (HEAD_DIM ** (-0.5))).astype(BF)

    grads = [dq_ref[...], dk_ref[...], dv_ref[...]]
    if narrow:
        blank = jnp.zeros((rows, HEAD_DIM), BF)
        sides = [
            jnp.concatenate([g[:, c : c + HEAD_DIM] for g in grads] + [blank], axis=1)
            for c in (0, HEAD_DIM)
        ]
    else:
        sides = [jnp.concatenate(grads, axis=1)]
    pairs = side_s.shape[1] // (wide * len(sides))
    for at in range(pairs):

        @pl.when(step == at)
        def _(at=at):
            for i, side in enumerate(sides):
                spot = at * len(sides) + i
                side_s[:, spot * wide : (spot + 1) * wide] = side

    @pl.when(step == pairs - 1)
    def _():
        pltpu.make_async_copy(n_ref, n_s, n_sem).wait()
        low_col = 3 * PAIR if narrow else 0
        columns = slice(low_col, low_col + wide)
        for part in range(2):
            cols = slice(part * width // 2, (part + 1) * width // 2)
            grad = dot_tn(n_s[:, cols], side_s[...]).astype(BF)
            for spot in range(stage.shape[0]):
                t = spot if narrow else first + spot
                begin = spot * wide
                if narrow:
                    stage[spot, cols, :PAIR] = grad[:, begin : begin + PAIR]
                    extra = out_ref[cols, spot * HEAD_DIM : (spot + 1) * HEAD_DIM]
                    stage[spot, cols, PAIR:] = jnp.concatenate(
                        [grad[:, begin + PAIR : begin + PAIR + HEAD_DIM], extra], axis=1
                    )
                else:
                    stage[spot, cols, :] = grad[:, begin : begin + wide]
                send_rows(place_ref, stage.at[spot], outs, sem, t, columns, part)
        wait_all(stage, sem)


def attend_back(
    place, lengths, first, pairs, wide, q, k, v, out, d_out, lse, normed, last_out, blocks,
    so_far, fast,
):
    rows, width = q.shape
    at_pair = pl.BlockSpec((rows, PAIR), lambda i, *_: (0, first + i))
    own_pair = pl.BlockSpec((rows, PAIR), lambda i, *_: (0, i))
    grads = grad_shapes(fast, blocks, width, 5 * PAIR)
    so_far = so_far or []
    sides = 1 if wide == 3 * PAIR else 2
    return pl.pallas_call(
        functools.partial(attend_back_kernel, first, len(grads), bool(so_far)),
        grid_spec=pltpu.PrefetchScalarGridSpec(
            num_scalar_prefetch=2,
            grid=(pairs,),
            in_specs=[at_pair] * 5
            + [
                pl.BlockSpec((1, 8, rows), lambda i, *_: (first + i, 0, 0)),
                ANY_SPEC,
                once(last_out.shape, lambda i, *_: (0, 0)),
            ]
            + [ANY_SPEC] * len(so_far),
            out_specs=[own_pair] * 3 + [ANY_SPEC] * len(grads),
            scratch_shapes=[
                pltpu.VMEM((rows, PAIR), F32),
                pltpu.VMEM((rows, pairs * sides * wide), BF),
                pltpu.VMEM((rows, width), BF),
                pltpu.VMEM((pairs * sides, width, wide), BF),
                pltpu.SemaphoreType.DMA(()),
                pltpu.SemaphoreType.DMA(()),
            ],
        ),
        out_shape=[jax.ShapeDtypeStruct((rows, pairs * PAIR), BF)] * 3 + grads,
        input_output_aliases={10 + i: 3 + i for i in range(len(so_far))},
        compiler_params=params(),
        cost_estimate=cost(3e9 * pairs, 5e6 * pairs),
        name="attend_back",
    )(lengths, place, q, k, v, out, d_out, lse, normed, last_out, *so_far)


def vec_rows(vec_ref):
    return lambda i: vec_ref[i : i + 1, :]


def tile_rows(i):
    return pl.ds(pl.multiple_of(i * TILE, TILE), TILE)


def grad_shapes(fast, blocks, width, wide):
    if fast:
        return [jax.ShapeDtypeStruct((16, width // 8, wide), BF)] * 2
    return [jax.ShapeDtypeStruct((blocks, width, wide), BF)]


def feed_kernel(
    counts, place_ref, att_ref, x_ref, cot_ref, wo_ref, vec_ref, bup_ref, *refs
):
    one, two = counts
    refs, sources = refs[one + two :], (refs[:one], refs[one : one + two])
    resid_out, act_ref, gbup_ref, dres_out, datt_out, sums_ref, last_out_ref = refs[:7]
    refs = refs[7:]
    n_out = (len(refs) - 13) // 2
    up_outs, down_outs = refs[:n_out], refs[n_out : 2 * n_out]
    raw, sems, n_two, d_pre_s, d_norm, low, stage, stage_down, sem = refs[2 * n_out : -4]
    resid_ref, dres_ref, datt_ref, out_sems = refs[-4:]
    rows, width = x_ref.shape
    step = pl.program_id(0)
    tiles = rows // TILE
    blocks = stage.shape[0]
    vec = vec_rows(vec_ref)
    half_width = width // 2
    cut = sources[0][0].shape[-1] // 2

    @pl.when(step == 0)
    def _():
        begin = 0
        sizes, orders = (cut, width - cut), ("ring", "last")
        for source, size, order in zip(sources, sizes, orders, strict=True):
            for to in (begin, width + begin):
                start_blocks(
                    place_ref,
                    source,
                    slice(0 if to < width else size, size if to < width else 2 * size),
                    raw,
                    slice(to, to + size),
                    sems,
                    order,
                )
            begin += size

        def body(i, _):
            r = tile_rows(i)
            res = x_ref[r, :].astype(F32) + dot_nt(att_ref[r, :], wo_ref[0]) + vec(0)
            resid_ref[r, :] = res
            normed, _ = norm_parts(res)
            n_two[r, :] = (normed * vec(1) + vec(2)).astype(BF)
            d_norm[r, :] = jnp.zeros((TILE, width), F32)
            return 0

        lax.fori_loop(0, tiles, body, 0)
        pltpu.make_async_copy(resid_ref, resid_out, out_sems.at[0]).start()

    wait_all(raw.at[step], sems.at[step])
    w_up = raw[step, :, :width]
    w_down = raw[step, :, width:]
    c_one = 0.7978845608028654
    c_two = 0.044715

    def body(i, total):
        r = tile_rows(i)
        u = dot_nn(n_two[r, :], w_up) + bup_ref[0]
        d_act = dot_nn(cot_ref[r, :], w_down)
        square = u * u
        t = jnp.tanh(c_one * u * (1.0 + c_two * square))
        half = 0.5 * (1.0 + t)
        act_ref[r, :] = (u * half).astype(BF)
        slope = half + 0.5 * u * (1.0 - t * t) * (c_one * (1.0 + 3.0 * c_two * square))
        d_pre = (d_act * slope).astype(BF)
        d_pre_s[r, :] = d_pre
        d_norm[r, :] += dot_nt(d_pre, w_up)
        return total + col_sum(d_pre.astype(F32))

    gbup_ref[0] = lax.fori_loop(0, tiles, body, jnp.zeros((1, width), F32), unroll=True)
    def grads(i, _):
        cols = tile_rows(i)
        stage[step, cols, :width] = dot_tn(n_two[:, cols], d_pre_s[...]).astype(BF)
        stage_down[step, cols, :] = dot_tn(cot_ref[:, cols], act_ref[...]).astype(BF)
        return 0

    lax.fori_loop(0, width // TILE, grads, 0)
    first_cols = slice(0, width)
    for t in range(blocks):

        @pl.when(step == t)
        def _(t=t):
            send_rows(place_ref, stage.at[t, :, first_cols], up_outs, sem, t, first_cols)
            send_rows(place_ref, stage_down.at[t], down_outs, sem, t, first_cols)

    @pl.when(step == pl.num_programs(0) - 1)
    def _():
        def body(i, sums):
            r = tile_rows(i)
            normed, scale = norm_parts(resid_ref[r, :])
            d_n = d_norm[r, :]
            d_out = cot_ref[r, :].astype(F32)
            d_res = d_out + norm_back(d_n * vec(1), normed, scale)
            dres_ref[r, :] = d_res
            d_low = d_res.astype(BF)
            low[r, :] = d_low
            datt_ref[r, :] = dot_nn(d_low, wo_ref[0]).astype(BF)
            pltpu.make_async_copy(dres_ref.at[r, :], dres_out.at[r, :], out_sems.at[1]).start()
            pltpu.make_async_copy(datt_ref.at[r, :], datt_out.at[r, :], out_sems.at[2]).start()
            more = (col_sum(d_n * normed), col_sum(d_n), col_sum(d_res), col_sum(d_out))
            return tuple(a + b for a, b in zip(sums, more, strict=True))

        sums = lax.fori_loop(0, tiles, body, (jnp.zeros((1, width), F32),) * 4)
        sums_ref[...] = jnp.zeros_like(sums_ref)
        for i in range(4):
            sums_ref[i : i + 1, :] = sums[i]
        side = width
        for c in range(0, width, half_width):
            rows_c = slice(c, c + half_width)
            go = dot_tn(low[:, rows_c], att_ref[...]).astype(BF)
            last_out_ref[rows_c, :] = go[:, blocks * PAIR :]
            for t in range(blocks):
                stage[t, rows_c, side:] = go[:, t * PAIR : (t + 1) * PAIR]
        cols = slice(side, side + PAIR)
        for t in range(blocks):
            send_rows(place_ref, stage.at[t, :, cols], up_outs, sem, t, cols)
        wait_all(stage, sem)
        wait_all(stage_down, sem)
        for i, ref in enumerate((resid_ref, dres_ref, datt_ref)):
            wait_all(ref, out_sems.at[i])


def feed_forward(place, att, x, cot, w_all, vecs, b_up, sources_one, sources_two, fast):
    rows, width = x.shape
    blocks = b_up.shape[0]
    whole = once((rows, width), lambda t, *_: (0, 0))
    up_vec = pl.BlockSpec((1, 1, width), lambda t, *_: (t, 0, 0))
    grads = grad_shapes(fast, blocks, width, width + PAIR)
    grads += grad_shapes(fast, blocks, width, width)
    counts = (len(sources_one), len(sources_two))
    return pl.pallas_call(
        functools.partial(feed_kernel, counts),
        grid_spec=pltpu.PrefetchScalarGridSpec(
            num_scalar_prefetch=1,
            grid=(blocks,),
            in_specs=[
                whole,
                whole,
                whole,
                once((1, width, width), lambda t, *_: (3, 0, 0)),
                once((8, width), lambda t, *_: (0, 0)),
                up_vec,
            ]
            + [ANY_SPEC] * sum(counts),
            out_specs=[
                ANY_SPEC,
                pl.BlockSpec((rows, width), lambda t, *_: (0, t)),
                up_vec,
                ANY_SPEC,
                ANY_SPEC,
                once((8, width), lambda t, *_: (0, 0)),
                once((width, width - blocks * PAIR), lambda t, *_: (0, 0)),
            ]
            + [ANY_SPEC] * len(grads),
            scratch_shapes=[
                pltpu.VMEM((blocks, width, 2 * width), BF),
                pltpu.SemaphoreType.DMA((blocks,)),
                pltpu.VMEM((rows, width), BF),
                pltpu.VMEM((rows, width), BF),
                pltpu.VMEM((rows, width), F32),
                pltpu.VMEM((rows, width), BF),
                pltpu.VMEM((blocks, width, width + PAIR), BF),
                pltpu.VMEM((blocks, width, width), BF),
                pltpu.SemaphoreType.DMA(()),
                pltpu.VMEM((rows, width), F32),
                pltpu.VMEM((rows, width), F32),
                pltpu.VMEM((rows, width), BF),
                pltpu.SemaphoreType.DMA((3,)),
            ],
        ),
        out_shape=[
            jax.ShapeDtypeStruct((rows, width), F32),
            jax.ShapeDtypeStruct((rows, blocks * width), BF),
            jax.ShapeDtypeStruct((blocks, 1, width), F32),
            jax.ShapeDtypeStruct((rows, width), F32),
            jax.ShapeDtypeStruct((rows, width), BF),
            jax.ShapeDtypeStruct((8, width), F32),
            jax.ShapeDtypeStruct((width, width - blocks * PAIR), BF),
        ]
        + grads,
        compiler_params=params(),
        cost_estimate=cost(40e9, 40e6),
        name="feed_forward",
    )(place, att, x, cot, w_all, vecs, b_up, *sources_one, *sources_two)


def hidden_kernel(counts, place_ref, act_ref, resid_ref, vec_ref, *refs):
    one, two = counts
    refs, sources = refs[one + two :], (refs[:one], refs[one : one + two])
    out_ref, raw, sems = refs
    blocks, _, width = raw.shape
    cut = sources[0][0].shape[-1] // 2

    @pl.when(pl.program_id(0) == 0)
    def _():
        begin = 0
        sizes, orders = (cut, width - cut), ("ring", "last")
        for source, size, order in zip(sources, sizes, orders, strict=True):
            to = slice(begin, begin + size)
            start_blocks(place_ref, source, slice(size, 2 * size), raw, to, sems, order)
            begin += size
        for t in range(blocks):
            wait_all(raw.at[t], sems.at[t])

    acc = resid_ref[...] + vec_ref[3:4, :]
    for t in range(blocks):
        acc = acc + dot_nt(act_ref[:, t * width : (t + 1) * width], raw[t])
    out_ref[...] = acc.astype(BF)


def hidden_rows(place, act, resid, vecs, sources_one, sources_two):
    rows, width = resid.shape
    blocks = act.shape[1] // width
    row_spec = pl.BlockSpec((TILE, width), lambda i, *_: (i, 0))
    counts = (len(sources_one), len(sources_two))
    return pl.pallas_call(
        functools.partial(hidden_kernel, counts),
        grid_spec=pltpu.PrefetchScalarGridSpec(
            num_scalar_prefetch=1,
            grid=(rows // TILE,),
            in_specs=[
                pl.BlockSpec((TILE, blocks * width), lambda i, *_: (i, 0)),
                row_spec,
                once((8, width), lambda i, *_: (0, 0)),
            ]
            + [ANY_SPEC] * sum(counts),
            out_specs=row_spec,
            scratch_shapes=[
                pltpu.VMEM((blocks, width, width), BF),
                pltpu.SemaphoreType.DMA((blocks,)),
            ],
        ),
        out_shape=jax.ShapeDtypeStruct((rows, width), BF),
        compiler_params=params(),
        cost_estimate=cost(5e9, 12e6),
        name="hidden_rows",
    )(place, act, resid, vecs, *sources_one, *sources_two)


def input_kernel(*refs):
    parts = refs[:6]
    w_ref, x_ref, dres_ref, gain_ref, gin_ref, sums_ref = refs[6:]

    @pl.when(pl.program_id(0) == 0)
    def _():
        sums_ref[...] = jnp.zeros_like(sums_ref)

    dq, dk, dv = (jnp.concatenate([part[...] for part in parts[i::3]], axis=1) for i in range(3))
    d_norm = dot_nt(dq, w_ref[0]) + dot_nt(dk, w_ref[1]) + dot_nt(dv, w_ref[2])
    normed, scale = norm_parts(x_ref[...].astype(F32))
    gin_ref[...] = dres_ref[...] + norm_back(d_norm * gain_ref[...], normed, scale)
    more = (
        col_sum(d_norm * normed),
        col_sum(d_norm),
        col_sum(dq.astype(F32)),
        col_sum(dv.astype(F32)),
    )
    for i, value in enumerate(more):
        sums_ref[i : i + 1, :] += value


def input_grad(parts, w_all, x, d_resid, gain):
    rows, width = x.shape
    row_spec = pl.BlockSpec((TILE, width), lambda i: (i, 0))
    return pl.pallas_call(
        input_kernel,
        grid=(rows // TILE,),
        in_specs=[pl.BlockSpec((TILE, part.shape[1]), lambda i: (i, 0)) for part in parts]
        + [
            once((3, width, width), lambda i: (0, 0, 0)),
            row_spec,
            row_spec,
            once((1, width), lambda i: (0, 0)),
        ],
        out_specs=[row_spec, pl.BlockSpec((8, width), lambda i: (0, 0))],
        out_shape=[
            jax.ShapeDtypeStruct((rows, width), F32),
            jax.ShapeDtypeStruct((8, width), F32),
        ],
        compiler_params=params(),
        cost_estimate=cost(6 * rows * width * width, 16 * rows * width),
        name="input_grad",
    )(*parts, w_all, x, d_resid, gain)


def body(
    n_dp,
    n_tensor,
    hidden_in,
    cotangent,
    lengths,
    latent,
    ln1_gain,
    ln1_bias,
    w_qkv,
    b_qv,
    w_out,
    b_out,
    ln2_gain,
    ln2_bias,
    w_up,
    b_up,
    w_down,
    b_down,
):
    rows, width = hidden_in.shape
    t_index = lax.axis_index("tensor")
    block = w_up.shape[0]
    heads = w_qkv.shape[2] // HEAD_DIM

    out_t = w_out.T
    packed = jnp.concatenate(
        [w_qkv[0, :, :PAIR], w_qkv[1, :, :PAIR], w_qkv[2, :, :PAIR], out_t[:, :PAIR]]
        + [w_qkv[0, :, PAIR:], w_qkv[1, :, PAIR:], w_qkv[2, :, PAIR:], out_t[:, PAIR:]],
        axis=1,
    ).astype(BF)
    packed, up_part, down_part = after(packed, w_up, w_down)
    down_t = down_part.T
    cut = w_up.shape[1] * 2 // 3
    packed_one = jnp.concatenate([up_part[:, :cut], down_t[:, :cut]], axis=1).astype(BF)
    packed_two = jnp.concatenate([up_part[:, cut:], down_t[:, cut:]], axis=1).astype(BF)
    own_length = lax.dynamic_slice_in_dim(lengths, t_index, 1, 0)
    own_latent = lax.dynamic_slice_in_dim(latent, t_index, 1, 0)
    positions = lax.broadcasted_iota(jnp.int32, (1, rows), 1)
    keep = ((positions < own_length) & (own_latent == 0)).astype(BF).reshape(rows, 1)
    cot = cotangent * keep

    fast = n_dp == 8 and n_tensor == 4
    d_index = lax.axis_index("dp")
    place = jnp.stack([d_index >> 1, d_index & 1, t_index >> 1, t_index & 1]).astype(jnp.int32)

    def gather(piece):
        wide = piece.shape[1]
        full = lax.all_gather(piece, BOTH, axis=0, tiled=False)
        full = full.reshape(n_dp, n_tensor, block, wide)
        if fast:
            return full
        return full.transpose(1, 0, 2, 3).reshape(1, n_tensor, width, wide)

    project_place = place
    def to_inner(b):
        split = b.reshape(b.shape[0], n_tensor, heads, HEAD_DIM)
        return jnp.concatenate(
            [split[:, :, :2].reshape(b.shape[0], -1), split[:, :, 2:].reshape(b.shape[0], -1)],
            axis=1,
        )

    zero = jnp.zeros_like(b_out)
    early = [
        cot,
        place,
        own_length,
        to_inner(b_qv),
        ln1_gain[None],
        ln1_bias[None],
        jnp.stack([b_out, ln2_gain, ln2_bias, b_down, zero, zero, zero, zero]),
        b_up.reshape(n_tensor, 1, width),
    ]
    if fast:
        def grow(array, came):
            return jnp.concatenate([array, came])

        att, one, two = packed[None], packed_one[None], packed_two[None]
        att_came, two_came, one, *early = after(
            exchange(att, flip_near), exchange(two, flip_first), one, *early
        )
        att, two = grow(att, att_came), grow(two, two_came)
        att_came, two_came, one_one = after(
            exchange(att, flip_far), exchange(two, flip_second), exchange(one, flip_ring)
        )
        att, two = grow(att, att_came), grow(two, two_came)
        att_first, att_second, one_two, two_one = after(
            exchange(att, flip_first),
            exchange(att, flip_second),
            exchange(one_one, flip_ring),
            exchange(two, flip_ring),
        )
        halves = [att, att_first, att_second]
        att_both, one_last, *cores = after(
            exchange(att_first, flip_second),
            exchange(one_two, flip_ring),
            *(exchange(half, flip_core) for half in halves),
        )
        sources = [*halves, att_both, *cores, exchange(att_both, flip_core)]
        one = jnp.concatenate([one, one_one, one_two, one_last])
        one_first, two_two = exchange(one, flip_first), exchange(two_one, flip_ring)
    else:
        sources = [gather(packed)]
        sources_one, sources_two = [gather(packed_one)], [gather(packed_two)]

    def from_inner(b):
        cut = n_tensor * PAIR
        first = b[:, :cut].reshape(b.shape[0], n_tensor, 2, HEAD_DIM)
        rest = b[:, cut:].reshape(b.shape[0], n_tensor, heads - 2, HEAD_DIM)
        return jnp.concatenate([first, rest], axis=2).reshape(b.shape[0], width)

    cot, place, own_length, inner_bqv, gain, bias, vecs, up_bias = early
    q, k, v, normed_one, w_all = project(
        place, hidden_in, gain, bias, inner_bqv, sources, n_tensor
    )
    if fast:
        one_first, two_two, q = after(one_first, two_two, q)
        halves = [one, one_first, two, two_one, two_two]
        cores = [exchange(half, flip_core) for half in halves]
        came = [exchange(half, flip_second) for half in halves[:2]]
        came.append(exchange(two_two, flip_ring))
    attended, lse = attend(own_length, q, k, v)
    if fast:
        attended, *moved = after(attended, *came, *cores)
        came, cores = moved[:3], moved[3:]
        cores += [exchange(half, flip_core) for half in came]
        sources_one = [*halves[:2], *came[:2], *cores[:2], *cores[5:7]]
        sources_two = [*halves[2:], came[2], *cores[2:5], cores[7]]
    resid, act, g_b_up, d_resid, d_attended, sums_two, last_out, *g_mlp = feed_forward(
        place, attended, hidden_in, cot, w_all, vecs, up_bias, sources_one, sources_two, fast
    )

    half = len(g_mlp) // 2

    def back(length, first, pairs, wide, so_far):
        return list(
            attend_back(
                place, length, first, pairs, wide, q, k, v, attended, d_attended, lse,
                normed_one, last_out, n_tensor, so_far, fast,
            )
        )

    def vectors(sums_one):
        return jnp.concatenate([sums_one[:4], sums_two[:4], g_b_up.reshape(n_tensor, width)])

    if fast:
        up, down = Scatter(*g_mlp[:half]), Scatter(*g_mlp[half:])
        came_up, came_down = up.step(), down.step()
        hidden_out = hidden_rows(place, act, resid, vecs, sources_one, sources_two)
        came_up, came_down, length, hidden_out = after(
            came_up, came_down, own_length, hidden_out
        )
        up.sent, down.sent = sums(up.want(came_up), down.want(came_down))
        came_up, came_down = up.step(), down.step()
        back_one = back(length, 0, 4, 3 * PAIR, None)
        came_up, length, *back_one = after(came_up, own_length, *back_one)
        (up.sent,) = sums(up.want(came_up))
        came_up = up.step()
        back_two = back(length, 4, 2, 2 * PAIR, back_one[3:])
        came_up, came_down, gain, *back_two = after(came_up, came_down, gain, *back_two)
        rest = Scatter(*back_two[3:])
        came_rest = rest.step()
        up.sent, down.sent = sums(up.want(came_up), down.want(came_down))
        came_rest, up.sent, down.sent = after(came_rest, up.sent, down.sent)
        came_up, came_down = up.step(), down.step()
        (rest.sent,) = sums(rest.want(came_rest))
        came_rest = rest.step()
        parts = [*back_one[:3], *back_two[:3]]
        grad_in, sums_one = input_grad(parts, w_all, hidden_in, d_resid, gain)
        came_rest, came_down, sums_one, grad_in = after(came_rest, came_down, sums_one, grad_in)
        rest.sent, down.sent = sums(rest.want(came_rest), down.want(came_down))
        came_up, rest.sent, down.sent = after(came_up, rest.sent, down.sent)
        came_rest, came_down = rest.step(), down.step()
        (up.sent,) = plain_sums(up.want(came_up))
        came_up = up.step()
        small = vectors(sums_one)
        small = small + exchange(small, flip_core)
        came_small = exchange(small, flip_second)
        small = small + came_small
        came_small = exchange(small, flip_first)
        came_rest, came_down, came_small = after(came_rest, came_down, came_small)
        (rest.sent,) = plain_sums(rest.want(came_rest))
        small = small + came_small
        rest.sent, came_down = after(rest.sent, came_down)
        came_rest, came_small = rest.step(), exchange(small, flip_far)
        (down.sent,) = plain_sums(down.want(came_down))
        came_down = down.step()
        came_rest, came_small, came_up, came_down = after(
            came_rest, came_small, came_up, came_down
        )
        (rest.sent,) = plain_sums(rest.want(came_rest))
        small = small + came_small
        came_rest, came_small = rest.step(), exchange(small, flip_near)
        small = small + came_small
        g_up, g_out, g_down, g_qkv = last_sums(
            [*up.terms, came_up], [*down.terms, came_down], [*rest.terms, came_rest]
        )
    else:
        back_one = back(own_length, 0, 4, 3 * PAIR, None)
        back_two = back(own_length, 4, 2, 2 * PAIR, back_one[3:])
        parts = [*back_one[:3], *back_two[:3]]
        grad_in, sums_one = input_grad(parts, w_all, hidden_in, d_resid, gain)
        hidden_out = hidden_rows(place, act, resid, vecs, sources_one, sources_two)
        small = lax.psum(vectors(sums_one), BOTH)

        def scatter_all(grads):
            wide = grads.shape[-1]
            grads = grads.reshape(n_tensor, n_dp, block, wide).transpose(1, 0, 2, 3)
            flat = grads.reshape(n_dp * n_tensor * block, wide)
            total = lax.psum_scatter(flat, BOTH, scatter_dimension=0, tiled=True)
            return total.astype(F32)

        g_up, g_down, g_rest = (scatter_all(g) for g in (*g_mlp, back_two[3]))
        g_out, g_qkv = split_columns(g_up, g_rest)
        g_out = g_out.T
        g_up = g_up[:, :width]
    g_bqv = from_inner(small[2:4])

    return (
        hidden_out,
        grad_in,
        small[0],
        small[1],
        g_qkv,
        g_bqv,
        g_out,
        small[6],
        small[4],
        small[5],
        g_up,
        small[8:].reshape(-1),
        g_down.T,
        small[7],
    )


def solution(mesh):
    placed = (
        P(BOTH, None),
        P(BOTH, None),
        P("dp"),
        P("dp", None),
        P(),
        P(),
        P(None, "dp", "tensor"),
        P(),
        P("tensor", "dp"),
        P(),
        P(),
        P(),
        P("dp", "tensor"),
        P(),
        P("tensor", "dp"),
        P(),
    )
    return jax.shard_map(
        functools.partial(body, mesh.shape["dp"], mesh.shape["tensor"]),
        mesh=mesh,
        in_specs=placed,
        out_specs=(
            P(BOTH, None),
            P(BOTH, None),
            P(),
            P(),
            P(None, "dp", "tensor"),
            P(),
            P("tensor", "dp"),
            P(),
            P(),
            P(),
            P("dp", "tensor"),
            P(),
            P("tensor", "dp"),
            P(),
        ),
        check_vma=False,
    )
```

```python
import functools

import jax
import jax.numpy as jnp
from jax import lax
from jax.experimental import pallas as pl
from jax.experimental.pallas import tpu as pltpu
from jax.sharding import PartitionSpec as P

HEAD_DIM = 64
LEN = 1024
PAIR = 2 * HEAD_DIM
TILE = 256
NEG_BIG = -1e30
EPSILON = 1e-05
VMEM_BYTES = 66_900_000
BF = jnp.bfloat16
F32 = jnp.float32
BOTH = ("dp", "tensor")
ANY_SPEC = pl.BlockSpec(memory_space=pl.ANY)


def dot_nn(a, b):
    return lax.dot_general(a, b, (((1,), (0,)), ((), ())), preferred_element_type=F32)


def dot_nt(a, b):
    return lax.dot_general(a, b, (((1,), (1,)), ((), ())), preferred_element_type=F32)


def dot_tn(a, b):
    return lax.dot_general(a, b, (((0,), (0,)), ((), ())), preferred_element_type=F32)


def norm_parts(rows_in):
    center = rows_in - jnp.mean(rows_in, axis=-1, keepdims=True)
    spread = jnp.mean(center * center, axis=-1, keepdims=True)
    scale = lax.rsqrt(spread + EPSILON)
    return center * scale, scale


def norm_back(gy, normed, scale):
    mean_gy = jnp.mean(gy, axis=-1, keepdims=True)
    mean_gyn = jnp.mean(gy * normed, axis=-1, keepdims=True)
    return (gy - mean_gy - normed * mean_gyn) * scale


def col_sum(values):
    return jnp.sum(values, axis=0, keepdims=True)


def once(shape, index):
    return pl.BlockSpec(shape, index, pipeline_mode=pl.Buffered(1))


def params(side_effects=False):
    return pltpu.CompilerParams(
        dimension_semantics=("arbitrary",),
        vmem_limit_bytes=VMEM_BYTES,
        has_side_effects=side_effects,
    )


def cost(flops, moved, exps=0):
    return pl.CostEstimate(flops=int(flops), bytes_accessed=int(moved), transcendentals=int(exps))


def place_of(index):
    return (index >> 3) & 3, (index >> 2) & 1, (index >> 1) & 1, index & 1


def index_of(z, x, y, core):
    return (z << 3) | (x << 2) | (y << 1) | core


def exchange(array, flip):
    pairs = [(i, index_of(*flip(*place_of(i)))) for i in range(32)]
    return lax.ppermute(array, BOTH, pairs)


def flip_first(z, x, y, core):
    return (z, x, y ^ 1, core) if core else (z, x ^ 1, y, core)


def flip_second(z, x, y, core):
    return (z, x ^ 1, y, core) if core else (z, x, y ^ 1, core)


def flip_core(z, x, y, core):
    return z, x, y, core ^ 1


def flip_near(z, x, y, core):
    return z ^ 1, x, y, core


def flip_far(z, x, y, core):
    return z ^ 2, x, y, core


def sums_kernel(plan, *refs):
    count_in = sum(len(offsets) for offsets, _ in plan)
    outs = refs[count_in : count_in + len(plan)]
    scratch = refs[count_in + len(plan) :]
    position = 0
    for i, (offsets, count) in enumerate(plan):
        terms, _, sems, _ = scratch[4 * i : 4 * i + 4]
        for slot in range(count):
            for k, offset in enumerate(offsets):
                pltpu.make_async_copy(
                    refs[position + k].at[offset + slot], terms.at[slot, k], sems.at[slot]
                ).start()
        position += len(offsets)
    for i, (offsets, count) in enumerate(plan):
        terms, result, sems, out_sem = scratch[4 * i : 4 * i + 4]

        def body(slot, _, i=i, size=len(offsets)):
            terms, result, sems, out_sem = scratch[4 * i : 4 * i + 4]
            wait_all(terms.at[slot], sems.at[slot])
            total = terms[slot, 0].astype(F32)
            for k in range(1, size):
                total = total + terms[slot, k].astype(F32)
            result[slot] = total.astype(BF)
            pltpu.make_async_copy(result.at[slot], outs[i].at[slot], out_sem).start()
            return 0

        lax.fori_loop(0, count, body, 0)
    for i in range(len(plan)):
        wait_all(scratch[4 * i + 1], scratch[4 * i + 3])


def sums(*requests):
    plan, arrays, shapes, scratch = [], [], [], []
    for terms, count in requests:
        block = terms[0][0].shape[1:]
        plan.append((tuple(offset for _, offset in terms), count))
        arrays += [array for array, _ in terms]
        shapes.append(jax.ShapeDtypeStruct((count, *block), BF))
        scratch += [
            pltpu.VMEM((count, len(terms), *block), BF),
            pltpu.VMEM((count, *block), BF),
            pltpu.SemaphoreType.DMA((count,)),
            pltpu.SemaphoreType.DMA(()),
        ]
    return pl.pallas_call(
        functools.partial(sums_kernel, plan),
        in_specs=[ANY_SPEC] * len(arrays),
        out_specs=[ANY_SPEC] * len(shapes),
        out_shape=shapes,
        scratch_shapes=scratch,
        compiler_params=pltpu.CompilerParams(vmem_limit_bytes=VMEM_BYTES),
        cost_estimate=cost(1e6, 8e6),
        name="sums",
    )(*arrays)


def plain_sums(*requests):
    results = []
    for terms, count in requests:
        total = None
        for array, offset in terms:
            part = array[offset : offset + count].astype(F32)
            total = part if total is None else total + part
        results.append(total.astype(BF))
    return results


def split_columns(up, rest):
    width = up.shape[1] - PAIR
    side = 3 * PAIR
    out = jnp.concatenate([up[:, width:], rest[:, side + 3 * HEAD_DIM :]], axis=1)
    three = []
    for i in range(3):
        begin = side + i * HEAD_DIM
        parts = [rest[:, i * PAIR : (i + 1) * PAIR], rest[:, begin : begin + HEAD_DIM]]
        three.append(jnp.concatenate(parts, axis=1))
    return out, jnp.stack(three)


def last_kernel(counts, *refs):
    sources, rest_of = refs[: sum(counts)], refs[sum(counts) :]
    up_ref, out_ref, down_ref, qkv_ref = rest_of[:4]
    scratch, sems = rest_of[4:7], rest_of[7]
    position = 0
    for i, count in enumerate(counts):
        for k in range(count):
            pltpu.make_async_copy(
                sources[position + k].at[0], scratch[i].at[k], sems.at[i]
            ).start()
        position += count
    totals = []
    for i, count in enumerate(counts):
        wait_all(scratch[i], sems.at[i])
        total = scratch[i][0].astype(F32)
        for k in range(1, count):
            total = total + scratch[i][k].astype(F32)
        totals.append(total)
    up, down, rest = totals
    up_ref[...] = up[:, : up_ref.shape[1]]
    down_ref[...] = down
    out, qkv_ref[...] = split_columns(up, rest)
    out_ref[...] = jnp.transpose(out)


def last_sums(*chains):
    counts = [len(terms) for terms in chains]
    block = chains[0][0].shape[1]
    width, third = chains[1][0].shape[2], 3 * HEAD_DIM
    whole = pl.BlockSpec(memory_space=pltpu.VMEM)
    return pl.pallas_call(
        functools.partial(last_kernel, counts),
        in_specs=[ANY_SPEC] * sum(counts),
        out_specs=[whole] * 4,
        out_shape=[
            jax.ShapeDtypeStruct((block, width), F32),
            jax.ShapeDtypeStruct((third, block), F32),
            jax.ShapeDtypeStruct((block, width), F32),
            jax.ShapeDtypeStruct((3, block, third), F32),
        ],
        scratch_shapes=[
            pltpu.VMEM((len(terms), block, terms[0].shape[2]), BF) for terms in chains
        ]
        + [pltpu.SemaphoreType.DMA((3,))],
        compiler_params=pltpu.CompilerParams(vmem_limit_bytes=VMEM_BYTES),
        cost_estimate=cost(1e6, 4e6),
        name="last_sums",
    )(*(term for terms in chains for term in terms))


class Scatter:
    def __init__(self, kept, sent):
        self.terms, self.sent = [kept], sent
        self.flips = [flip_core, flip_second, flip_first, flip_far, flip_near]

    def step(self):
        return exchange(self.sent, self.flips.pop(0))

    def want(self, came):
        self.terms = [*self.terms, came]
        count = came.shape[0] // 2
        return [(array, count) for array in self.terms], count


def after(value, *others):
    return lax.optimization_barrier((value, *others))


def ring_place(z):
    z = z & 3
    return z ^ (z >> 1)


def flip_ring(z, x, y, core):
    return ring_place(ring_place(z) + 1), x, y, core


def start_blocks(place_ref, sources, cols, raw, to, sems, order="xor"):
    if len(sources) == 1:
        nd, blocks, block, _ = sources[0].shape
        for d in range(nd):
            for t in range(blocks):
                pltpu.make_async_copy(
                    sources[0].at[d, t, :, cols],
                    raw.at[t, d * block : (d + 1) * block, to],
                    sems.at[t],
                ).start()
        return
    z, x, y, core = (place_ref[i] for i in range(4))
    block = sources[0].shape[1]
    for i, source in enumerate(sources):
        for slot in range(4):
            to_core = core ^ (i >> 2)
            pair, step = (slot, i & 3) if order == "last" else (i & 3, slot)
            second, first = pair >> 1, pair & 1
            to_x = x ^ (first + to_core * (second - first))
            to_y = y ^ (second + to_core * (first - second))
            to_z = z ^ step if order == "xor" else ring_place(ring_place(z) - step)
            to_t = to_y * 2 + to_core
            low = pl.multiple_of((to_z * 2 + to_x) * block, block)
            pltpu.make_async_copy(
                source.at[slot, :, cols], raw.at[to_t, pl.ds(low, block), to], sems.at[to_t]
            ).start()


def wait_all(ref, sem):
    pltpu.make_async_copy(ref, ref, sem).wait()


def send_block(place_ref, staged, outs, sem, d, t, ring):
    z, x, y, core = (place_ref[i] for i in range(4))
    far, near_core = d >> 1, t & 1
    x_off, y_off = x ^ (d & 1), y ^ (t >> 1)
    first, second = (y_off, x_off) if near_core else (x_off, y_off)
    along = (ring_place(far) - ring_place(z)) & 3 if ring else z ^ far
    slot = second * 8 + first * 4 + along
    for side in range(2):

        @pl.when((core ^ near_core) == side)
        def _(side=side):
            pltpu.make_async_copy(staged, outs[side].at[slot], sem).start()


def send_rows(place_ref, stage, outs, sem, t, cols, part=None, ring=False):
    if len(outs) == 1:
        half = stage.shape[0] // 2
        rows = slice(None) if part is None else slice(part * half, (part + 1) * half)
        pltpu.make_async_copy(stage.at[rows, :], outs[0].at[t, rows, cols], sem).start()
        return
    block = outs[0].shape[1]
    for d in range(8) if part is None else range(4 * part, 4 * part + 4):
        staged = stage.at[d * block : (d + 1) * block, :]
        send_block(place_ref, staged, [out.at[:, :, cols] for out in outs], sem, d, t, ring)


def qkv_kernel(count, place_ref, x_ref, gain_ref, bias_ref, bqv_ref, *refs):
    sources = refs[:count]
    q_ref, k_ref, v_ref, n_ref, w_out, raw, sems, w_ref, w_sem = refs[count:]
    blocks = raw.shape[0]
    normed, _ = norm_parts(x_ref[...].astype(F32))
    low = (normed * gain_ref[...] + bias_ref[...]).astype(BF)
    n_ref[...] = low

    @pl.when(pl.program_id(0) == 0)
    def _():
        cols = slice(0, raw.shape[2])
        start_blocks(place_ref, sources, cols, raw, cols, sems)
        for t in range(blocks):
            wait_all(raw.at[t], sems.at[t])

        def piece(t, c):
            return raw[t, :, c * PAIR : (c + 1) * PAIR]

        for t in range(blocks):
            for c in range(4):
                w_ref[c, :, t * PAIR : (t + 1) * PAIR] = piece(t, c)
        for u in range(blocks // 2):
            col = (blocks + u) * PAIR
            for half in range(2):
                left = piece(2 * u, 4 + half)
                right = piece(2 * u + 1, 4 + half)
                w_ref[2 * half, :, col : col + PAIR] = jnp.concatenate(
                    [left[:, :HEAD_DIM], right[:, :HEAD_DIM]], axis=1
                )
                w_ref[2 * half + 1, :, col : col + PAIR] = jnp.concatenate(
                    [left[:, HEAD_DIM:], right[:, HEAD_DIM:]], axis=1
                )
        pltpu.make_async_copy(w_ref, w_out, w_sem).start()

    q_low = (dot_nn(low, w_ref[0]) + bqv_ref[0:1, :]).astype(BF)
    q_ref[...] = q_low * BF(HEAD_DIM ** (-0.5))
    k_ref[...] = dot_nn(low, w_ref[1]).astype(BF)
    v_ref[...] = (dot_nn(low, w_ref[2]) + bqv_ref[1:2, :]).astype(BF)

    @pl.when(pl.program_id(0) == pl.num_programs(0) - 1)
    def _():
        wait_all(w_ref, w_sem)


def project(place, x, gain, bias, bqv, sources, blocks):
    rows, width = x.shape
    row_spec = pl.BlockSpec((TILE, width), lambda i, *_: (i, 0))
    return pl.pallas_call(
        functools.partial(qkv_kernel, len(sources)),
        grid_spec=pltpu.PrefetchScalarGridSpec(
            num_scalar_prefetch=1,
            grid=(rows // TILE,),
            in_specs=[
                row_spec,
                once((1, width), lambda i, *_: (0, 0)),
                once((1, width), lambda i, *_: (0, 0)),
                once((2, width), lambda i, *_: (0, 0)),
            ]
            + [ANY_SPEC] * len(sources),
            out_specs=[row_spec] * 4 + [ANY_SPEC],
            scratch_shapes=[
                pltpu.VMEM((blocks, width, sources[0].shape[-1]), BF),
                pltpu.SemaphoreType.DMA((blocks,)),
                pltpu.VMEM((4, width, width), BF),
                pltpu.SemaphoreType.DMA(()),
            ],
        ),
        out_shape=[jax.ShapeDtypeStruct((rows, width), BF)] * 4
        + [jax.ShapeDtypeStruct((4, width, width), BF)],
        compiler_params=params(),
        cost_estimate=cost(6 * rows * width * width, 16 * rows * width),
        name="project",
    )(place, x, gain, bias, bqv, *sources)


def half_masks():
    lane = lax.broadcasted_iota(jnp.int32, (1, PAIR), 1)
    first = (lane < HEAD_DIM).astype(F32)
    return first.astype(BF), (1.0 - first).astype(BF)


def attend_kernel(len_ref, q_ref, k_ref, v_ref, o_ref, lse_ref):
    rows = q_ref.shape[0]
    length = len_ref[0]
    masks = half_masks()
    lane = lax.broadcasted_iota(jnp.int32, (TILE, PAIR), 1)
    k_pos = lax.broadcasted_iota(jnp.int32, (1, rows), 1)
    bias = jnp.where(k_pos < length, 0.0, NEG_BIG)
    tri = lax.broadcasted_iota(jnp.int32, (TILE, TILE), 0) >= lax.broadcasted_iota(
        jnp.int32, (TILE, TILE), 1
    )
    for n in range(0, rows, TILE):
        q_block = q_ref[n : n + TILE, :]
        scores = []
        for mask in masks:
            q_one = q_block * mask
            s_diag = dot_nt(q_one, k_ref[n : n + TILE, :]) + bias[:, n : n + TILE]
            s_diag = jnp.where(tri, s_diag, NEG_BIG)
            s_rest = dot_nt(q_one, k_ref[:n, :]) + bias[:, :n] if n else None
            scores.append((s_diag, s_rest))
        outs = []
        peaks = []
        totals = []
        for s_diag, s_rest in scores:
            peak = jnp.max(s_diag, axis=1, keepdims=True)
            if n:
                peak = jnp.maximum(peak, jnp.max(s_rest, axis=1, keepdims=True))
            e_diag = jnp.exp(s_diag - peak)
            total = jnp.sum(e_diag, axis=1, keepdims=True)
            acc = dot_nn(e_diag.astype(BF), v_ref[n : n + TILE, :])
            if n:
                e_rest = jnp.exp(s_rest - peak)
                total = total + jnp.sum(e_rest, axis=1, keepdims=True)
                acc = acc + dot_nn(e_rest.astype(BF), v_ref[:n, :])
            outs.append(acc)
            peaks.append(peak)
            totals.append(total)
        first = lane < HEAD_DIM
        both = jnp.where(first, outs[0], outs[1])
        o_ref[n : n + TILE, :] = (both / jnp.where(first, totals[0], totals[1])).astype(BF)
        packed = jnp.where(lane < 8, peaks[0], totals[0])
        packed = jnp.where(lane % 8 == 1, jnp.where(lane < 8, peaks[1], totals[1]), packed)
        flipped = jnp.transpose(packed)
        lse_ref[0, :, n : n + TILE] = flipped[:8, :] + jnp.log(flipped[8:16, :])


def attend(lengths, q, k, v):
    rows, width = q.shape
    pairs = width // PAIR
    pair_spec = pl.BlockSpec((rows, PAIR), lambda i, *_: (0, i))
    return pl.pallas_call(
        attend_kernel,
        grid_spec=pltpu.PrefetchScalarGridSpec(
            num_scalar_prefetch=1,
            grid=(pairs,),
            in_specs=[pair_spec] * 3,
            out_specs=[pair_spec, pl.BlockSpec((1, 8, rows), lambda i, *_: (i, 0, 0))],
        ),
        out_shape=[
            jax.ShapeDtypeStruct((rows, width), BF),
            jax.ShapeDtypeStruct((pairs, 8, rows), F32),
        ],
        compiler_params=params(),
        cost_estimate=cost(16e9 * width / 768, 8 * rows * width),
        name="attend",
    )(lengths, q, k, v)


def attend_back_kernel(
    first, n_out, more, len_ref, place_ref, q_ref, k_ref, v_ref, o_ref, do_ref, lse_ref, n_ref,
    out_ref, *refs
):
    refs = refs[n_out:] if more else refs
    dq_ref, dk_ref, dv_ref = refs[:3]
    outs = refs[3 : 3 + n_out]
    dq_acc, side_s, n_s, stage, n_sem, sem = refs[3 + n_out :]
    rows = q_ref.shape[0]
    width = n_ref.shape[1]
    step = pl.program_id(0)
    length = len_ref[0]
    masks = half_masks()
    wide = stage.shape[2]
    narrow = wide != 3 * PAIR

    @pl.when(step == 0)
    def _():
        pltpu.make_async_copy(n_ref, n_s, n_sem).start()

    prod = jnp.transpose(do_ref[...].astype(F32) * o_ref[...].astype(F32))
    tri = lax.broadcasted_iota(jnp.int32, (TILE, TILE), 0) <= lax.broadcasted_iota(
        jnp.int32, (TILE, TILE), 1
    )
    k_pos = lax.broadcasted_iota(jnp.int32, (TILE, 1), 0)
    dq_acc[...] = jnp.zeros_like(dq_acc)
    heads = []
    for h, mask in enumerate(masks):
        heads.append(
            (
                mask,
                q_ref[...] * mask,
                do_ref[...] * mask,
                lse_ref[0, h : h + 1, :],
                jnp.sum(prod[h * HEAD_DIM : (h + 1) * HEAD_DIM, :], axis=0, keepdims=True),
            )
        )
    for n in range(0, rows, TILE):
        k_block = k_ref[n : n + TILE, :]
        v_block = v_ref[n : n + TILE, :]
        bias = jnp.where(k_pos + n < length, 0.0, NEG_BIG)
        dk = jnp.zeros((TILE, PAIR), F32)
        dv = jnp.zeros((TILE, PAIR), F32)
        work = []
        for mask, q_one, do_one, lse, delta in heads:
            for low, high in ((n, n + TILE), (n + TILE, rows)):
                if low == high:
                    continue
                s = dot_nt(k_block, q_one[low:high]) + bias
                dp = dot_nt(v_block, do_one[low:high])
                work.append((mask, q_one, do_one, lse, delta, low, high, s, dp))
        for mask, q_one, do_one, lse, delta, low, high, s, dp in work:
            if low == n:
                s = jnp.where(tri, s, NEG_BIG)
            p = jnp.exp(s - lse[:, low:high])
            ds = (p * (dp - delta[:, low:high])).astype(BF)
            dv = dv + dot_nn(p.astype(BF), do_one[low:high])
            dk = dk + dot_nn(ds, q_one[low:high])
            dq_acc[low:high, :] += dot_tn(ds, k_block * mask)
        dk_ref[n : n + TILE, :] = dk.astype(BF)
        dv_ref[n : n + TILE, :] = dv.astype(BF)
    dq_ref[...] = (dq_acc[...] * (HEAD_DIM ** (-0.5))).astype(BF)

    grads = [dq_ref[...], dk_ref[...], dv_ref[...]]
    if narrow:
        blank = jnp.zeros((rows, HEAD_DIM), BF)
        sides = [
            jnp.concatenate([g[:, c : c + HEAD_DIM] for g in grads] + [blank], axis=1)
            for c in (0, HEAD_DIM)
        ]
    else:
        sides = [jnp.concatenate(grads, axis=1)]
    pairs = side_s.shape[1] // (wide * len(sides))
    for at in range(pairs):

        @pl.when(step == at)
        def _(at=at):
            for i, side in enumerate(sides):
                spot = at * len(sides) + i
                side_s[:, spot * wide : (spot + 1) * wide] = side

    @pl.when(step == pairs - 1)
    def _():
        pltpu.make_async_copy(n_ref, n_s, n_sem).wait()
        low_col = 3 * PAIR if narrow else 0
        columns = slice(low_col, low_col + wide)
        for part in range(2):
            cols = slice(part * width // 2, (part + 1) * width // 2)
            grad = dot_tn(n_s[:, cols], side_s[...]).astype(BF)
            for spot in range(stage.shape[0]):
                t = spot if narrow else first + spot
                begin = spot * wide
                if narrow:
                    stage[spot, cols, :PAIR] = grad[:, begin : begin + PAIR]
                    extra = out_ref[cols, spot * HEAD_DIM : (spot + 1) * HEAD_DIM]
                    stage[spot, cols, PAIR:] = jnp.concatenate(
                        [grad[:, begin + PAIR : begin + PAIR + HEAD_DIM], extra], axis=1
                    )
                else:
                    stage[spot, cols, :] = grad[:, begin : begin + wide]
                send_rows(place_ref, stage.at[spot], outs, sem, t, columns, part)
        wait_all(stage, sem)


def attend_back(
    place, lengths, first, pairs, wide, q, k, v, out, d_out, lse, normed, last_out, blocks,
    so_far, fast,
):
    rows, width = q.shape
    at_pair = pl.BlockSpec((rows, PAIR), lambda i, *_: (0, first + i))
    own_pair = pl.BlockSpec((rows, PAIR), lambda i, *_: (0, i))
    grads = grad_shapes(fast, blocks, width, 5 * PAIR)
    so_far = so_far or []
    sides = 1 if wide == 3 * PAIR else 2
    return pl.pallas_call(
        functools.partial(attend_back_kernel, first, len(grads), bool(so_far)),
        grid_spec=pltpu.PrefetchScalarGridSpec(
            num_scalar_prefetch=2,
            grid=(pairs,),
            in_specs=[at_pair] * 5
            + [
                pl.BlockSpec((1, 8, rows), lambda i, *_: (first + i, 0, 0)),
                ANY_SPEC,
                once(last_out.shape, lambda i, *_: (0, 0)),
            ]
            + [ANY_SPEC] * len(so_far),
            out_specs=[own_pair] * 3 + [ANY_SPEC] * len(grads),
            scratch_shapes=[
                pltpu.VMEM((rows, PAIR), F32),
                pltpu.VMEM((rows, pairs * sides * wide), BF),
                pltpu.VMEM((rows, width), BF),
                pltpu.VMEM((pairs * sides, width, wide), BF),
                pltpu.SemaphoreType.DMA(()),
                pltpu.SemaphoreType.DMA(()),
            ],
        ),
        out_shape=[jax.ShapeDtypeStruct((rows, pairs * PAIR), BF)] * 3 + grads,
        input_output_aliases={10 + i: 3 + i for i in range(len(so_far))},
        compiler_params=params(),
        cost_estimate=cost(3e9 * pairs, 5e6 * pairs),
        name="attend_back",
    )(lengths, place, q, k, v, out, d_out, lse, normed, last_out, *so_far)


def vec_rows(vec_ref):
    return lambda i: vec_ref[i : i + 1, :]


def tile_rows(i):
    return pl.ds(pl.multiple_of(i * TILE, TILE), TILE)


def grad_shapes(fast, blocks, width, wide):
    if fast:
        return [jax.ShapeDtypeStruct((16, width // 8, wide), BF)] * 2
    return [jax.ShapeDtypeStruct((blocks, width, wide), BF)]


def feed_kernel(
    counts, place_ref, att_ref, x_ref, cot_ref, wo_ref, vec_ref, bup_ref, *refs
):
    one, two = counts
    refs, sources = refs[one + two :], (refs[:one], refs[one : one + two])
    resid_out, act_ref, gbup_ref, dres_out, datt_out, sums_ref, last_out_ref = refs[:7]
    refs = refs[7:]
    n_out = (len(refs) - 13) // 2
    up_outs, down_outs = refs[:n_out], refs[n_out : 2 * n_out]
    raw, sems, n_two, d_pre_s, d_norm, low, stage, stage_down, sem = refs[2 * n_out : -4]
    resid_ref, dres_ref, datt_ref, out_sems = refs[-4:]
    rows, width = x_ref.shape
    step = pl.program_id(0)
    tiles = rows // TILE
    blocks = stage.shape[0]
    vec = vec_rows(vec_ref)
    half_width = width // 2
    cut = sources[0][0].shape[-1] // 2

    @pl.when(step == 0)
    def _():
        begin = 0
        sizes, orders = (cut, width - cut), ("ring", "last")
        for source, size, order in zip(sources, sizes, orders, strict=True):
            for to in (begin, width + begin):
                start_blocks(
                    place_ref,
                    source,
                    slice(0 if to < width else size, size if to < width else 2 * size),
                    raw,
                    slice(to, to + size),
                    sems,
                    order,
                )
            begin += size

        def body(i, _):
            r = tile_rows(i)
            res = x_ref[r, :].astype(F32) + dot_nt(att_ref[r, :], wo_ref[0]) + vec(0)
            resid_ref[r, :] = res
            normed, _ = norm_parts(res)
            n_two[r, :] = (normed * vec(1) + vec(2)).astype(BF)
            d_norm[r, :] = jnp.zeros((TILE, width), F32)
            return 0

        lax.fori_loop(0, tiles, body, 0)
        pltpu.make_async_copy(resid_ref, resid_out, out_sems.at[0]).start()

    wait_all(raw.at[step], sems.at[step])
    w_up = raw[step, :, :width]
    w_down = raw[step, :, width:]
    c_one = 0.7978845608028654
    c_two = 0.044715

    def body(i, total):
        r = tile_rows(i)
        u = dot_nn(n_two[r, :], w_up) + bup_ref[0]
        d_act = dot_nn(cot_ref[r, :], w_down)
        square = u * u
        t = jnp.tanh(c_one * u * (1.0 + c_two * square))
        half = 0.5 * (1.0 + t)
        act_ref[r, :] = (u * half).astype(BF)
        slope = half + 0.5 * u * (1.0 - t * t) * (c_one * (1.0 + 3.0 * c_two * square))
        d_pre = (d_act * slope).astype(BF)
        d_pre_s[r, :] = d_pre
        d_norm[r, :] += dot_nt(d_pre, w_up)
        return total + col_sum(d_pre.astype(F32))

    gbup_ref[0] = lax.fori_loop(0, tiles, body, jnp.zeros((1, width), F32), unroll=True)
    def grads(i, _):
        cols = tile_rows(i)
        stage[step, cols, :width] = dot_tn(n_two[:, cols], d_pre_s[...]).astype(BF)
        stage_down[step, cols, :] = dot_tn(cot_ref[:, cols], act_ref[...]).astype(BF)
        return 0

    lax.fori_loop(0, width // TILE, grads, 0)
    first_cols = slice(0, width)
    for t in range(blocks):

        @pl.when(step == t)
        def _(t=t):
            send_rows(place_ref, stage.at[t, :, first_cols], up_outs, sem, t, first_cols)
            send_rows(place_ref, stage_down.at[t], down_outs, sem, t, first_cols)

    @pl.when(step == pl.num_programs(0) - 1)
    def _():
        def body(i, sums):
            r = tile_rows(i)
            normed, scale = norm_parts(resid_ref[r, :])
            d_n = d_norm[r, :]
            d_out = cot_ref[r, :].astype(F32)
            d_res = d_out + norm_back(d_n * vec(1), normed, scale)
            dres_ref[r, :] = d_res
            d_low = d_res.astype(BF)
            low[r, :] = d_low
            datt_ref[r, :] = dot_nn(d_low, wo_ref[0]).astype(BF)
            pltpu.make_async_copy(dres_ref.at[r, :], dres_out.at[r, :], out_sems.at[1]).start()
            pltpu.make_async_copy(datt_ref.at[r, :], datt_out.at[r, :], out_sems.at[2]).start()
            more = (col_sum(d_n * normed), col_sum(d_n), col_sum(d_res), col_sum(d_out))
            return tuple(a + b for a, b in zip(sums, more, strict=True))

        sums = lax.fori_loop(0, tiles, body, (jnp.zeros((1, width), F32),) * 4)
        sums_ref[...] = jnp.zeros_like(sums_ref)
        for i in range(4):
            sums_ref[i : i + 1, :] = sums[i]
        side = width
        for c in range(0, width, half_width):
            rows_c = slice(c, c + half_width)
            go = dot_tn(low[:, rows_c], att_ref[...]).astype(BF)
            last_out_ref[rows_c, :] = go[:, blocks * PAIR :]
            for t in range(blocks):
                stage[t, rows_c, side:] = go[:, t * PAIR : (t + 1) * PAIR]
        cols = slice(side, side + PAIR)
        for t in range(blocks):
            send_rows(place_ref, stage.at[t, :, cols], up_outs, sem, t, cols)
        wait_all(stage, sem)
        wait_all(stage_down, sem)
        for i, ref in enumerate((resid_ref, dres_ref, datt_ref)):
            wait_all(ref, out_sems.at[i])


def feed_forward(place, att, x, cot, w_all, vecs, b_up, sources_one, sources_two, fast):
    rows, width = x.shape
    blocks = b_up.shape[0]
    whole = once((rows, width), lambda t, *_: (0, 0))
    up_vec = pl.BlockSpec((1, 1, width), lambda t, *_: (t, 0, 0))
    grads = grad_shapes(fast, blocks, width, width + PAIR)
    grads += grad_shapes(fast, blocks, width, width)
    counts = (len(sources_one), len(sources_two))
    return pl.pallas_call(
        functools.partial(feed_kernel, counts),
        grid_spec=pltpu.PrefetchScalarGridSpec(
            num_scalar_prefetch=1,
            grid=(blocks,),
            in_specs=[
                whole,
                whole,
                whole,
                once((1, width, width), lambda t, *_: (3, 0, 0)),
                once((8, width), lambda t, *_: (0, 0)),
                up_vec,
            ]
            + [ANY_SPEC] * sum(counts),
            out_specs=[
                ANY_SPEC,
                pl.BlockSpec((rows, width), lambda t, *_: (0, t)),
                up_vec,
                ANY_SPEC,
                ANY_SPEC,
                once((8, width), lambda t, *_: (0, 0)),
                once((width, width - blocks * PAIR), lambda t, *_: (0, 0)),
            ]
            + [ANY_SPEC] * len(grads),
            scratch_shapes=[
                pltpu.VMEM((blocks, width, 2 * width), BF),
                pltpu.SemaphoreType.DMA((blocks,)),
                pltpu.VMEM((rows, width), BF),
                pltpu.VMEM((rows, width), BF),
                pltpu.VMEM((rows, width), F32),
                pltpu.VMEM((rows, width), BF),
                pltpu.VMEM((blocks, width, width + PAIR), BF),
                pltpu.VMEM((blocks, width, width), BF),
                pltpu.SemaphoreType.DMA(()),
                pltpu.VMEM((rows, width), F32),
                pltpu.VMEM((rows, width), F32),
                pltpu.VMEM((rows, width), BF),
                pltpu.SemaphoreType.DMA((3,)),
            ],
        ),
        out_shape=[
            jax.ShapeDtypeStruct((rows, width), F32),
            jax.ShapeDtypeStruct((rows, blocks * width), BF),
            jax.ShapeDtypeStruct((blocks, 1, width), F32),
            jax.ShapeDtypeStruct((rows, width), F32),
            jax.ShapeDtypeStruct((rows, width), BF),
            jax.ShapeDtypeStruct((8, width), F32),
            jax.ShapeDtypeStruct((width, width - blocks * PAIR), BF),
        ]
        + grads,
        compiler_params=params(),
        cost_estimate=cost(40e9, 40e6),
        name="feed_forward",
    )(place, att, x, cot, w_all, vecs, b_up, *sources_one, *sources_two)


def hidden_kernel(counts, place_ref, act_ref, resid_ref, vec_ref, *refs):
    one, two = counts
    refs, sources = refs[one + two :], (refs[:one], refs[one : one + two])
    out_ref, raw, sems = refs
    blocks, _, width = raw.shape
    cut = sources[0][0].shape[-1] // 2

    @pl.when(pl.program_id(0) == 0)
    def _():
        begin = 0
        sizes, orders = (cut, width - cut), ("ring", "last")
        for source, size, order in zip(sources, sizes, orders, strict=True):
            to = slice(begin, begin + size)
            start_blocks(place_ref, source, slice(size, 2 * size), raw, to, sems, order)
            begin += size
        for t in range(blocks):
            wait_all(raw.at[t], sems.at[t])

    acc = resid_ref[...] + vec_ref[3:4, :]
    for t in range(blocks):
        acc = acc + dot_nt(act_ref[:, t * width : (t + 1) * width], raw[t])
    out_ref[...] = acc.astype(BF)


def hidden_rows(place, act, resid, vecs, sources_one, sources_two):
    rows, width = resid.shape
    blocks = act.shape[1] // width
    row_spec = pl.BlockSpec((TILE, width), lambda i, *_: (i, 0))
    counts = (len(sources_one), len(sources_two))
    return pl.pallas_call(
        functools.partial(hidden_kernel, counts),
        grid_spec=pltpu.PrefetchScalarGridSpec(
            num_scalar_prefetch=1,
            grid=(rows // TILE,),
            in_specs=[
                pl.BlockSpec((TILE, blocks * width), lambda i, *_: (i, 0)),
                row_spec,
                once((8, width), lambda i, *_: (0, 0)),
            ]
            + [ANY_SPEC] * sum(counts),
            out_specs=row_spec,
            scratch_shapes=[
                pltpu.VMEM((blocks, width, width), BF),
                pltpu.SemaphoreType.DMA((blocks,)),
            ],
        ),
        out_shape=jax.ShapeDtypeStruct((rows, width), BF),
        compiler_params=params(),
        cost_estimate=cost(5e9, 12e6),
        name="hidden_rows",
    )(place, act, resid, vecs, *sources_one, *sources_two)


def input_kernel(*refs):
    parts = refs[:6]
    w_ref, x_ref, dres_ref, gain_ref, gin_ref, sums_ref = refs[6:]

    @pl.when(pl.program_id(0) == 0)
    def _():
        sums_ref[...] = jnp.zeros_like(sums_ref)

    dq, dk, dv = (jnp.concatenate([part[...] for part in parts[i::3]], axis=1) for i in range(3))
    d_norm = dot_nt(dq, w_ref[0]) + dot_nt(dk, w_ref[1]) + dot_nt(dv, w_ref[2])
    normed, scale = norm_parts(x_ref[...].astype(F32))
    gin_ref[...] = dres_ref[...] + norm_back(d_norm * gain_ref[...], normed, scale)
    more = (
        col_sum(d_norm * normed),
        col_sum(d_norm),
        col_sum(dq.astype(F32)),
        col_sum(dv.astype(F32)),
    )
    for i, value in enumerate(more):
        sums_ref[i : i + 1, :] += value


def input_grad(parts, w_all, x, d_resid, gain):
    rows, width = x.shape
    row_spec = pl.BlockSpec((TILE, width), lambda i: (i, 0))
    return pl.pallas_call(
        input_kernel,
        grid=(rows // TILE,),
        in_specs=[pl.BlockSpec((TILE, part.shape[1]), lambda i: (i, 0)) for part in parts]
        + [
            once((3, width, width), lambda i: (0, 0, 0)),
            row_spec,
            row_spec,
            once((1, width), lambda i: (0, 0)),
        ],
        out_specs=[row_spec, pl.BlockSpec((8, width), lambda i: (0, 0))],
        out_shape=[
            jax.ShapeDtypeStruct((rows, width), F32),
            jax.ShapeDtypeStruct((8, width), F32),
        ],
        compiler_params=params(),
        cost_estimate=cost(6 * rows * width * width, 16 * rows * width),
        name="input_grad",
    )(*parts, w_all, x, d_resid, gain)


def body(
    n_dp,
    n_tensor,
    hidden_in,
    cotangent,
    lengths,
    latent,
    ln1_gain,
    ln1_bias,
    w_qkv,
    b_qv,
    w_out,
    b_out,
    ln2_gain,
    ln2_bias,
    w_up,
    b_up,
    w_down,
    b_down,
):
    rows, width = hidden_in.shape
    t_index = lax.axis_index("tensor")
    block = w_up.shape[0]
    heads = w_qkv.shape[2] // HEAD_DIM

    out_t = w_out.T
    packed = jnp.concatenate(
        [w_qkv[0, :, :PAIR], w_qkv[1, :, :PAIR], w_qkv[2, :, :PAIR], out_t[:, :PAIR]]
        + [w_qkv[0, :, PAIR:], w_qkv[1, :, PAIR:], w_qkv[2, :, PAIR:], out_t[:, PAIR:]],
        axis=1,
    ).astype(BF)
    packed, up_part, down_part = after(packed, w_up, w_down)
    down_t = down_part.T
    cut = w_up.shape[1] * 2 // 3
    packed_one = jnp.concatenate([up_part[:, :cut], down_t[:, :cut]], axis=1).astype(BF)
    packed_two = jnp.concatenate([up_part[:, cut:], down_t[:, cut:]], axis=1).astype(BF)

    fast = n_dp == 8 and n_tensor == 4
    d_index = lax.axis_index("dp")
    place = jnp.stack([d_index >> 1, d_index & 1, t_index >> 1, t_index & 1]).astype(jnp.int32)

    def gather(piece):
        wide = piece.shape[1]
        full = lax.all_gather(piece, BOTH, axis=0, tiled=False)
        full = full.reshape(n_dp, n_tensor, block, wide)
        if fast:
            return full
        return full.transpose(1, 0, 2, 3).reshape(1, n_tensor, width, wide)

    project_place = place
    def to_inner(b):
        split = b.reshape(b.shape[0], n_tensor, heads, HEAD_DIM)
        return jnp.concatenate(
            [split[:, :, :2].reshape(b.shape[0], -1), split[:, :, 2:].reshape(b.shape[0], -1)],
            axis=1,
        )

    raw = [cotangent, lengths, latent, b_qv, ln1_gain, ln1_bias, b_out, ln2_gain, ln2_bias, b_down, b_up]

    def small_operands(
        cotangent, lengths, latent, b_qv, ln1_gain, ln1_bias, b_out, ln2_gain, ln2_bias, b_down, b_up
    ):
        own_length = lax.dynamic_slice_in_dim(lengths, t_index, 1, 0)
        own_latent = lax.dynamic_slice_in_dim(latent, t_index, 1, 0)
        positions = lax.broadcasted_iota(jnp.int32, (1, rows), 1)
        keep = ((positions < own_length) & (own_latent == 0)).astype(BF).reshape(rows, 1)
        cot = cotangent * keep
        zero = jnp.zeros_like(b_out)
        return [
            cot,
            place,
            own_length,
            to_inner(b_qv),
            ln1_gain[None],
            ln1_bias[None],
            jnp.stack([b_out, ln2_gain, ln2_bias, b_down, zero, zero, zero, zero]),
            b_up.reshape(n_tensor, 1, width),
        ]
    if fast:
        def grow(array, came):
            return jnp.concatenate([array, came])

        att, one, two = packed[None], packed_one[None], packed_two[None]
        att_came, two, one, *raw = after(exchange(att, flip_near), two, one, *raw)
        early = small_operands(*raw)
        att = grow(att, att_came)
        two = grow(two, exchange(two, flip_first))
        att_came, two_came, one_one, *early = after(
            exchange(att, flip_far), exchange(two, flip_second), exchange(one, flip_ring), *early
        )
        att, two = grow(att, att_came), grow(two, two_came)
        att_first, att_second, one_two, two_one = after(
            exchange(att, flip_first),
            exchange(att, flip_second),
            exchange(one_one, flip_ring),
            exchange(two, flip_ring),
        )
        halves = [att, att_first, att_second]
        att_both, one_last, *cores = after(
            exchange(att_first, flip_second),
            exchange(one_two, flip_ring),
            *(exchange(half, flip_core) for half in halves),
        )
        sources = [*halves, att_both, *cores, exchange(att_both, flip_core)]
        one = jnp.concatenate([one, one_one, one_two, one_last])
        one_first, two_two = exchange(one, flip_first), exchange(two_one, flip_ring)
    else:
        early = small_operands(*raw)
        sources = [gather(packed)]
        sources_one, sources_two = [gather(packed_one)], [gather(packed_two)]

    def from_inner(b):
        cut = n_tensor * PAIR
        first = b[:, :cut].reshape(b.shape[0], n_tensor, 2, HEAD_DIM)
        rest = b[:, cut:].reshape(b.shape[0], n_tensor, heads - 2, HEAD_DIM)
        return jnp.concatenate([first, rest], axis=2).reshape(b.shape[0], width)

    cot, place, own_length, inner_bqv, gain, bias, vecs, up_bias = early
    q, k, v, normed_one, w_all = project(
        place, hidden_in, gain, bias, inner_bqv, sources, n_tensor
    )
    if fast:
        one_first, two_two, q = after(one_first, two_two, q)
        halves = [one, one_first, two, two_one, two_two]
        cores = [exchange(half, flip_core) for half in halves]
        came = [exchange(half, flip_second) for half in halves[:2]]
        came.append(exchange(two_two, flip_ring))
    attended, lse = attend(own_length, q, k, v)
    if fast:
        attended, *moved = after(attended, *came, *cores)
        came, cores = moved[:3], moved[3:]
        cores += [exchange(half, flip_core) for half in came]
        sources_one = [*halves[:2], *came[:2], *cores[:2], *cores[5:7]]
        sources_two = [*halves[2:], came[2], *cores[2:5], cores[7]]
    resid, act, g_b_up, d_resid, d_attended, sums_two, last_out, *g_mlp = feed_forward(
        place, attended, hidden_in, cot, w_all, vecs, up_bias, sources_one, sources_two, fast
    )

    half = len(g_mlp) // 2

    def back(length, first, pairs, wide, so_far):
        return list(
            attend_back(
                place, length, first, pairs, wide, q, k, v, attended, d_attended, lse,
                normed_one, last_out, n_tensor, so_far, fast,
            )
        )

    def vectors(sums_one):
        return jnp.concatenate([sums_one[:4], sums_two[:4], g_b_up.reshape(n_tensor, width)])

    if fast:
        up, down = Scatter(*g_mlp[:half]), Scatter(*g_mlp[half:])
        came_up, came_down = up.step(), down.step()
        hidden_out = hidden_rows(place, act, resid, vecs, sources_one, sources_two)
        came_up, came_down, length, hidden_out = after(
            came_up, came_down, own_length, hidden_out
        )
        up.sent, down.sent = sums(up.want(came_up), down.want(came_down))
        came_up, came_down = up.step(), down.step()
        back_one = back(length, 0, 4, 3 * PAIR, None)
        came_up, length, *back_one = after(came_up, own_length, *back_one)
        (up.sent,) = sums(up.want(came_up))
        came_up = up.step()
        back_two = back(length, 4, 2, 2 * PAIR, back_one[3:])
        came_up, came_down, gain, *back_two = after(came_up, came_down, gain, *back_two)
        rest = Scatter(*back_two[3:])
        came_rest = rest.step()
        up.sent, down.sent = sums(up.want(came_up), down.want(came_down))
        came_rest, up.sent, down.sent = after(came_rest, up.sent, down.sent)
        came_up, came_down = up.step(), down.step()
        (rest.sent,) = sums(rest.want(came_rest))
        came_rest = rest.step()
        parts = [*back_one[:3], *back_two[:3]]
        grad_in, sums_one = input_grad(parts, w_all, hidden_in, d_resid, gain)
        came_rest, came_down, sums_one, grad_in = after(came_rest, came_down, sums_one, grad_in)
        rest.sent, down.sent = sums(rest.want(came_rest), down.want(came_down))
        came_up, rest.sent, down.sent = after(came_up, rest.sent, down.sent)
        came_rest, came_down = rest.step(), down.step()
        (up.sent,) = plain_sums(up.want(came_up))
        came_up = up.step()
        small = vectors(sums_one)
        small = small + exchange(small, flip_core)
        came_small = exchange(small, flip_second)
        small = small + came_small
        came_small = exchange(small, flip_first)
        came_rest, came_down, came_small = after(came_rest, came_down, came_small)
        (rest.sent,) = plain_sums(rest.want(came_rest))
        small = small + came_small
        rest.sent, came_down = after(rest.sent, came_down)
        came_rest, came_small = rest.step(), exchange(small, flip_far)
        (down.sent,) = plain_sums(down.want(came_down))
        came_down = down.step()
        came_rest, came_small, came_up, came_down = after(
            came_rest, came_small, came_up, came_down
        )
        (rest.sent,) = plain_sums(rest.want(came_rest))
        small = small + came_small
        came_rest, came_small = rest.step(), exchange(small, flip_near)
        small = small + came_small
        g_up, g_out, g_down, g_qkv = last_sums(
            [*up.terms, came_up], [*down.terms, came_down], [*rest.terms, came_rest]
        )
    else:
        back_one = back(own_length, 0, 4, 3 * PAIR, None)
        back_two = back(own_length, 4, 2, 2 * PAIR, back_one[3:])
        parts = [*back_one[:3], *back_two[:3]]
        grad_in, sums_one = input_grad(parts, w_all, hidden_in, d_resid, gain)
        hidden_out = hidden_rows(place, act, resid, vecs, sources_one, sources_two)
        small = lax.psum(vectors(sums_one), BOTH)

        def scatter_all(grads):
            wide = grads.shape[-1]
            grads = grads.reshape(n_tensor, n_dp, block, wide).transpose(1, 0, 2, 3)
            flat = grads.reshape(n_dp * n_tensor * block, wide)
            total = lax.psum_scatter(flat, BOTH, scatter_dimension=0, tiled=True)
            return total.astype(F32)

        g_up, g_down, g_rest = (scatter_all(g) for g in (*g_mlp, back_two[3]))
        g_out, g_qkv = split_columns(g_up, g_rest)
        g_out = g_out.T
        g_up = g_up[:, :width]
    g_bqv = from_inner(small[2:4])

    return (
        hidden_out,
        grad_in,
        small[0],
        small[1],
        g_qkv,
        g_bqv,
        g_out,
        small[6],
        small[4],
        small[5],
        g_up,
        small[8:].reshape(-1),
        g_down.T,
        small[7],
    )


def solution(mesh):
    placed = (
        P(BOTH, None),
        P(BOTH, None),
        P("dp"),
        P("dp", None),
        P(),
        P(),
        P(None, "dp", "tensor"),
        P(),
        P("tensor", "dp"),
        P(),
        P(),
        P(),
        P("dp", "tensor"),
        P(),
        P("tensor", "dp"),
        P(),
    )
    return jax.shard_map(
        functools.partial(body, mesh.shape["dp"], mesh.shape["tensor"]),
        mesh=mesh,
        in_specs=placed,
        out_specs=(
            P(BOTH, None),
            P(BOTH, None),
            P(),
            P(),
            P(None, "dp", "tensor"),
            P(),
            P("tensor", "dp"),
            P(),
            P(),
            P(),
            P("dp", "tensor"),
            P(),
            P("tensor", "dp"),
            P(),
        ),
        check_vma=False,
    )
```

```python
import functools

import jax
import jax.numpy as jnp
from jax import lax
from jax.experimental import pallas as pl
from jax.experimental.pallas import tpu as pltpu
from jax.sharding import PartitionSpec as P

HEAD_DIM = 64
LEN = 1024
PAIR = 2 * HEAD_DIM
TILE = 256
NEG_BIG = -1e30
EPSILON = 1e-05
VMEM_BYTES = 66_900_000
BF = jnp.bfloat16
F32 = jnp.float32
BOTH = ("dp", "tensor")
ANY_SPEC = pl.BlockSpec(memory_space=pl.ANY)


def dot_nn(a, b):
    return lax.dot_general(a, b, (((1,), (0,)), ((), ())), preferred_element_type=F32)


def dot_nt(a, b):
    return lax.dot_general(a, b, (((1,), (1,)), ((), ())), preferred_element_type=F32)


def dot_tn(a, b):
    return lax.dot_general(a, b, (((0,), (0,)), ((), ())), preferred_element_type=F32)


def norm_parts(rows_in):
    center = rows_in - jnp.mean(rows_in, axis=-1, keepdims=True)
    spread = jnp.mean(center * center, axis=-1, keepdims=True)
    scale = lax.rsqrt(spread + EPSILON)
    return center * scale, scale


def norm_back(gy, normed, scale):
    mean_gy = jnp.mean(gy, axis=-1, keepdims=True)
    mean_gyn = jnp.mean(gy * normed, axis=-1, keepdims=True)
    return (gy - mean_gy - normed * mean_gyn) * scale


def col_sum(values):
    return jnp.sum(values, axis=0, keepdims=True)


def once(shape, index):
    return pl.BlockSpec(shape, index, pipeline_mode=pl.Buffered(1))


def params(side_effects=False):
    return pltpu.CompilerParams(
        dimension_semantics=("arbitrary",),
        vmem_limit_bytes=VMEM_BYTES,
        has_side_effects=side_effects,
    )


def cost(flops, moved, exps=0):
    return pl.CostEstimate(flops=int(flops), bytes_accessed=int(moved), transcendentals=int(exps))


def place_of(index):
    return (index >> 3) & 3, (index >> 2) & 1, (index >> 1) & 1, index & 1


def index_of(z, x, y, core):
    return (z << 3) | (x << 2) | (y << 1) | core


def exchange(array, flip):
    pairs = [(i, index_of(*flip(*place_of(i)))) for i in range(32)]
    return lax.ppermute(array, BOTH, pairs)


def flip_first(z, x, y, core):
    return (z, x, y ^ 1, core) if core else (z, x ^ 1, y, core)


def flip_second(z, x, y, core):
    return (z, x ^ 1, y, core) if core else (z, x, y ^ 1, core)


def flip_core(z, x, y, core):
    return z, x, y, core ^ 1


def flip_near(z, x, y, core):
    return z ^ 1, x, y, core


def flip_far(z, x, y, core):
    return z ^ 2, x, y, core


def sums_kernel(plan, *refs):
    count_in = sum(len(offsets) for offsets, _ in plan)
    outs = refs[count_in : count_in + len(plan)]
    scratch = refs[count_in + len(plan) :]
    position = 0
    for i, (offsets, count) in enumerate(plan):
        terms, _, sems, _ = scratch[4 * i : 4 * i + 4]
        for slot in range(count):
            for k, offset in enumerate(offsets):
                pltpu.make_async_copy(
                    refs[position + k].at[offset + slot], terms.at[slot, k], sems.at[slot]
                ).start()
        position += len(offsets)
    for i, (offsets, count) in enumerate(plan):
        terms, result, sems, out_sem = scratch[4 * i : 4 * i + 4]

        def body(slot, _, i=i, size=len(offsets)):
            terms, result, sems, out_sem = scratch[4 * i : 4 * i + 4]
            wait_all(terms.at[slot], sems.at[slot])
            total = terms[slot, 0].astype(F32)
            for k in range(1, size):
                total = total + terms[slot, k].astype(F32)
            result[slot] = total.astype(BF)
            pltpu.make_async_copy(result.at[slot], outs[i].at[slot], out_sem).start()
            return 0

        lax.fori_loop(0, count, body, 0)
    for i in range(len(plan)):
        wait_all(scratch[4 * i + 1], scratch[4 * i + 3])


def sums(*requests):
    plan, arrays, shapes, scratch = [], [], [], []
    for terms, count in requests:
        block = terms[0][0].shape[1:]
        plan.append((tuple(offset for _, offset in terms), count))
        arrays += [array for array, _ in terms]
        shapes.append(jax.ShapeDtypeStruct((count, *block), BF))
        scratch += [
            pltpu.VMEM((count, len(terms), *block), BF),
            pltpu.VMEM((count, *block), BF),
            pltpu.SemaphoreType.DMA((count,)),
            pltpu.SemaphoreType.DMA(()),
        ]
    return pl.pallas_call(
        functools.partial(sums_kernel, plan),
        in_specs=[ANY_SPEC] * len(arrays),
        out_specs=[ANY_SPEC] * len(shapes),
        out_shape=shapes,
        scratch_shapes=scratch,
        compiler_params=pltpu.CompilerParams(vmem_limit_bytes=VMEM_BYTES),
        cost_estimate=cost(1e6, 8e6),
        name="sums",
    )(*arrays)


def plain_sums(*requests):
    results = []
    for terms, count in requests:
        total = None
        for array, offset in terms:
            part = array[offset : offset + count].astype(F32)
            total = part if total is None else total + part
        results.append(total.astype(BF))
    return results


def split_columns(up, rest):
    width = up.shape[1] - PAIR
    side = 3 * PAIR
    out = jnp.concatenate([up[:, width:], rest[:, side + 3 * HEAD_DIM :]], axis=1)
    three = []
    for i in range(3):
        begin = side + i * HEAD_DIM
        parts = [rest[:, i * PAIR : (i + 1) * PAIR], rest[:, begin : begin + HEAD_DIM]]
        three.append(jnp.concatenate(parts, axis=1))
    return out, jnp.stack(three)


def last_kernel(counts, *refs):
    sources, rest_of = refs[: sum(counts)], refs[sum(counts) :]
    up_ref, out_ref, down_ref, qkv_ref = rest_of[:4]
    scratch, sems = rest_of[4:7], rest_of[7]
    position = 0
    for i, count in enumerate(counts):
        for k in range(count):
            pltpu.make_async_copy(
                sources[position + k].at[0], scratch[i].at[k], sems.at[i]
            ).start()
        position += count
    totals = []
    for i, count in enumerate(counts):
        wait_all(scratch[i], sems.at[i])
        total = scratch[i][0].astype(F32)
        for k in range(1, count):
            total = total + scratch[i][k].astype(F32)
        totals.append(total)
    up, down, rest = totals
    up_ref[...] = up[:, : up_ref.shape[1]]
    down_ref[...] = down
    out, qkv_ref[...] = split_columns(up, rest)
    out_ref[...] = jnp.transpose(out)


def last_sums(*chains):
    counts = [len(terms) for terms in chains]
    block = chains[0][0].shape[1]
    width, third = chains[1][0].shape[2], 3 * HEAD_DIM
    whole = pl.BlockSpec(memory_space=pltpu.VMEM)
    return pl.pallas_call(
        functools.partial(last_kernel, counts),
        in_specs=[ANY_SPEC] * sum(counts),
        out_specs=[whole] * 4,
        out_shape=[
            jax.ShapeDtypeStruct((block, width), F32),
            jax.ShapeDtypeStruct((third, block), F32),
            jax.ShapeDtypeStruct((block, width), F32),
            jax.ShapeDtypeStruct((3, block, third), F32),
        ],
        scratch_shapes=[
            pltpu.VMEM((len(terms), block, terms[0].shape[2]), BF) for terms in chains
        ]
        + [pltpu.SemaphoreType.DMA((3,))],
        compiler_params=pltpu.CompilerParams(vmem_limit_bytes=VMEM_BYTES),
        cost_estimate=cost(1e6, 4e6),
        name="last_sums",
    )(*(term for terms in chains for term in terms))


class Scatter:
    def __init__(self, kept, sent):
        self.terms, self.sent = [kept], sent
        self.flips = [flip_core, flip_second, flip_first, flip_far, flip_near]

    def step(self):
        return exchange(self.sent, self.flips.pop(0))

    def want(self, came):
        self.terms = [*self.terms, came]
        count = came.shape[0] // 2
        return [(array, count) for array in self.terms], count


def after(value, *others):
    return lax.optimization_barrier((value, *others))


def ring_place(z):
    z = z & 3
    return z ^ (z >> 1)


def flip_ring(z, x, y, core):
    return ring_place(ring_place(z) + 1), x, y, core


def start_blocks(place_ref, sources, cols, raw, to, sems, order="xor"):
    if len(sources) == 1:
        nd, blocks, block, _ = sources[0].shape
        for d in range(nd):
            for t in range(blocks):
                pltpu.make_async_copy(
                    sources[0].at[d, t, :, cols],
                    raw.at[t, d * block : (d + 1) * block, to],
                    sems.at[t],
                ).start()
        return
    z, x, y, core = (place_ref[i] for i in range(4))
    block = sources[0].shape[1]
    for i, source in enumerate(sources):
        for slot in range(4):
            to_core = core ^ (i >> 2)
            pair, step = (slot, i & 3) if order == "last" else (i & 3, slot)
            second, first = pair >> 1, pair & 1
            to_x = x ^ (first + to_core * (second - first))
            to_y = y ^ (second + to_core * (first - second))
            to_z = z ^ step if order == "xor" else ring_place(ring_place(z) - step)
            to_t = to_y * 2 + to_core
            low = pl.multiple_of((to_z * 2 + to_x) * block, block)
            pltpu.make_async_copy(
                source.at[slot, :, cols], raw.at[to_t, pl.ds(low, block), to], sems.at[to_t]
            ).start()


def wait_all(ref, sem):
    pltpu.make_async_copy(ref, ref, sem).wait()


def send_block(place_ref, staged, outs, sem, d, t, ring):
    z, x, y, core = (place_ref[i] for i in range(4))
    far, near_core = d >> 1, t & 1
    x_off, y_off = x ^ (d & 1), y ^ (t >> 1)
    first, second = (y_off, x_off) if near_core else (x_off, y_off)
    along = (ring_place(far) - ring_place(z)) & 3 if ring else z ^ far
    slot = second * 8 + first * 4 + along
    for side in range(2):

        @pl.when((core ^ near_core) == side)
        def _(side=side):
            pltpu.make_async_copy(staged, outs[side].at[slot], sem).start()


def send_rows(place_ref, stage, outs, sem, t, cols, part=None, ring=False):
    if len(outs) == 1:
        half = stage.shape[0] // 2
        rows = slice(None) if part is None else slice(part * half, (part + 1) * half)
        pltpu.make_async_copy(stage.at[rows, :], outs[0].at[t, rows, cols], sem).start()
        return
    block = outs[0].shape[1]
    for d in range(8) if part is None else range(4 * part, 4 * part + 4):
        staged = stage.at[d * block : (d + 1) * block, :]
        send_block(place_ref, staged, [out.at[:, :, cols] for out in outs], sem, d, t, ring)


def qkv_kernel(count, place_ref, x_ref, gain_ref, bias_ref, bqv_ref, *refs):
    sources = refs[:count]
    q_ref, k_ref, v_ref, n_ref, w_out, raw, sems, w_ref, w_sem = refs[count:]
    blocks = raw.shape[0]
    normed, _ = norm_parts(x_ref[...].astype(F32))
    low = (normed * gain_ref[...] + bias_ref[...]).astype(BF)
    n_ref[...] = low

    @pl.when(pl.program_id(0) == 0)
    def _():
        cols = slice(0, raw.shape[2])
        start_blocks(place_ref, sources, cols, raw, cols, sems)
        for t in range(blocks):
            wait_all(raw.at[t], sems.at[t])

        def piece(t, c):
            return raw[t, :, c * PAIR : (c + 1) * PAIR]

        for t in range(blocks):
            for c in range(4):
                w_ref[c, :, t * PAIR : (t + 1) * PAIR] = piece(t, c)
        for u in range(blocks // 2):
            col = (blocks + u) * PAIR
            for half in range(2):
                left = piece(2 * u, 4 + half)
                right = piece(2 * u + 1, 4 + half)
                w_ref[2 * half, :, col : col + PAIR] = jnp.concatenate(
                    [left[:, :HEAD_DIM], right[:, :HEAD_DIM]], axis=1
                )
                w_ref[2 * half + 1, :, col : col + PAIR] = jnp.concatenate(
                    [left[:, HEAD_DIM:], right[:, HEAD_DIM:]], axis=1
                )
        pltpu.make_async_copy(w_ref, w_out, w_sem).start()

    q_low = (dot_nn(low, w_ref[0]) + bqv_ref[0:1, :]).astype(BF)
    q_ref[...] = q_low * BF(HEAD_DIM ** (-0.5))
    k_ref[...] = dot_nn(low, w_ref[1]).astype(BF)
    v_ref[...] = (dot_nn(low, w_ref[2]) + bqv_ref[1:2, :]).astype(BF)

    @pl.when(pl.program_id(0) == pl.num_programs(0) - 1)
    def _():
        wait_all(w_ref, w_sem)


def project(place, x, gain, bias, bqv, sources, blocks):
    rows, width = x.shape
    row_spec = pl.BlockSpec((TILE, width), lambda i, *_: (i, 0))
    return pl.pallas_call(
        functools.partial(qkv_kernel, len(sources)),
        grid_spec=pltpu.PrefetchScalarGridSpec(
            num_scalar_prefetch=1,
            grid=(rows // TILE,),
            in_specs=[
                row_spec,
                once((1, width), lambda i, *_: (0, 0)),
                once((1, width), lambda i, *_: (0, 0)),
                once((2, width), lambda i, *_: (0, 0)),
            ]
            + [ANY_SPEC] * len(sources),
            out_specs=[row_spec] * 4 + [ANY_SPEC],
            scratch_shapes=[
                pltpu.VMEM((blocks, width, sources[0].shape[-1]), BF),
                pltpu.SemaphoreType.DMA((blocks,)),
                pltpu.VMEM((4, width, width), BF),
                pltpu.SemaphoreType.DMA(()),
            ],
        ),
        out_shape=[jax.ShapeDtypeStruct((rows, width), BF)] * 4
        + [jax.ShapeDtypeStruct((4, width, width), BF)],
        compiler_params=params(),
        cost_estimate=cost(6 * rows * width * width, 16 * rows * width),
        name="project",
    )(place, x, gain, bias, bqv, *sources)


def half_masks():
    lane = lax.broadcasted_iota(jnp.int32, (1, PAIR), 1)
    first = (lane < HEAD_DIM).astype(F32)
    return first.astype(BF), (1.0 - first).astype(BF)


def attend_kernel(len_ref, q_ref, k_ref, v_ref, o_ref, lse_ref):
    rows = q_ref.shape[0]
    length = len_ref[0]
    masks = half_masks()
    lane = lax.broadcasted_iota(jnp.int32, (TILE, PAIR), 1)
    k_pos = lax.broadcasted_iota(jnp.int32, (1, rows), 1)
    bias = jnp.where(k_pos < length, 0.0, NEG_BIG)
    tri = lax.broadcasted_iota(jnp.int32, (TILE, TILE), 0) >= lax.broadcasted_iota(
        jnp.int32, (TILE, TILE), 1
    )
    for n in range(0, rows, TILE):
        q_block = q_ref[n : n + TILE, :]
        scores = []
        for mask in masks:
            q_one = q_block * mask
            s_diag = dot_nt(q_one, k_ref[n : n + TILE, :]) + bias[:, n : n + TILE]
            s_diag = jnp.where(tri, s_diag, NEG_BIG)
            s_rest = dot_nt(q_one, k_ref[:n, :]) + bias[:, :n] if n else None
            scores.append((s_diag, s_rest))
        outs = []
        peaks = []
        totals = []
        for s_diag, s_rest in scores:
            peak = jnp.max(s_diag, axis=1, keepdims=True)
            if n:
                peak = jnp.maximum(peak, jnp.max(s_rest, axis=1, keepdims=True))
            e_diag = jnp.exp(s_diag - peak)
            total = jnp.sum(e_diag, axis=1, keepdims=True)
            acc = dot_nn(e_diag.astype(BF), v_ref[n : n + TILE, :])
            if n:
                e_rest = jnp.exp(s_rest - peak)
                total = total + jnp.sum(e_rest, axis=1, keepdims=True)
                acc = acc + dot_nn(e_rest.astype(BF), v_ref[:n, :])
            outs.append(acc)
            peaks.append(peak)
            totals.append(total)
        first = lane < HEAD_DIM
        both = jnp.where(first, outs[0], outs[1])
        o_ref[n : n + TILE, :] = (both / jnp.where(first, totals[0], totals[1])).astype(BF)
        packed = jnp.where(lane < 8, peaks[0], totals[0])
        packed = jnp.where(lane % 8 == 1, jnp.where(lane < 8, peaks[1], totals[1]), packed)
        flipped = jnp.transpose(packed)
        lse_ref[0, :, n : n + TILE] = flipped[:8, :] + jnp.log(flipped[8:16, :])


def attend(lengths, q, k, v):
    rows, width = q.shape
    pairs = width // PAIR
    pair_spec = pl.BlockSpec((rows, PAIR), lambda i, *_: (0, i))
    return pl.pallas_call(
        attend_kernel,
        grid_spec=pltpu.PrefetchScalarGridSpec(
            num_scalar_prefetch=1,
            grid=(pairs,),
            in_specs=[pair_spec] * 3,
            out_specs=[pair_spec, pl.BlockSpec((1, 8, rows), lambda i, *_: (i, 0, 0))],
        ),
        out_shape=[
            jax.ShapeDtypeStruct((rows, width), BF),
            jax.ShapeDtypeStruct((pairs, 8, rows), F32),
        ],
        compiler_params=params(),
        cost_estimate=cost(16e9 * width / 768, 8 * rows * width),
        name="attend",
    )(lengths, q, k, v)


def attend_back_kernel(
    first, n_out, more, len_ref, place_ref, q_ref, k_ref, v_ref, o_ref, do_ref, lse_ref, n_ref,
    out_ref, *refs
):
    refs = refs[n_out:] if more else refs
    dq_ref, dk_ref, dv_ref = refs[:3]
    outs = refs[3 : 3 + n_out]
    dq_acc, side_s, n_s, stage, n_sem, sem = refs[3 + n_out :]
    rows = q_ref.shape[0]
    width = n_ref.shape[1]
    step = pl.program_id(0)
    length = len_ref[0]
    masks = half_masks()
    wide = stage.shape[2]
    narrow = wide != 3 * PAIR

    @pl.when(step == 0)
    def _():
        pltpu.make_async_copy(n_ref, n_s, n_sem).start()

    prod = jnp.transpose(do_ref[...].astype(F32) * o_ref[...].astype(F32))
    tri = lax.broadcasted_iota(jnp.int32, (TILE, TILE), 0) <= lax.broadcasted_iota(
        jnp.int32, (TILE, TILE), 1
    )
    k_pos = lax.broadcasted_iota(jnp.int32, (TILE, 1), 0)
    dq_acc[...] = jnp.zeros_like(dq_acc)
    heads = []
    for h, mask in enumerate(masks):
        heads.append(
            (
                mask,
                q_ref[...] * mask,
                do_ref[...] * mask,
                lse_ref[0, h : h + 1, :],
                jnp.sum(prod[h * HEAD_DIM : (h + 1) * HEAD_DIM, :], axis=0, keepdims=True),
            )
        )
    for n in range(0, rows, TILE):
        k_block = k_ref[n : n + TILE, :]
        v_block = v_ref[n : n + TILE, :]
        bias = jnp.where(k_pos + n < length, 0.0, NEG_BIG)
        dk = jnp.zeros((TILE, PAIR), F32)
        dv = jnp.zeros((TILE, PAIR), F32)
        work = []
        for mask, q_one, do_one, lse, delta in heads:
            for low, high in ((n, n + TILE), (n + TILE, rows)):
                if low == high:
                    continue
                s = dot_nt(k_block, q_one[low:high]) + bias
                dp = dot_nt(v_block, do_one[low:high])
                work.append((mask, q_one, do_one, lse, delta, low, high, s, dp))
        for mask, q_one, do_one, lse, delta, low, high, s, dp in work:
            if low == n:
                s = jnp.where(tri, s, NEG_BIG)
            p = jnp.exp(s - lse[:, low:high])
            ds = (p * (dp - delta[:, low:high])).astype(BF)
            dv = dv + dot_nn(p.astype(BF), do_one[low:high])
            dk = dk + dot_nn(ds, q_one[low:high])
            dq_acc[low:high, :] += dot_tn(ds, k_block * mask)
        dk_ref[n : n + TILE, :] = dk.astype(BF)
        dv_ref[n : n + TILE, :] = dv.astype(BF)
    dq_ref[...] = (dq_acc[...] * (HEAD_DIM ** (-0.5))).astype(BF)

    grads = [dq_ref[...], dk_ref[...], dv_ref[...]]
    if narrow:
        blank = jnp.zeros((rows, HEAD_DIM), BF)
        sides = [
            jnp.concatenate([g[:, c : c + HEAD_DIM] for g in grads] + [blank], axis=1)
            for c in (0, HEAD_DIM)
        ]
    else:
        sides = [jnp.concatenate(grads, axis=1)]
    pairs = side_s.shape[1] // (wide * len(sides))
    for at in range(pairs):

        @pl.when(step == at)
        def _(at=at):
            for i, side in enumerate(sides):
                spot = at * len(sides) + i
                side_s[:, spot * wide : (spot + 1) * wide] = side

    @pl.when(step == pairs - 1)
    def _():
        pltpu.make_async_copy(n_ref, n_s, n_sem).wait()
        low_col = 3 * PAIR if narrow else 0
        columns = slice(low_col, low_col + wide)
        for part in range(2):
            cols = slice(part * width // 2, (part + 1) * width // 2)
            grad = dot_tn(n_s[:, cols], side_s[...]).astype(BF)
            for spot in range(stage.shape[0]):
                t = spot if narrow else first + spot
                begin = spot * wide
                if narrow:
                    stage[spot, cols, :PAIR] = grad[:, begin : begin + PAIR]
                    extra = out_ref[cols, spot * HEAD_DIM : (spot + 1) * HEAD_DIM]
                    stage[spot, cols, PAIR:] = jnp.concatenate(
                        [grad[:, begin + PAIR : begin + PAIR + HEAD_DIM], extra], axis=1
                    )
                else:
                    stage[spot, cols, :] = grad[:, begin : begin + wide]
                send_rows(place_ref, stage.at[spot], outs, sem, t, columns, part)
        wait_all(stage, sem)


def attend_back(
    place, lengths, first, pairs, wide, q, k, v, out, d_out, lse, normed, last_out, blocks,
    so_far, fast,
):
    rows, width = q.shape
    at_pair = pl.BlockSpec((rows, PAIR), lambda i, *_: (0, first + i))
    own_pair = pl.BlockSpec((rows, PAIR), lambda i, *_: (0, i))
    grads = grad_shapes(fast, blocks, width, 5 * PAIR)
    so_far = so_far or []
    sides = 1 if wide == 3 * PAIR else 2
    return pl.pallas_call(
        functools.partial(attend_back_kernel, first, len(grads), bool(so_far)),
        grid_spec=pltpu.PrefetchScalarGridSpec(
            num_scalar_prefetch=2,
            grid=(pairs,),
            in_specs=[at_pair] * 5
            + [
                pl.BlockSpec((1, 8, rows), lambda i, *_: (first + i, 0, 0)),
                ANY_SPEC,
                once(last_out.shape, lambda i, *_: (0, 0)),
            ]
            + [ANY_SPEC] * len(so_far),
            out_specs=[own_pair] * 3 + [ANY_SPEC] * len(grads),
            scratch_shapes=[
                pltpu.VMEM((rows, PAIR), F32),
                pltpu.VMEM((rows, pairs * sides * wide), BF),
                pltpu.VMEM((rows, width), BF),
                pltpu.VMEM((pairs * sides, width, wide), BF),
                pltpu.SemaphoreType.DMA(()),
                pltpu.SemaphoreType.DMA(()),
            ],
        ),
        out_shape=[jax.ShapeDtypeStruct((rows, pairs * PAIR), BF)] * 3 + grads,
        input_output_aliases={10 + i: 3 + i for i in range(len(so_far))},
        compiler_params=params(),
        cost_estimate=cost(3e9 * pairs, 5e6 * pairs),
        name="attend_back",
    )(lengths, place, q, k, v, out, d_out, lse, normed, last_out, *so_far)


def vec_rows(vec_ref):
    return lambda i: vec_ref[i : i + 1, :]


def tile_rows(i):
    return pl.ds(pl.multiple_of(i * TILE, TILE), TILE)


def grad_shapes(fast, blocks, width, wide):
    if fast:
        return [jax.ShapeDtypeStruct((16, width // 8, wide), BF)] * 2
    return [jax.ShapeDtypeStruct((blocks, width, wide), BF)]


def feed_kernel(
    counts, place_ref, att_ref, x_ref, cot_ref, wo_ref, vec_ref, bup_ref, *refs
):
    one, two = counts
    refs, sources = refs[one + two :], (refs[:one], refs[one : one + two])
    resid_out, act_ref, gbup_ref, dres_out, datt_out, sums_ref, last_out_ref = refs[:7]
    refs = refs[7:]
    n_out = (len(refs) - 13) // 2
    up_outs, down_outs = refs[:n_out], refs[n_out : 2 * n_out]
    raw, sems, n_two, d_pre_s, d_norm, low, stage, stage_down, sem = refs[2 * n_out : -4]
    resid_ref, dres_ref, datt_ref, out_sems = refs[-4:]
    rows, width = x_ref.shape
    step = pl.program_id(0)
    tiles = rows // TILE
    blocks = stage.shape[0]
    vec = vec_rows(vec_ref)
    half_width = width // 2
    cut = sources[0][0].shape[-1] // 2

    @pl.when(step == 0)
    def _():
        begin = 0
        sizes, orders = (cut, width - cut), ("ring", "last")
        for source, size, order in zip(sources, sizes, orders, strict=True):
            for to in (begin, width + begin):
                start_blocks(
                    place_ref,
                    source,
                    slice(0 if to < width else size, size if to < width else 2 * size),
                    raw,
                    slice(to, to + size),
                    sems,
                    order,
                )
            begin += size

        def body(i, _):
            r = tile_rows(i)
            res = x_ref[r, :].astype(F32) + dot_nt(att_ref[r, :], wo_ref[0]) + vec(0)
            resid_ref[r, :] = res
            normed, _ = norm_parts(res)
            n_two[r, :] = (normed * vec(1) + vec(2)).astype(BF)
            d_norm[r, :] = jnp.zeros((TILE, width), F32)
            return 0

        lax.fori_loop(0, tiles, body, 0)
        pltpu.make_async_copy(resid_ref, resid_out, out_sems.at[0]).start()

    wait_all(raw.at[step], sems.at[step])
    w_up = raw[step, :, :width]
    w_down = raw[step, :, width:]
    c_one = 0.7978845608028654
    c_two = 0.044715

    def body(i, total):
        r = tile_rows(i)
        u = dot_nn(n_two[r, :], w_up) + bup_ref[0]
        d_act = dot_nn(cot_ref[r, :], w_down)
        square = u * u
        t = jnp.tanh(c_one * u * (1.0 + c_two * square))
        half = 0.5 * (1.0 + t)
        act_ref[r, :] = (u * half).astype(BF)
        slope = half + 0.5 * u * (1.0 - t * t) * (c_one * (1.0 + 3.0 * c_two * square))
        d_pre = (d_act * slope).astype(BF)
        d_pre_s[r, :] = d_pre
        d_norm[r, :] += dot_nt(d_pre, w_up)
        return total + col_sum(d_pre.astype(F32))

    gbup_ref[0] = lax.fori_loop(0, tiles, body, jnp.zeros((1, width), F32), unroll=True)
    def grads(i, _):
        cols = tile_rows(i)
        stage[step, cols, :width] = dot_tn(n_two[:, cols], d_pre_s[...]).astype(BF)
        stage_down[step, cols, :] = dot_tn(cot_ref[:, cols], act_ref[...]).astype(BF)
        return 0

    lax.fori_loop(0, width // TILE, grads, 0)
    first_cols = slice(0, width)
    for t in range(blocks):

        @pl.when(step == t)
        def _(t=t):
            send_rows(place_ref, stage.at[t, :, first_cols], up_outs, sem, t, first_cols)
            send_rows(place_ref, stage_down.at[t], down_outs, sem, t, first_cols)

    @pl.when(step == pl.num_programs(0) - 1)
    def _():
        def body(i, sums):
            r = tile_rows(i)
            normed, scale = norm_parts(resid_ref[r, :])
            d_n = d_norm[r, :]
            d_out = cot_ref[r, :].astype(F32)
            d_res = d_out + norm_back(d_n * vec(1), normed, scale)
            dres_ref[r, :] = d_res
            d_low = d_res.astype(BF)
            low[r, :] = d_low
            datt_ref[r, :] = dot_nn(d_low, wo_ref[0]).astype(BF)
            pltpu.make_async_copy(dres_ref.at[r, :], dres_out.at[r, :], out_sems.at[1]).start()
            pltpu.make_async_copy(datt_ref.at[r, :], datt_out.at[r, :], out_sems.at[2]).start()
            more = (col_sum(d_n * normed), col_sum(d_n), col_sum(d_res), col_sum(d_out))
            return tuple(a + b for a, b in zip(sums, more, strict=True))

        sums = lax.fori_loop(0, tiles, body, (jnp.zeros((1, width), F32),) * 4)
        sums_ref[...] = jnp.zeros_like(sums_ref)
        for i in range(4):
            sums_ref[i : i + 1, :] = sums[i]
        side = width
        for c in range(0, width, half_width):
            rows_c = slice(c, c + half_width)
            go = dot_tn(low[:, rows_c], att_ref[...]).astype(BF)
            last_out_ref[rows_c, :] = go[:, blocks * PAIR :]
            for t in range(blocks):
                stage[t, rows_c, side:] = go[:, t * PAIR : (t + 1) * PAIR]
        cols = slice(side, side + PAIR)
        for t in range(blocks):
            send_rows(place_ref, stage.at[t, :, cols], up_outs, sem, t, cols)
        wait_all(stage, sem)
        wait_all(stage_down, sem)
        for i, ref in enumerate((resid_ref, dres_ref, datt_ref)):
            wait_all(ref, out_sems.at[i])


def feed_forward(place, att, x, cot, w_all, vecs, b_up, sources_one, sources_two, fast):
    rows, width = x.shape
    blocks = b_up.shape[0]
    whole = once((rows, width), lambda t, *_: (0, 0))
    up_vec = pl.BlockSpec((1, 1, width), lambda t, *_: (t, 0, 0))
    grads = grad_shapes(fast, blocks, width, width + PAIR)
    grads += grad_shapes(fast, blocks, width, width)
    counts = (len(sources_one), len(sources_two))
    return pl.pallas_call(
        functools.partial(feed_kernel, counts),
        grid_spec=pltpu.PrefetchScalarGridSpec(
            num_scalar_prefetch=1,
            grid=(blocks,),
            in_specs=[
                whole,
                whole,
                whole,
                once((1, width, width), lambda t, *_: (3, 0, 0)),
                once((8, width), lambda t, *_: (0, 0)),
                up_vec,
            ]
            + [ANY_SPEC] * sum(counts),
            out_specs=[
                ANY_SPEC,
                pl.BlockSpec((rows, width), lambda t, *_: (0, t)),
                up_vec,
                ANY_SPEC,
                ANY_SPEC,
                once((8, width), lambda t, *_: (0, 0)),
                once((width, width - blocks * PAIR), lambda t, *_: (0, 0)),
            ]
            + [ANY_SPEC] * len(grads),
            scratch_shapes=[
                pltpu.VMEM((blocks, width, 2 * width), BF),
                pltpu.SemaphoreType.DMA((blocks,)),
                pltpu.VMEM((rows, width), BF),
                pltpu.VMEM((rows, width), BF),
                pltpu.VMEM((rows, width), F32),
                pltpu.VMEM((rows, width), BF),
                pltpu.VMEM((blocks, width, width + PAIR), BF),
                pltpu.VMEM((blocks, width, width), BF),
                pltpu.SemaphoreType.DMA(()),
                pltpu.VMEM((rows, width), F32),
                pltpu.VMEM((rows, width), F32),
                pltpu.VMEM((rows, width), BF),
                pltpu.SemaphoreType.DMA((3,)),
            ],
        ),
        out_shape=[
            jax.ShapeDtypeStruct((rows, width), F32),
            jax.ShapeDtypeStruct((rows, blocks * width), BF),
            jax.ShapeDtypeStruct((blocks, 1, width), F32),
            jax.ShapeDtypeStruct((rows, width), F32),
            jax.ShapeDtypeStruct((rows, width), BF),
            jax.ShapeDtypeStruct((8, width), F32),
            jax.ShapeDtypeStruct((width, width - blocks * PAIR), BF),
        ]
        + grads,
        compiler_params=params(),
        cost_estimate=cost(40e9, 40e6),
        name="feed_forward",
    )(place, att, x, cot, w_all, vecs, b_up, *sources_one, *sources_two)


def hidden_kernel(counts, place_ref, act_ref, resid_ref, vec_ref, *refs):
    one, two = counts
    refs, sources = refs[one + two :], (refs[:one], refs[one : one + two])
    out_ref, raw, sems = refs
    blocks, _, width = raw.shape
    cut = sources[0][0].shape[-1] // 2

    @pl.when(pl.program_id(0) == 0)
    def _():
        begin = 0
        sizes, orders = (cut, width - cut), ("ring", "last")
        for source, size, order in zip(sources, sizes, orders, strict=True):
            to = slice(begin, begin + size)
            start_blocks(place_ref, source, slice(size, 2 * size), raw, to, sems, order)
            begin += size
        for t in range(blocks):
            wait_all(raw.at[t], sems.at[t])

    acc = resid_ref[...] + vec_ref[3:4, :]
    for t in range(blocks):
        acc = acc + dot_nt(act_ref[:, t * width : (t + 1) * width], raw[t])
    out_ref[...] = acc.astype(BF)


def hidden_rows(place, act, resid, vecs, sources_one, sources_two):
    rows, width = resid.shape
    blocks = act.shape[1] // width
    row_spec = pl.BlockSpec((TILE, width), lambda i, *_: (i, 0))
    counts = (len(sources_one), len(sources_two))
    return pl.pallas_call(
        functools.partial(hidden_kernel, counts),
        grid_spec=pltpu.PrefetchScalarGridSpec(
            num_scalar_prefetch=1,
            grid=(rows // TILE,),
            in_specs=[
                pl.BlockSpec((TILE, blocks * width), lambda i, *_: (i, 0)),
                row_spec,
                once((8, width), lambda i, *_: (0, 0)),
            ]
            + [ANY_SPEC] * sum(counts),
            out_specs=row_spec,
            scratch_shapes=[
                pltpu.VMEM((blocks, width, width), BF),
                pltpu.SemaphoreType.DMA((blocks,)),
            ],
        ),
        out_shape=jax.ShapeDtypeStruct((rows, width), BF),
        compiler_params=params(),
        cost_estimate=cost(5e9, 12e6),
        name="hidden_rows",
    )(place, act, resid, vecs, *sources_one, *sources_two)


def input_kernel(*refs):
    parts = refs[:6]
    w_ref, x_ref, dres_ref, gain_ref, gin_ref, sums_ref = refs[6:]

    @pl.when(pl.program_id(0) == 0)
    def _():
        sums_ref[...] = jnp.zeros_like(sums_ref)

    dq, dk, dv = (jnp.concatenate([part[...] for part in parts[i::3]], axis=1) for i in range(3))
    d_norm = dot_nt(dq, w_ref[0]) + dot_nt(dk, w_ref[1]) + dot_nt(dv, w_ref[2])
    normed, scale = norm_parts(x_ref[...].astype(F32))
    gin_ref[...] = dres_ref[...] + norm_back(d_norm * gain_ref[...], normed, scale)
    more = (
        col_sum(d_norm * normed),
        col_sum(d_norm),
        col_sum(dq.astype(F32)),
        col_sum(dv.astype(F32)),
    )
    for i, value in enumerate(more):
        sums_ref[i : i + 1, :] += value


def input_grad(parts, w_all, x, d_resid, gain):
    rows, width = x.shape
    row_spec = pl.BlockSpec((TILE, width), lambda i: (i, 0))
    return pl.pallas_call(
        input_kernel,
        grid=(rows // TILE,),
        in_specs=[pl.BlockSpec((TILE, part.shape[1]), lambda i: (i, 0)) for part in parts]
        + [
            once((3, width, width), lambda i: (0, 0, 0)),
            row_spec,
            row_spec,
            once((1, width), lambda i: (0, 0)),
        ],
        out_specs=[row_spec, pl.BlockSpec((8, width), lambda i: (0, 0))],
        out_shape=[
            jax.ShapeDtypeStruct((rows, width), F32),
            jax.ShapeDtypeStruct((8, width), F32),
        ],
        compiler_params=params(),
        cost_estimate=cost(6 * rows * width * width, 16 * rows * width),
        name="input_grad",
    )(*parts, w_all, x, d_resid, gain)


def body(
    n_dp,
    n_tensor,
    hidden_in,
    cotangent,
    lengths,
    latent,
    ln1_gain,
    ln1_bias,
    w_qkv,
    b_qv,
    w_out,
    b_out,
    ln2_gain,
    ln2_bias,
    w_up,
    b_up,
    w_down,
    b_down,
):
    rows, width = hidden_in.shape
    t_index = lax.axis_index("tensor")
    block = w_up.shape[0]
    heads = w_qkv.shape[2] // HEAD_DIM

    out_t = w_out.T
    packed = jnp.concatenate(
        [w_qkv[0, :, :PAIR], w_qkv[1, :, :PAIR], w_qkv[2, :, :PAIR], out_t[:, :PAIR]]
        + [w_qkv[0, :, PAIR:], w_qkv[1, :, PAIR:], w_qkv[2, :, PAIR:], out_t[:, PAIR:]],
        axis=1,
    ).astype(BF)
    packed, up_part, down_part = after(packed, w_up, w_down)
    down_t = down_part.T
    cut = w_up.shape[1] * 2 // 3
    packed_one = jnp.concatenate([up_part[:, :cut], down_t[:, :cut]], axis=1).astype(BF)
    packed_two = jnp.concatenate([up_part[:, cut:], down_t[:, cut:]], axis=1).astype(BF)

    fast = n_dp == 8 and n_tensor == 4
    d_index = lax.axis_index("dp")
    place = jnp.stack([d_index >> 1, d_index & 1, t_index >> 1, t_index & 1]).astype(jnp.int32)

    def gather(piece):
        wide = piece.shape[1]
        full = lax.all_gather(piece, BOTH, axis=0, tiled=False)
        full = full.reshape(n_dp, n_tensor, block, wide)
        if fast:
            return full
        return full.transpose(1, 0, 2, 3).reshape(1, n_tensor, width, wide)

    project_place = place
    def to_inner(b):
        split = b.reshape(b.shape[0], n_tensor, heads, HEAD_DIM)
        return jnp.concatenate(
            [split[:, :, :2].reshape(b.shape[0], -1), split[:, :, 2:].reshape(b.shape[0], -1)],
            axis=1,
        )

    raw = [cotangent, lengths, latent, b_qv, ln1_gain, ln1_bias, b_out, ln2_gain, ln2_bias, b_down, b_up]

    def small_operands(
        cotangent, lengths, latent, b_qv, ln1_gain, ln1_bias, b_out, ln2_gain, ln2_bias, b_down, b_up
    ):
        own_length = lax.dynamic_slice_in_dim(lengths, t_index, 1, 0)
        own_latent = lax.dynamic_slice_in_dim(latent, t_index, 1, 0)
        positions = lax.broadcasted_iota(jnp.int32, (1, rows), 1)
        keep = ((positions < own_length) & (own_latent == 0)).astype(BF).reshape(rows, 1)
        cot = cotangent * keep
        zero = jnp.zeros_like(b_out)
        return [
            cot,
            place,
            own_length,
            to_inner(b_qv),
            ln1_gain[None],
            ln1_bias[None],
            jnp.stack([b_out, ln2_gain, ln2_bias, b_down, zero, zero, zero, zero]),
            b_up.reshape(n_tensor, 1, width),
        ]
    if fast:
        def grow(array, came):
            return jnp.concatenate([array, came])

        att, one, two = packed[None], packed_one[None], packed_two[None]
        att_came, two, one, *raw = after(exchange(att, flip_near), two, one, *raw)
        early = small_operands(*raw)
        att = grow(att, att_came)
        two = grow(two, exchange(two, flip_first))
        att_came, two_came, one_one, *early = after(
            exchange(att, flip_far), exchange(two, flip_second), exchange(one, flip_ring), *early
        )
        att, two = grow(att, att_came), grow(two, two_came)
        att_first, att_second, one_two, two_one = after(
            exchange(att, flip_first),
            exchange(att, flip_second),
            exchange(one_one, flip_ring),
            exchange(two, flip_ring),
        )
        halves = [att, att_first, att_second]
        att_both, one_last, *cores = after(
            exchange(att_first, flip_second),
            exchange(one_two, flip_ring),
            *(exchange(half, flip_core) for half in halves),
        )
        sources = [*halves, att_both, *cores, exchange(att_both, flip_core)]
        one = jnp.concatenate([one, one_one, one_two, one_last])
        one_first, two_two = exchange(one, flip_first), exchange(two_one, flip_ring)
    else:
        early = small_operands(*raw)
        sources = [gather(packed)]
        sources_one, sources_two = [gather(packed_one)], [gather(packed_two)]

    def from_inner(b):
        cut = n_tensor * PAIR
        first = b[:, :cut].reshape(b.shape[0], n_tensor, 2, HEAD_DIM)
        rest = b[:, cut:].reshape(b.shape[0], n_tensor, heads - 2, HEAD_DIM)
        return jnp.concatenate([first, rest], axis=2).reshape(b.shape[0], width)

    cot, place, own_length, inner_bqv, gain, bias, vecs, up_bias = early
    q, k, v, normed_one, w_all = project(
        place, hidden_in, gain, bias, inner_bqv, sources, n_tensor
    )
    if fast:
        one_first, two_two, q = after(one_first, two_two, q)
        halves = [one, one_first, two, two_one, two_two]
        cores = [exchange(half, flip_core) for half in halves]
        came = [exchange(half, flip_second) for half in halves[:2]]
        came.append(exchange(two_two, flip_ring))
    attended, lse = attend(own_length, q, k, v)
    if fast:
        attended, *moved = after(attended, *came, *cores)
        came, cores = moved[:3], moved[3:]
        cores += [exchange(half, flip_core) for half in came]
        sources_one = [*halves[:2], *came[:2], *cores[:2], *cores[5:7]]
        sources_two = [*halves[2:], came[2], *cores[2:5], cores[7]]
    resid, act, g_b_up, d_resid, d_attended, sums_two, last_out, *g_mlp = feed_forward(
        place, attended, hidden_in, cot, w_all, vecs, up_bias, sources_one, sources_two, fast
    )

    half = len(g_mlp) // 2

    def back(length, first, pairs, wide, so_far):
        return list(
            attend_back(
                place, length, first, pairs, wide, q, k, v, attended, d_attended, lse,
                normed_one, last_out, n_tensor, so_far, fast,
            )
        )

    def vectors(sums_one):
        return jnp.concatenate([sums_one[:4], sums_two[:4], g_b_up.reshape(n_tensor, width)])

    if fast:
        up, down = Scatter(*g_mlp[:half]), Scatter(*g_mlp[half:])
        came_up, came_down = up.step(), down.step()
        hidden_out = hidden_rows(place, act, resid, vecs, sources_one, sources_two)
        came_up, came_down, length, hidden_out = after(
            came_up, came_down, own_length, hidden_out
        )
        up.sent, down.sent = sums(up.want(came_up), down.want(came_down))
        came_up, came_down = up.step(), down.step()
        back_one = back(length, 0, 4, 3 * PAIR, None)
        came_up, length, *back_one = after(came_up, own_length, *back_one)
        (up.sent,) = sums(up.want(came_up))
        came_up = up.step()
        back_two = back(length, 4, 2, 2 * PAIR, back_one[3:])
        came_up, came_down, gain, *back_two = after(came_up, came_down, gain, *back_two)
        rest = Scatter(*back_two[3:])
        came_rest = rest.step()
        up.sent, down.sent = sums(up.want(came_up), down.want(came_down))
        came_rest, up.sent, down.sent = after(came_rest, up.sent, down.sent)
        came_up, came_down = up.step(), down.step()
        (rest.sent,) = sums(rest.want(came_rest))
        came_rest = rest.step()
        parts = [*back_one[:3], *back_two[:3]]
        grad_in, sums_one = input_grad(parts, w_all, hidden_in, d_resid, gain)
        came_rest, came_down, sums_one, grad_in = after(came_rest, came_down, sums_one, grad_in)
        rest.sent, down.sent = sums(rest.want(came_rest), down.want(came_down))
        came_up, rest.sent, down.sent = after(came_up, rest.sent, down.sent)
        came_rest, came_down = rest.step(), down.step()
        (up.sent,) = plain_sums(up.want(came_up))
        came_up = up.step()
        small = vectors(sums_one)
        small = small + exchange(small, flip_core)
        came_small = exchange(small, flip_second)
        small = small + came_small
        came_small = exchange(small, flip_first)
        came_rest, came_small = after(came_rest, came_small)
        (rest.sent,) = plain_sums(rest.want(came_rest))
        small = small + came_small
        came_rest, came_small = rest.step(), exchange(small, flip_far)
        came_small, came_down = after(came_small, came_down)
        (down.sent,) = plain_sums(down.want(came_down))
        came_down = down.step()
        came_rest, came_small, came_up = after(came_rest, came_small, came_up)
        (rest.sent,) = plain_sums(rest.want(came_rest))
        small = small + came_small
        came_rest, came_small = rest.step(), exchange(small, flip_near)
        small = small + came_small
        g_up, g_out, g_down, g_qkv = last_sums(
            [*up.terms, came_up], [*down.terms, came_down], [*rest.terms, came_rest]
        )
    else:
        back_one = back(own_length, 0, 4, 3 * PAIR, None)
        back_two = back(own_length, 4, 2, 2 * PAIR, back_one[3:])
        parts = [*back_one[:3], *back_two[:3]]
        grad_in, sums_one = input_grad(parts, w_all, hidden_in, d_resid, gain)
        hidden_out = hidden_rows(place, act, resid, vecs, sources_one, sources_two)
        small = lax.psum(vectors(sums_one), BOTH)

        def scatter_all(grads):
            wide = grads.shape[-1]
            grads = grads.reshape(n_tensor, n_dp, block, wide).transpose(1, 0, 2, 3)
            flat = grads.reshape(n_dp * n_tensor * block, wide)
            total = lax.psum_scatter(flat, BOTH, scatter_dimension=0, tiled=True)
            return total.astype(F32)

        g_up, g_down, g_rest = (scatter_all(g) for g in (*g_mlp, back_two[3]))
        g_out, g_qkv = split_columns(g_up, g_rest)
        g_out = g_out.T
        g_up = g_up[:, :width]
    g_bqv = from_inner(small[2:4])

    return (
        hidden_out,
        grad_in,
        small[0],
        small[1],
        g_qkv,
        g_bqv,
        g_out,
        small[6],
        small[4],
        small[5],
        g_up,
        small[8:].reshape(-1),
        g_down.T,
        small[7],
    )


def solution(mesh):
    placed = (
        P(BOTH, None),
        P(BOTH, None),
        P("dp"),
        P("dp", None),
        P(),
        P(),
        P(None, "dp", "tensor"),
        P(),
        P("tensor", "dp"),
        P(),
        P(),
        P(),
        P("dp", "tensor"),
        P(),
        P("tensor", "dp"),
        P(),
    )
    return jax.shard_map(
        functools.partial(body, mesh.shape["dp"], mesh.shape["tensor"]),
        mesh=mesh,
        in_specs=placed,
        out_specs=(
            P(BOTH, None),
            P(BOTH, None),
            P(),
            P(),
            P(None, "dp", "tensor"),
            P(),
            P("tensor", "dp"),
            P(),
            P(),
            P(),
            P("dp", "tensor"),
            P(),
            P("tensor", "dp"),
            P(),
        ),
        check_vma=False,
    )
```

```python
import functools

import jax
import jax.numpy as jnp
from jax import lax
from jax.experimental import pallas as pl
from jax.experimental.pallas import tpu as pltpu
from jax.sharding import PartitionSpec as P

HEAD_DIM = 64
LEN = 1024
PAIR = 2 * HEAD_DIM
TILE = 256
NEG_BIG = -1e30
EPSILON = 1e-05
VMEM_BYTES = 66_900_000
BF = jnp.bfloat16
F32 = jnp.float32
BOTH = ("dp", "tensor")
ANY_SPEC = pl.BlockSpec(memory_space=pl.ANY)


def dot_nn(a, b):
    return lax.dot_general(a, b, (((1,), (0,)), ((), ())), preferred_element_type=F32)


def dot_nt(a, b):
    return lax.dot_general(a, b, (((1,), (1,)), ((), ())), preferred_element_type=F32)


def dot_tn(a, b):
    return lax.dot_general(a, b, (((0,), (0,)), ((), ())), preferred_element_type=F32)


def norm_parts(rows_in):
    center = rows_in - jnp.mean(rows_in, axis=-1, keepdims=True)
    spread = jnp.mean(center * center, axis=-1, keepdims=True)
    scale = lax.rsqrt(spread + EPSILON)
    return center * scale, scale


def norm_back(gy, normed, scale):
    mean_gy = jnp.mean(gy, axis=-1, keepdims=True)
    mean_gyn = jnp.mean(gy * normed, axis=-1, keepdims=True)
    return (gy - mean_gy - normed * mean_gyn) * scale


def col_sum(values):
    return jnp.sum(values, axis=0, keepdims=True)


def once(shape, index):
    return pl.BlockSpec(shape, index, pipeline_mode=pl.Buffered(1))


def params(side_effects=False):
    return pltpu.CompilerParams(
        dimension_semantics=("arbitrary",),
        vmem_limit_bytes=VMEM_BYTES,
        has_side_effects=side_effects,
    )


def cost(flops, moved, exps=0):
    return pl.CostEstimate(flops=int(flops), bytes_accessed=int(moved), transcendentals=int(exps))


def place_of(index):
    return (index >> 3) & 3, (index >> 2) & 1, (index >> 1) & 1, index & 1


def index_of(z, x, y, core):
    return (z << 3) | (x << 2) | (y << 1) | core


def exchange(array, flip):
    pairs = [(i, index_of(*flip(*place_of(i)))) for i in range(32)]
    return lax.ppermute(array, BOTH, pairs)


def flip_first(z, x, y, core):
    return (z, x, y ^ 1, core) if core else (z, x ^ 1, y, core)


def flip_second(z, x, y, core):
    return (z, x ^ 1, y, core) if core else (z, x, y ^ 1, core)


def flip_core(z, x, y, core):
    return z, x, y, core ^ 1


def flip_near(z, x, y, core):
    return z ^ 1, x, y, core


def flip_far(z, x, y, core):
    return z ^ 2, x, y, core


def sums_kernel(plan, *refs):
    count_in = sum(len(offsets) for offsets, _ in plan)
    outs = refs[count_in : count_in + len(plan)]
    scratch = refs[count_in + len(plan) :]
    position = 0
    for i, (offsets, count) in enumerate(plan):
        terms, _, sems, _ = scratch[4 * i : 4 * i + 4]
        for slot in range(count):
            for k, offset in enumerate(offsets):
                pltpu.make_async_copy(
                    refs[position + k].at[offset + slot], terms.at[slot, k], sems.at[slot]
                ).start()
        position += len(offsets)
    for i, (offsets, count) in enumerate(plan):
        terms, result, sems, out_sem = scratch[4 * i : 4 * i + 4]

        def body(slot, _, i=i, size=len(offsets)):
            terms, result, sems, out_sem = scratch[4 * i : 4 * i + 4]
            wait_all(terms.at[slot], sems.at[slot])
            total = terms[slot, 0].astype(F32)
            for k in range(1, size):
                total = total + terms[slot, k].astype(F32)
            result[slot] = total.astype(BF)
            pltpu.make_async_copy(result.at[slot], outs[i].at[slot], out_sem).start()
            return 0

        lax.fori_loop(0, count, body, 0)
    for i in range(len(plan)):
        wait_all(scratch[4 * i + 1], scratch[4 * i + 3])


def sums(*requests):
    plan, arrays, shapes, scratch = [], [], [], []
    for terms, count in requests:
        block = terms[0][0].shape[1:]
        plan.append((tuple(offset for _, offset in terms), count))
        arrays += [array for array, _ in terms]
        shapes.append(jax.ShapeDtypeStruct((count, *block), BF))
        scratch += [
            pltpu.VMEM((count, len(terms), *block), BF),
            pltpu.VMEM((count, *block), BF),
            pltpu.SemaphoreType.DMA((count,)),
            pltpu.SemaphoreType.DMA(()),
        ]
    return pl.pallas_call(
        functools.partial(sums_kernel, plan),
        in_specs=[ANY_SPEC] * len(arrays),
        out_specs=[ANY_SPEC] * len(shapes),
        out_shape=shapes,
        scratch_shapes=scratch,
        compiler_params=pltpu.CompilerParams(vmem_limit_bytes=VMEM_BYTES),
        cost_estimate=cost(1e6, 8e6),
        name="sums",
    )(*arrays)


def plain_sums(*requests):
    results = []
    for terms, count in requests:
        total = None
        for array, offset in terms:
            part = array[offset : offset + count].astype(F32)
            total = part if total is None else total + part
        results.append(total.astype(BF))
    return results


def split_columns(up, rest):
    width = up.shape[1] - PAIR
    side = 3 * PAIR
    out = jnp.concatenate([up[:, width:], rest[:, side + 3 * HEAD_DIM :]], axis=1)
    three = []
    for i in range(3):
        begin = side + i * HEAD_DIM
        parts = [rest[:, i * PAIR : (i + 1) * PAIR], rest[:, begin : begin + HEAD_DIM]]
        three.append(jnp.concatenate(parts, axis=1))
    return out, jnp.stack(three)


def last_kernel(counts, *refs):
    sources, rest_of = refs[: sum(counts)], refs[sum(counts) :]
    up_ref, out_ref, down_ref, qkv_ref = rest_of[:4]
    scratch, sems = rest_of[4:7], rest_of[7]
    position = 0
    for i, count in enumerate(counts):
        for k in range(count):
            pltpu.make_async_copy(
                sources[position + k].at[0], scratch[i].at[k], sems.at[i]
            ).start()
        position += count
    totals = []
    for i, count in enumerate(counts):
        wait_all(scratch[i], sems.at[i])
        total = scratch[i][0].astype(F32)
        for k in range(1, count):
            total = total + scratch[i][k].astype(F32)
        totals.append(total)
    up, down, rest = totals
    up_ref[...] = up[:, : up_ref.shape[1]]
    down_ref[...] = down
    out, qkv_ref[...] = split_columns(up, rest)
    out_ref[...] = jnp.transpose(out)


def last_sums(*chains):
    counts = [len(terms) for terms in chains]
    block = chains[0][0].shape[1]
    width, third = chains[1][0].shape[2], 3 * HEAD_DIM
    whole = pl.BlockSpec(memory_space=pltpu.VMEM)
    return pl.pallas_call(
        functools.partial(last_kernel, counts),
        in_specs=[ANY_SPEC] * sum(counts),
        out_specs=[whole] * 4,
        out_shape=[
            jax.ShapeDtypeStruct((block, width), F32),
            jax.ShapeDtypeStruct((third, block), F32),
            jax.ShapeDtypeStruct((block, width), F32),
            jax.ShapeDtypeStruct((3, block, third), F32),
        ],
        scratch_shapes=[
            pltpu.VMEM((len(terms), block, terms[0].shape[2]), BF) for terms in chains
        ]
        + [pltpu.SemaphoreType.DMA((3,))],
        compiler_params=pltpu.CompilerParams(vmem_limit_bytes=VMEM_BYTES),
        cost_estimate=cost(1e6, 4e6),
        name="last_sums",
    )(*(term for terms in chains for term in terms))


class Scatter:
    def __init__(self, kept, sent):
        self.terms, self.sent = [kept], sent
        self.flips = [flip_core, flip_second, flip_first, flip_far, flip_near]

    def step(self):
        return exchange(self.sent, self.flips.pop(0))

    def want(self, came):
        self.terms = [*self.terms, came]
        count = came.shape[0] // 2
        return [(array, count) for array in self.terms], count


def after(value, *others):
    return lax.optimization_barrier((value, *others))


def ring_place(z):
    z = z & 3
    return z ^ (z >> 1)


def flip_ring(z, x, y, core):
    return ring_place(ring_place(z) + 1), x, y, core


def start_blocks(place_ref, sources, cols, raw, to, sems, order="xor"):
    if len(sources) == 1:
        nd, blocks, block, _ = sources[0].shape
        for d in range(nd):
            for t in range(blocks):
                pltpu.make_async_copy(
                    sources[0].at[d, t, :, cols],
                    raw.at[t, d * block : (d + 1) * block, to],
                    sems.at[t],
                ).start()
        return
    z, x, y, core = (place_ref[i] for i in range(4))
    block = sources[0].shape[1]
    for i, source in enumerate(sources):
        for slot in range(4):
            to_core = core ^ (i >> 2)
            pair, step = (slot, i & 3) if order == "last" else (i & 3, slot)
            second, first = pair >> 1, pair & 1
            to_x = x ^ (first + to_core * (second - first))
            to_y = y ^ (second + to_core * (first - second))
            to_z = z ^ step if order == "xor" else ring_place(ring_place(z) - step)
            to_t = to_y * 2 + to_core
            low = pl.multiple_of((to_z * 2 + to_x) * block, block)
            pltpu.make_async_copy(
                source.at[slot, :, cols], raw.at[to_t, pl.ds(low, block), to], sems.at[to_t]
            ).start()


def wait_all(ref, sem):
    pltpu.make_async_copy(ref, ref, sem).wait()


def send_block(place_ref, staged, outs, sem, d, t, ring):
    z, x, y, core = (place_ref[i] for i in range(4))
    far, near_core = d >> 1, t & 1
    x_off, y_off = x ^ (d & 1), y ^ (t >> 1)
    first, second = (y_off, x_off) if near_core else (x_off, y_off)
    along = (ring_place(far) - ring_place(z)) & 3 if ring else z ^ far
    slot = second * 8 + first * 4 + along
    for side in range(2):

        @pl.when((core ^ near_core) == side)
        def _(side=side):
            pltpu.make_async_copy(staged, outs[side].at[slot], sem).start()


def send_rows(place_ref, stage, outs, sem, t, cols, part=None, ring=False):
    if len(outs) == 1:
        half = stage.shape[0] // 2
        rows = slice(None) if part is None else slice(part * half, (part + 1) * half)
        pltpu.make_async_copy(stage.at[rows, :], outs[0].at[t, rows, cols], sem).start()
        return
    block = outs[0].shape[1]
    for d in range(8) if part is None else range(4 * part, 4 * part + 4):
        staged = stage.at[d * block : (d + 1) * block, :]
        send_block(place_ref, staged, [out.at[:, :, cols] for out in outs], sem, d, t, ring)


def qkv_kernel(count, place_ref, x_ref, gain_ref, bias_ref, bqv_ref, *refs):
    sources = refs[:count]
    q_ref, k_ref, v_ref, n_ref, w_out, raw, sems, w_ref, w_sem = refs[count:]
    blocks = raw.shape[0]
    normed, _ = norm_parts(x_ref[...].astype(F32))
    low = (normed * gain_ref[...] + bias_ref[...]).astype(BF)
    n_ref[...] = low

    @pl.when(pl.program_id(0) == 0)
    def _():
        cols = slice(0, raw.shape[2])
        start_blocks(place_ref, sources, cols, raw, cols, sems)
        for t in range(blocks):
            wait_all(raw.at[t], sems.at[t])

        def piece(t, c):
            return raw[t, :, c * PAIR : (c + 1) * PAIR]

        for t in range(blocks):
            for c in range(4):
                w_ref[c, :, t * PAIR : (t + 1) * PAIR] = piece(t, c)
        for u in range(blocks // 2):
            col = (blocks + u) * PAIR
            for half in range(2):
                left = piece(2 * u, 4 + half)
                right = piece(2 * u + 1, 4 + half)
                w_ref[2 * half, :, col : col + PAIR] = jnp.concatenate(
                    [left[:, :HEAD_DIM], right[:, :HEAD_DIM]], axis=1
                )
                w_ref[2 * half + 1, :, col : col + PAIR] = jnp.concatenate(
                    [left[:, HEAD_DIM:], right[:, HEAD_DIM:]], axis=1
                )
        pltpu.make_async_copy(w_ref, w_out, w_sem).start()

    q_low = (dot_nn(low, w_ref[0]) + bqv_ref[0:1, :]).astype(BF)
    q_ref[...] = q_low * BF(HEAD_DIM ** (-0.5))
    k_ref[...] = dot_nn(low, w_ref[1]).astype(BF)
    v_ref[...] = (dot_nn(low, w_ref[2]) + bqv_ref[1:2, :]).astype(BF)

    @pl.when(pl.program_id(0) == pl.num_programs(0) - 1)
    def _():
        wait_all(w_ref, w_sem)


def project(place, x, gain, bias, bqv, sources, blocks):
    rows, width = x.shape
    row_spec = pl.BlockSpec((TILE, width), lambda i, *_: (i, 0))
    return pl.pallas_call(
        functools.partial(qkv_kernel, len(sources)),
        grid_spec=pltpu.PrefetchScalarGridSpec(
            num_scalar_prefetch=1,
            grid=(rows // TILE,),
            in_specs=[
                row_spec,
                once((1, width), lambda i, *_: (0, 0)),
                once((1, width), lambda i, *_: (0, 0)),
                once((2, width), lambda i, *_: (0, 0)),
            ]
            + [ANY_SPEC] * len(sources),
            out_specs=[row_spec] * 4 + [ANY_SPEC],
            scratch_shapes=[
                pltpu.VMEM((blocks, width, sources[0].shape[-1]), BF),
                pltpu.SemaphoreType.DMA((blocks,)),
                pltpu.VMEM((4, width, width), BF),
                pltpu.SemaphoreType.DMA(()),
            ],
        ),
        out_shape=[jax.ShapeDtypeStruct((rows, width), BF)] * 4
        + [jax.ShapeDtypeStruct((4, width, width), BF)],
        compiler_params=params(),
        cost_estimate=cost(6 * rows * width * width, 16 * rows * width),
        name="project",
    )(place, x, gain, bias, bqv, *sources)


def half_masks():
    lane = lax.broadcasted_iota(jnp.int32, (1, PAIR), 1)
    first = (lane < HEAD_DIM).astype(F32)
    return first.astype(BF), (1.0 - first).astype(BF)


def attend_kernel(len_ref, q_ref, k_ref, v_ref, o_ref, lse_ref):
    rows = q_ref.shape[0]
    length = len_ref[0]
    masks = half_masks()
    lane = lax.broadcasted_iota(jnp.int32, (TILE, PAIR), 1)
    k_pos = lax.broadcasted_iota(jnp.int32, (1, rows), 1)
    bias = jnp.where(k_pos < length, 0.0, NEG_BIG)
    tri = lax.broadcasted_iota(jnp.int32, (TILE, TILE), 0) >= lax.broadcasted_iota(
        jnp.int32, (TILE, TILE), 1
    )
    for n in range(0, rows, TILE):
        q_block = q_ref[n : n + TILE, :]
        scores = []
        for mask in masks:
            q_one = q_block * mask
            s_diag = dot_nt(q_one, k_ref[n : n + TILE, :]) + bias[:, n : n + TILE]
            s_diag = jnp.where(tri, s_diag, NEG_BIG)
            s_rest = dot_nt(q_one, k_ref[:n, :]) + bias[:, :n] if n else None
            scores.append((s_diag, s_rest))
        outs = []
        peaks = []
        totals = []
        for s_diag, s_rest in scores:
            peak = jnp.max(s_diag, axis=1, keepdims=True)
            if n:
                peak = jnp.maximum(peak, jnp.max(s_rest, axis=1, keepdims=True))
            e_diag = jnp.exp(s_diag - peak)
            total = jnp.sum(e_diag, axis=1, keepdims=True)
            acc = dot_nn(e_diag.astype(BF), v_ref[n : n + TILE, :])
            if n:
                e_rest = jnp.exp(s_rest - peak)
                total = total + jnp.sum(e_rest, axis=1, keepdims=True)
                acc = acc + dot_nn(e_rest.astype(BF), v_ref[:n, :])
            outs.append(acc)
            peaks.append(peak)
            totals.append(total)
        first = lane < HEAD_DIM
        both = jnp.where(first, outs[0], outs[1])
        o_ref[n : n + TILE, :] = (both / jnp.where(first, totals[0], totals[1])).astype(BF)
        packed = jnp.where(lane < 8, peaks[0], totals[0])
        packed = jnp.where(lane % 8 == 1, jnp.where(lane < 8, peaks[1], totals[1]), packed)
        flipped = jnp.transpose(packed)
        lse_ref[0, :, n : n + TILE] = flipped[:8, :] + jnp.log(flipped[8:16, :])


def attend(lengths, q, k, v):
    rows, width = q.shape
    pairs = width // PAIR
    pair_spec = pl.BlockSpec((rows, PAIR), lambda i, *_: (0, i))
    return pl.pallas_call(
        attend_kernel,
        grid_spec=pltpu.PrefetchScalarGridSpec(
            num_scalar_prefetch=1,
            grid=(pairs,),
            in_specs=[pair_spec] * 3,
            out_specs=[pair_spec, pl.BlockSpec((1, 8, rows), lambda i, *_: (i, 0, 0))],
        ),
        out_shape=[
            jax.ShapeDtypeStruct((rows, width), BF),
            jax.ShapeDtypeStruct((pairs, 8, rows), F32),
        ],
        compiler_params=params(),
        cost_estimate=cost(16e9 * width / 768, 8 * rows * width),
        name="attend",
    )(lengths, q, k, v)


def attend_back_kernel(
    first, n_out, more, len_ref, place_ref, q_ref, k_ref, v_ref, o_ref, do_ref, lse_ref, n_ref,
    out_ref, *refs
):
    refs = refs[n_out:] if more else refs
    dq_ref, dk_ref, dv_ref = refs[:3]
    outs = refs[3 : 3 + n_out]
    dq_acc, side_s, n_s, stage, n_sem, sem = refs[3 + n_out :]
    rows = q_ref.shape[0]
    width = n_ref.shape[1]
    step = pl.program_id(0)
    length = len_ref[0]
    masks = half_masks()
    wide = stage.shape[2]
    narrow = wide != 3 * PAIR

    @pl.when(step == 0)
    def _():
        pltpu.make_async_copy(n_ref, n_s, n_sem).start()

    prod = jnp.transpose(do_ref[...].astype(F32) * o_ref[...].astype(F32))
    tri = lax.broadcasted_iota(jnp.int32, (TILE, TILE), 0) <= lax.broadcasted_iota(
        jnp.int32, (TILE, TILE), 1
    )
    k_pos = lax.broadcasted_iota(jnp.int32, (TILE, 1), 0)
    dq_acc[...] = jnp.zeros_like(dq_acc)
    heads = []
    for h, mask in enumerate(masks):
        heads.append(
            (
                mask,
                q_ref[...] * mask,
                do_ref[...] * mask,
                lse_ref[0, h : h + 1, :],
                jnp.sum(prod[h * HEAD_DIM : (h + 1) * HEAD_DIM, :], axis=0, keepdims=True),
            )
        )
    for n in range(0, rows, TILE):
        k_block = k_ref[n : n + TILE, :]
        v_block = v_ref[n : n + TILE, :]
        bias = jnp.where(k_pos + n < length, 0.0, NEG_BIG)
        dk = jnp.zeros((TILE, PAIR), F32)
        dv = jnp.zeros((TILE, PAIR), F32)
        work = []
        for mask, q_one, do_one, lse, delta in heads:
            for low, high in ((n, n + TILE), (n + TILE, rows)):
                if low == high:
                    continue
                s = dot_nt(k_block, q_one[low:high]) + bias
                dp = dot_nt(v_block, do_one[low:high])
                work.append((mask, q_one, do_one, lse, delta, low, high, s, dp))
        for mask, q_one, do_one, lse, delta, low, high, s, dp in work:
            if low == n:
                s = jnp.where(tri, s, NEG_BIG)
            p = jnp.exp(s - lse[:, low:high])
            ds = (p * (dp - delta[:, low:high])).astype(BF)
            dv = dv + dot_nn(p.astype(BF), do_one[low:high])
            dk = dk + dot_nn(ds, q_one[low:high])
            dq_acc[low:high, :] += dot_tn(ds, k_block * mask)
        dk_ref[n : n + TILE, :] = dk.astype(BF)
        dv_ref[n : n + TILE, :] = dv.astype(BF)
    dq_ref[...] = (dq_acc[...] * (HEAD_DIM ** (-0.5))).astype(BF)

    grads = [dq_ref[...], dk_ref[...], dv_ref[...]]
    if narrow:
        blank = jnp.zeros((rows, HEAD_DIM), BF)
        sides = [
            jnp.concatenate([g[:, c : c + HEAD_DIM] for g in grads] + [blank], axis=1)
            for c in (0, HEAD_DIM)
        ]
    else:
        sides = [jnp.concatenate(grads, axis=1)]
    pairs = side_s.shape[1] // (wide * len(sides))
    for at in range(pairs):

        @pl.when(step == at)
        def _(at=at):
            for i, side in enumerate(sides):
                spot = at * len(sides) + i
                side_s[:, spot * wide : (spot + 1) * wide] = side

    @pl.when(step == pairs - 1)
    def _():
        pltpu.make_async_copy(n_ref, n_s, n_sem).wait()
        low_col = 3 * PAIR if narrow else 0
        columns = slice(low_col, low_col + wide)
        for part in range(2):
            cols = slice(part * width // 2, (part + 1) * width // 2)
            grad = dot_tn(n_s[:, cols], side_s[...]).astype(BF)
            for spot in range(stage.shape[0]):
                t = spot if narrow else first + spot
                begin = spot * wide
                if narrow:
                    stage[spot, cols, :PAIR] = grad[:, begin : begin + PAIR]
                    extra = out_ref[cols, spot * HEAD_DIM : (spot + 1) * HEAD_DIM]
                    stage[spot, cols, PAIR:] = jnp.concatenate(
                        [grad[:, begin + PAIR : begin + PAIR + HEAD_DIM], extra], axis=1
                    )
                else:
                    stage[spot, cols, :] = grad[:, begin : begin + wide]
                send_rows(place_ref, stage.at[spot], outs, sem, t, columns, part)
        wait_all(stage, sem)


def attend_back(
    place, lengths, first, pairs, wide, q, k, v, out, d_out, lse, normed, last_out, blocks,
    so_far, fast,
):
    rows, width = q.shape
    at_pair = pl.BlockSpec((rows, PAIR), lambda i, *_: (0, first + i))
    own_pair = pl.BlockSpec((rows, PAIR), lambda i, *_: (0, i))
    grads = grad_shapes(fast, blocks, width, 5 * PAIR)
    so_far = so_far or []
    sides = 1 if wide == 3 * PAIR else 2
    return pl.pallas_call(
        functools.partial(attend_back_kernel, first, len(grads), bool(so_far)),
        grid_spec=pltpu.PrefetchScalarGridSpec(
            num_scalar_prefetch=2,
            grid=(pairs,),
            in_specs=[at_pair] * 5
            + [
                pl.BlockSpec((1, 8, rows), lambda i, *_: (first + i, 0, 0)),
                ANY_SPEC,
                once(last_out.shape, lambda i, *_: (0, 0)),
            ]
            + [ANY_SPEC] * len(so_far),
            out_specs=[own_pair] * 3 + [ANY_SPEC] * len(grads),
            scratch_shapes=[
                pltpu.VMEM((rows, PAIR), F32),
                pltpu.VMEM((rows, pairs * sides * wide), BF),
                pltpu.VMEM((rows, width), BF),
                pltpu.VMEM((pairs * sides, width, wide), BF),
                pltpu.SemaphoreType.DMA(()),
                pltpu.SemaphoreType.DMA(()),
            ],
        ),
        out_shape=[jax.ShapeDtypeStruct((rows, pairs * PAIR), BF)] * 3 + grads,
        input_output_aliases={10 + i: 3 + i for i in range(len(so_far))},
        compiler_params=params(),
        cost_estimate=cost(3e9 * pairs, 5e6 * pairs),
        name="attend_back",
    )(lengths, place, q, k, v, out, d_out, lse, normed, last_out, *so_far)


def vec_rows(vec_ref):
    return lambda i: vec_ref[i : i + 1, :]


def tile_rows(i):
    return pl.ds(pl.multiple_of(i * TILE, TILE), TILE)


def grad_shapes(fast, blocks, width, wide):
    if fast:
        return [jax.ShapeDtypeStruct((16, width // 8, wide), BF)] * 2
    return [jax.ShapeDtypeStruct((blocks, width, wide), BF)]


def feed_kernel(
    counts, place_ref, att_ref, x_ref, cot_ref, wo_ref, vec_ref, bup_ref, *refs
):
    one, two = counts
    refs, sources = refs[one + two :], (refs[:one], refs[one : one + two])
    resid_out, act_ref, gbup_ref, dres_out, datt_out, sums_ref, last_out_ref = refs[:7]
    refs = refs[7:]
    n_out = (len(refs) - 13) // 2
    up_outs, down_outs = refs[:n_out], refs[n_out : 2 * n_out]
    raw, sems, n_two, d_pre_s, d_norm, low, stage, stage_down, sem = refs[2 * n_out : -4]
    resid_ref, dres_ref, datt_ref, out_sems = refs[-4:]
    rows, width = x_ref.shape
    step = pl.program_id(0)
    tiles = rows // TILE
    blocks = stage.shape[0]
    vec = vec_rows(vec_ref)
    half_width = width // 2
    cut = sources[0][0].shape[-1] // 2

    @pl.when(step == 0)
    def _():
        begin = 0
        sizes, orders = (cut, width - cut), ("ring", "last")
        for source, size, order in zip(sources, sizes, orders, strict=True):
            for to in (begin, width + begin):
                start_blocks(
                    place_ref,
                    source,
                    slice(0 if to < width else size, size if to < width else 2 * size),
                    raw,
                    slice(to, to + size),
                    sems,
                    order,
                )
            begin += size

        def body(i, _):
            r = tile_rows(i)
            res = x_ref[r, :].astype(F32) + dot_nt(att_ref[r, :], wo_ref[0]) + vec(0)
            resid_ref[r, :] = res
            normed, _ = norm_parts(res)
            n_two[r, :] = (normed * vec(1) + vec(2)).astype(BF)
            d_norm[r, :] = jnp.zeros((TILE, width), F32)
            return 0

        lax.fori_loop(0, tiles, body, 0, unroll=2)
        pltpu.make_async_copy(resid_ref, resid_out, out_sems.at[0]).start()

    wait_all(raw.at[step], sems.at[step])
    w_up = raw[step, :, :width]
    w_down = raw[step, :, width:]
    c_one = 0.7978845608028654
    c_two = 0.044715

    def body(i, total):
        r = tile_rows(i)
        u = dot_nn(n_two[r, :], w_up) + bup_ref[0]
        d_act = dot_nn(cot_ref[r, :], w_down)
        square = u * u
        t = jnp.tanh(c_one * u * (1.0 + c_two * square))
        half = 0.5 * (1.0 + t)
        act_ref[r, :] = (u * half).astype(BF)
        slope = half + 0.5 * u * (1.0 - t * t) * (c_one * (1.0 + 3.0 * c_two * square))
        d_pre = (d_act * slope).astype(BF)
        d_pre_s[r, :] = d_pre
        d_norm[r, :] += dot_nt(d_pre, w_up)
        return total + col_sum(d_pre.astype(F32))

    gbup_ref[0] = lax.fori_loop(0, tiles, body, jnp.zeros((1, width), F32), unroll=True)
    def grads(i, _):
        cols = tile_rows(i)
        stage[step, cols, :width] = dot_tn(n_two[:, cols], d_pre_s[...]).astype(BF)
        stage_down[step, cols, :] = dot_tn(cot_ref[:, cols], act_ref[...]).astype(BF)
        return 0

    lax.fori_loop(0, width // TILE, grads, 0)
    first_cols = slice(0, width)
    for t in range(blocks):

        @pl.when(step == t)
        def _(t=t):
            send_rows(place_ref, stage.at[t, :, first_cols], up_outs, sem, t, first_cols)
            send_rows(place_ref, stage_down.at[t], down_outs, sem, t, first_cols)

    @pl.when(step == pl.num_programs(0) - 1)
    def _():
        def body(i, sums):
            r = tile_rows(i)
            normed, scale = norm_parts(resid_ref[r, :])
            d_n = d_norm[r, :]
            d_out = cot_ref[r, :].astype(F32)
            d_res = d_out + norm_back(d_n * vec(1), normed, scale)
            dres_ref[r, :] = d_res
            d_low = d_res.astype(BF)
            low[r, :] = d_low
            datt_ref[r, :] = dot_nn(d_low, wo_ref[0]).astype(BF)
            pltpu.make_async_copy(dres_ref.at[r, :], dres_out.at[r, :], out_sems.at[1]).start()
            pltpu.make_async_copy(datt_ref.at[r, :], datt_out.at[r, :], out_sems.at[2]).start()
            more = (col_sum(d_n * normed), col_sum(d_n), col_sum(d_res), col_sum(d_out))
            return tuple(a + b for a, b in zip(sums, more, strict=True))

        sums = lax.fori_loop(0, tiles, body, (jnp.zeros((1, width), F32),) * 4)
        sums_ref[...] = jnp.zeros_like(sums_ref)
        for i in range(4):
            sums_ref[i : i + 1, :] = sums[i]
        side = width
        for c in range(0, width, half_width):
            rows_c = slice(c, c + half_width)
            go = dot_tn(low[:, rows_c], att_ref[...]).astype(BF)
            last_out_ref[rows_c, :] = go[:, blocks * PAIR :]
            for t in range(blocks):
                stage[t, rows_c, side:] = go[:, t * PAIR : (t + 1) * PAIR]
        cols = slice(side, side + PAIR)
        for t in range(blocks):
            send_rows(place_ref, stage.at[t, :, cols], up_outs, sem, t, cols)
        wait_all(stage, sem)
        wait_all(stage_down, sem)
        for i, ref in enumerate((resid_ref, dres_ref, datt_ref)):
            wait_all(ref, out_sems.at[i])


def feed_forward(place, att, x, cot, w_all, vecs, b_up, sources_one, sources_two, fast):
    rows, width = x.shape
    blocks = b_up.shape[0]
    whole = once((rows, width), lambda t, *_: (0, 0))
    up_vec = pl.BlockSpec((1, 1, width), lambda t, *_: (t, 0, 0))
    grads = grad_shapes(fast, blocks, width, width + PAIR)
    grads += grad_shapes(fast, blocks, width, width)
    counts = (len(sources_one), len(sources_two))
    return pl.pallas_call(
        functools.partial(feed_kernel, counts),
        grid_spec=pltpu.PrefetchScalarGridSpec(
            num_scalar_prefetch=1,
            grid=(blocks,),
            in_specs=[
                whole,
                whole,
                whole,
                once((1, width, width), lambda t, *_: (3, 0, 0)),
                once((8, width), lambda t, *_: (0, 0)),
                up_vec,
            ]
            + [ANY_SPEC] * sum(counts),
            out_specs=[
                ANY_SPEC,
                pl.BlockSpec((rows, width), lambda t, *_: (0, t)),
                up_vec,
                ANY_SPEC,
                ANY_SPEC,
                once((8, width), lambda t, *_: (0, 0)),
                once((width, width - blocks * PAIR), lambda t, *_: (0, 0)),
            ]
            + [ANY_SPEC] * len(grads),
            scratch_shapes=[
                pltpu.VMEM((blocks, width, 2 * width), BF),
                pltpu.SemaphoreType.DMA((blocks,)),
                pltpu.VMEM((rows, width), BF),
                pltpu.VMEM((rows, width), BF),
                pltpu.VMEM((rows, width), F32),
                pltpu.VMEM((rows, width), BF),
                pltpu.VMEM((blocks, width, width + PAIR), BF),
                pltpu.VMEM((blocks, width, width), BF),
                pltpu.SemaphoreType.DMA(()),
                pltpu.VMEM((rows, width), F32),
                pltpu.VMEM((rows, width), F32),
                pltpu.VMEM((rows, width), BF),
                pltpu.SemaphoreType.DMA((3,)),
            ],
        ),
        out_shape=[
            jax.ShapeDtypeStruct((rows, width), F32),
            jax.ShapeDtypeStruct((rows, blocks * width), BF),
            jax.ShapeDtypeStruct((blocks, 1, width), F32),
            jax.ShapeDtypeStruct((rows, width), F32),
            jax.ShapeDtypeStruct((rows, width), BF),
            jax.ShapeDtypeStruct((8, width), F32),
            jax.ShapeDtypeStruct((width, width - blocks * PAIR), BF),
        ]
        + grads,
        compiler_params=params(),
        cost_estimate=cost(40e9, 40e6),
        name="feed_forward",
    )(place, att, x, cot, w_all, vecs, b_up, *sources_one, *sources_two)


def hidden_kernel(counts, place_ref, act_ref, resid_ref, vec_ref, *refs):
    one, two = counts
    refs, sources = refs[one + two :], (refs[:one], refs[one : one + two])
    out_ref, raw, sems = refs
    blocks, _, width = raw.shape
    cut = sources[0][0].shape[-1] // 2

    @pl.when(pl.program_id(0) == 0)
    def _():
        begin = 0
        sizes, orders = (cut, width - cut), ("ring", "last")
        for source, size, order in zip(sources, sizes, orders, strict=True):
            to = slice(begin, begin + size)
            start_blocks(place_ref, source, slice(size, 2 * size), raw, to, sems, order)
            begin += size
        for t in range(blocks):
            wait_all(raw.at[t], sems.at[t])

    acc = resid_ref[...] + vec_ref[3:4, :]
    for t in range(blocks):
        acc = acc + dot_nt(act_ref[:, t * width : (t + 1) * width], raw[t])
    out_ref[...] = acc.astype(BF)


def hidden_rows(place, act, resid, vecs, sources_one, sources_two):
    rows, width = resid.shape
    blocks = act.shape[1] // width
    row_spec = pl.BlockSpec((TILE, width), lambda i, *_: (i, 0))
    counts = (len(sources_one), len(sources_two))
    return pl.pallas_call(
        functools.partial(hidden_kernel, counts),
        grid_spec=pltpu.PrefetchScalarGridSpec(
            num_scalar_prefetch=1,
            grid=(rows // TILE,),
            in_specs=[
                pl.BlockSpec((TILE, blocks * width), lambda i, *_: (i, 0)),
                row_spec,
                once((8, width), lambda i, *_: (0, 0)),
            ]
            + [ANY_SPEC] * sum(counts),
            out_specs=row_spec,
            scratch_shapes=[
                pltpu.VMEM((blocks, width, width), BF),
                pltpu.SemaphoreType.DMA((blocks,)),
            ],
        ),
        out_shape=jax.ShapeDtypeStruct((rows, width), BF),
        compiler_params=params(),
        cost_estimate=cost(5e9, 12e6),
        name="hidden_rows",
    )(place, act, resid, vecs, *sources_one, *sources_two)


def input_kernel(*refs):
    parts = refs[:6]
    w_ref, x_ref, dres_ref, gain_ref, gin_ref, sums_ref = refs[6:]

    @pl.when(pl.program_id(0) == 0)
    def _():
        sums_ref[...] = jnp.zeros_like(sums_ref)

    dq, dk, dv = (jnp.concatenate([part[...] for part in parts[i::3]], axis=1) for i in range(3))
    d_norm = dot_nt(dq, w_ref[0]) + dot_nt(dk, w_ref[1]) + dot_nt(dv, w_ref[2])
    normed, scale = norm_parts(x_ref[...].astype(F32))
    gin_ref[...] = dres_ref[...] + norm_back(d_norm * gain_ref[...], normed, scale)
    more = (
        col_sum(d_norm * normed),
        col_sum(d_norm),
        col_sum(dq.astype(F32)),
        col_sum(dv.astype(F32)),
    )
    for i, value in enumerate(more):
        sums_ref[i : i + 1, :] += value


def input_grad(parts, w_all, x, d_resid, gain):
    rows, width = x.shape
    row_spec = pl.BlockSpec((TILE, width), lambda i: (i, 0))
    return pl.pallas_call(
        input_kernel,
        grid=(rows // TILE,),
        in_specs=[pl.BlockSpec((TILE, part.shape[1]), lambda i: (i, 0)) for part in parts]
        + [
            once((3, width, width), lambda i: (0, 0, 0)),
            row_spec,
            row_spec,
            once((1, width), lambda i: (0, 0)),
        ],
        out_specs=[row_spec, pl.BlockSpec((8, width), lambda i: (0, 0))],
        out_shape=[
            jax.ShapeDtypeStruct((rows, width), F32),
            jax.ShapeDtypeStruct((8, width), F32),
        ],
        compiler_params=params(),
        cost_estimate=cost(6 * rows * width * width, 16 * rows * width),
        name="input_grad",
    )(*parts, w_all, x, d_resid, gain)


def body(
    n_dp,
    n_tensor,
    hidden_in,
    cotangent,
    lengths,
    latent,
    ln1_gain,
    ln1_bias,
    w_qkv,
    b_qv,
    w_out,
    b_out,
    ln2_gain,
    ln2_bias,
    w_up,
    b_up,
    w_down,
    b_down,
):
    rows, width = hidden_in.shape
    t_index = lax.axis_index("tensor")
    block = w_up.shape[0]
    heads = w_qkv.shape[2] // HEAD_DIM

    out_t = w_out.T
    packed = jnp.concatenate(
        [w_qkv[0, :, :PAIR], w_qkv[1, :, :PAIR], w_qkv[2, :, :PAIR], out_t[:, :PAIR]]
        + [w_qkv[0, :, PAIR:], w_qkv[1, :, PAIR:], w_qkv[2, :, PAIR:], out_t[:, PAIR:]],
        axis=1,
    ).astype(BF)
    packed, up_part, down_part = after(packed, w_up, w_down)
    down_t = down_part.T
    cut = w_up.shape[1] * 2 // 3
    packed_one = jnp.concatenate([up_part[:, :cut], down_t[:, :cut]], axis=1).astype(BF)
    packed_two = jnp.concatenate([up_part[:, cut:], down_t[:, cut:]], axis=1).astype(BF)

    fast = n_dp == 8 and n_tensor == 4
    d_index = lax.axis_index("dp")
    place = jnp.stack([d_index >> 1, d_index & 1, t_index >> 1, t_index & 1]).astype(jnp.int32)

    def gather(piece):
        wide = piece.shape[1]
        full = lax.all_gather(piece, BOTH, axis=0, tiled=False)
        full = full.reshape(n_dp, n_tensor, block, wide)
        if fast:
            return full
        return full.transpose(1, 0, 2, 3).reshape(1, n_tensor, width, wide)

    project_place = place
    def to_inner(b):
        split = b.reshape(b.shape[0], n_tensor, heads, HEAD_DIM)
        return jnp.concatenate(
            [split[:, :, :2].reshape(b.shape[0], -1), split[:, :, 2:].reshape(b.shape[0], -1)],
            axis=1,
        )

    raw = [cotangent, lengths, latent, b_qv, ln1_gain, ln1_bias, b_out, ln2_gain, ln2_bias, b_down, b_up]

    def small_operands(
        cotangent, lengths, latent, b_qv, ln1_gain, ln1_bias, b_out, ln2_gain, ln2_bias, b_down, b_up
    ):
        own_length = lax.dynamic_slice_in_dim(lengths, t_index, 1, 0)
        own_latent = lax.dynamic_slice_in_dim(latent, t_index, 1, 0)
        positions = lax.broadcasted_iota(jnp.int32, (1, rows), 1)
        keep = ((positions < own_length) & (own_latent == 0)).astype(BF).reshape(rows, 1)
        cot = cotangent * keep
        zero = jnp.zeros_like(b_out)
        return [
            cot,
            place,
            own_length,
            to_inner(b_qv),
            ln1_gain[None],
            ln1_bias[None],
            jnp.stack([b_out, ln2_gain, ln2_bias, b_down, zero, zero, zero, zero]),
            b_up.reshape(n_tensor, 1, width),
        ]
    if fast:
        def grow(array, came):
            return jnp.concatenate([array, came])

        att, one, two = packed[None], packed_one[None], packed_two[None]
        att_came, two, one, *raw = after(exchange(att, flip_near), two, one, *raw)
        early = small_operands(*raw)
        att = grow(att, att_came)
        two = grow(two, exchange(two, flip_first))
        att_came, two_came, one_one, *early = after(
            exchange(att, flip_far), exchange(two, flip_second), exchange(one, flip_ring), *early
        )
        att, two = grow(att, att_came), grow(two, two_came)
        att_first, att_second, one_two, two_one = after(
            exchange(att, flip_first),
            exchange(att, flip_second),
            exchange(one_one, flip_ring),
            exchange(two, flip_ring),
        )
        halves = [att, att_first, att_second]
        att_both, one_last, *cores = after(
            exchange(att_first, flip_second),
            exchange(one_two, flip_ring),
            *(exchange(half, flip_core) for half in halves),
        )
        sources = [*halves, att_both, *cores, exchange(att_both, flip_core)]
        one = jnp.concatenate([one, one_one, one_two, one_last])
        one_first, two_two = exchange(one, flip_first), exchange(two_one, flip_ring)
    else:
        early = small_operands(*raw)
        sources = [gather(packed)]
        sources_one, sources_two = [gather(packed_one)], [gather(packed_two)]

    def from_inner(b):
        cut = n_tensor * PAIR
        first = b[:, :cut].reshape(b.shape[0], n_tensor, 2, HEAD_DIM)
        rest = b[:, cut:].reshape(b.shape[0], n_tensor, heads - 2, HEAD_DIM)
        return jnp.concatenate([first, rest], axis=2).reshape(b.shape[0], width)

    cot, place, own_length, inner_bqv, gain, bias, vecs, up_bias = early
    q, k, v, normed_one, w_all = project(
        place, hidden_in, gain, bias, inner_bqv, sources, n_tensor
    )
    if fast:
        one_first, two_two, q = after(one_first, two_two, q)
        halves = [one, one_first, two, two_one, two_two]
        cores = [exchange(half, flip_core) for half in halves]
        came = [exchange(half, flip_second) for half in halves[:2]]
        came.append(exchange(two_two, flip_ring))
    attended, lse = attend(own_length, q, k, v)
    if fast:
        attended, *moved = after(attended, *came, *cores)
        came, cores = moved[:3], moved[3:]
        cores += [exchange(half, flip_core) for half in came]
        sources_one = [*halves[:2], *came[:2], *cores[:2], *cores[5:7]]
        sources_two = [*halves[2:], came[2], *cores[2:5], cores[7]]
    resid, act, g_b_up, d_resid, d_attended, sums_two, last_out, *g_mlp = feed_forward(
        place, attended, hidden_in, cot, w_all, vecs, up_bias, sources_one, sources_two, fast
    )

    half = len(g_mlp) // 2

    def back(length, first, pairs, wide, so_far):
        return list(
            attend_back(
                place, length, first, pairs, wide, q, k, v, attended, d_attended, lse,
                normed_one, last_out, n_tensor, so_far, fast,
            )
        )

    def vectors(sums_one):
        return jnp.concatenate([sums_one[:4], sums_two[:4], g_b_up.reshape(n_tensor, width)])

    if fast:
        up, down = Scatter(*g_mlp[:half]), Scatter(*g_mlp[half:])
        came_up, came_down = up.step(), down.step()
        hidden_out = hidden_rows(place, act, resid, vecs, sources_one, sources_two)
        came_up, came_down, length, hidden_out = after(
            came_up, came_down, own_length, hidden_out
        )
        up.sent, down.sent = sums(up.want(came_up), down.want(came_down))
        came_up, came_down = up.step(), down.step()
        back_one = back(length, 0, 4, 3 * PAIR, None)
        came_up, length, *back_one = after(came_up, own_length, *back_one)
        (up.sent,) = sums(up.want(came_up))
        came_up = up.step()
        back_two = back(length, 4, 2, 2 * PAIR, back_one[3:])
        came_up, came_down, gain, *back_two = after(came_up, came_down, gain, *back_two)
        rest = Scatter(*back_two[3:])
        came_rest = rest.step()
        up.sent, down.sent = sums(up.want(came_up), down.want(came_down))
        came_rest, up.sent, down.sent = after(came_rest, up.sent, down.sent)
        came_up, came_down = up.step(), down.step()
        (rest.sent,) = sums(rest.want(came_rest))
        came_rest = rest.step()
        parts = [*back_one[:3], *back_two[:3]]
        grad_in, sums_one = input_grad(parts, w_all, hidden_in, d_resid, gain)
        came_rest, came_down, sums_one, grad_in = after(came_rest, came_down, sums_one, grad_in)
        rest.sent, down.sent = sums(rest.want(came_rest), down.want(came_down))
        came_up, rest.sent, down.sent = after(came_up, rest.sent, down.sent)
        came_rest, came_down = rest.step(), down.step()
        (up.sent,) = plain_sums(up.want(came_up))
        came_up = up.step()
        small = vectors(sums_one)
        small = small + exchange(small, flip_core)
        came_small = exchange(small, flip_second)
        small = small + came_small
        came_small = exchange(small, flip_first)
        came_rest, came_small = after(came_rest, came_small)
        (rest.sent,) = plain_sums(rest.want(came_rest))
        small = small + came_small
        came_rest, came_small = rest.step(), exchange(small, flip_far)
        came_small, came_down = after(came_small, came_down)
        (down.sent,) = plain_sums(down.want(came_down))
        came_down = down.step()
        came_rest, came_small, came_up = after(came_rest, came_small, came_up)
        (rest.sent,) = plain_sums(rest.want(came_rest))
        small = small + came_small
        came_rest, came_small = rest.step(), exchange(small, flip_near)
        small = small + came_small
        g_up, g_out, g_down, g_qkv = last_sums(
            [*up.terms, came_up], [*down.terms, came_down], [*rest.terms, came_rest]
        )
    else:
        back_one = back(own_length, 0, 4, 3 * PAIR, None)
        back_two = back(own_length, 4, 2, 2 * PAIR, back_one[3:])
        parts = [*back_one[:3], *back_two[:3]]
        grad_in, sums_one = input_grad(parts, w_all, hidden_in, d_resid, gain)
        hidden_out = hidden_rows(place, act, resid, vecs, sources_one, sources_two)
        small = lax.psum(vectors(sums_one), BOTH)

        def scatter_all(grads):
            wide = grads.shape[-1]
            grads = grads.reshape(n_tensor, n_dp, block, wide).transpose(1, 0, 2, 3)
            flat = grads.reshape(n_dp * n_tensor * block, wide)
            total = lax.psum_scatter(flat, BOTH, scatter_dimension=0, tiled=True)
            return total.astype(F32)

        g_up, g_down, g_rest = (scatter_all(g) for g in (*g_mlp, back_two[3]))
        g_out, g_qkv = split_columns(g_up, g_rest)
        g_out = g_out.T
        g_up = g_up[:, :width]
    g_bqv = from_inner(small[2:4])

    return (
        hidden_out,
        grad_in,
        small[0],
        small[1],
        g_qkv,
        g_bqv,
        g_out,
        small[6],
        small[4],
        small[5],
        g_up,
        small[8:].reshape(-1),
        g_down.T,
        small[7],
    )


def solution(mesh):
    placed = (
        P(BOTH, None),
        P(BOTH, None),
        P("dp"),
        P("dp", None),
        P(),
        P(),
        P(None, "dp", "tensor"),
        P(),
        P("tensor", "dp"),
        P(),
        P(),
        P(),
        P("dp", "tensor"),
        P(),
        P("tensor", "dp"),
        P(),
    )
    return jax.shard_map(
        functools.partial(body, mesh.shape["dp"], mesh.shape["tensor"]),
        mesh=mesh,
        in_specs=placed,
        out_specs=(
            P(BOTH, None),
            P(BOTH, None),
            P(),
            P(),
            P(None, "dp", "tensor"),
            P(),
            P("tensor", "dp"),
            P(),
            P(),
            P(),
            P("dp", "tensor"),
            P(),
            P("tensor", "dp"),
            P(),
        ),
        check_vma=False,
    )
```
